32 devices in a mesh: dp: 4 (over z), ctx: 8 (over y, x, core).
Axes of the slice: x: 2, y: 2, z: 4, core: 2. Of those that a mesh axis runs over, the one named last changes fastest.
Arguments:
- tokens: bfloat16 [2, 4, 1024, 2048], P(None, 'dp', 'ctx'), may hold values from -6 to 6
- cotangent: bfloat16 [2, 4, 1024, 2048], P(None, 'dp', 'ctx'), may hold values from -6 to 6
- routes: int32 [2, 4, 1024, 8], P(None, 'dp', 'ctx'), may hold values from 0 to 15, all different within a row; in each aligned block of 128 rows (0 to 127, 128 to 255, ..., all dimensions but the last counted through in order) at most 67 rows name the same one
- lengths: int32 [2, 4], P(None, 'dp'), may hold values from 256 to 1024, as said below
- block_order: int32 [16], replicated, may hold values from 0 to 15, each once
- w_query: bfloat16 [2048, 2048], P(('dp', 'ctx')), may hold values from -0.125 to 0.125
- w_key: bfloat16 [2048, 2048], P(('dp', 'ctx')), may hold values from -0.125 to 0.125
- w_value: bfloat16 [2048, 2048], P(('dp', 'ctx')), may hold values from -0.125 to 0.125
- w_out: bfloat16 [2048, 2048], P(('dp', 'ctx')), may hold values from -2 to 2
- w_router: bfloat16 [2048, 16], P(('dp', 'ctx')), may hold values from -0.0625 to 0.0625
- w_gate: bfloat16 [16, 2048, 1024], P('ctx', 'dp'), may hold values from -0.125 to 0.125
- w_up: bfloat16 [16, 2048, 1024], P('ctx', 'dp'), may hold values from -0.125 to 0.125
- w_down: bfloat16 [16, 1024, 2048], P('ctx', 'dp'), may hold values from -3 to 3
- attn_gain: bfloat16 [2048], P(('dp', 'ctx')), may hold values from 0.099609375 to 1.8984375
- mlp_gain: bfloat16 [2048], P(('dp', 'ctx')), may hold values from 0.099609375 to 1.8984375
- query_gain: bfloat16 [2048], P(('dp', 'ctx')), may hold values from 0.099609375 to 1.8984375
- key_gain: bfloat16 [2048], P(('dp', 'ctx')), may hold values from 0.099609375 to 1.8984375
Outputs:
- mixed: bfloat16 [2, 4, 1024, 2048], P(None, 'dp', 'ctx')
- d_tokens: float32 [2, 4, 1024, 2048], P(None, 'dp', 'ctx')
- d_w_query: float32 [2048, 2048], P(('dp', 'ctx'))
- d_w_key: float32 [2048, 2048], P(('dp', 'ctx'))
- d_w_value: float32 [2048, 2048], P(('dp', 'ctx'))
- d_w_out: float32 [2048, 2048], P(('dp', 'ctx'))
- d_w_router: float32 [2048, 16], P(('dp', 'ctx'))
- d_w_gate: float32 [16, 2048, 1024], P('ctx', 'dp')
- d_w_up: float32 [16, 2048, 1024], P('ctx', 'dp')
- d_w_down: float32 [16, 1024, 2048], P('ctx', 'dp')
- d_attn_gain: float32 [2048], P(('dp', 'ctx'))
- d_mlp_gain: float32 [2048], P(('dp', 'ctx'))
- d_query_gain: float32 [2048], P(('dp', 'ctx'))
- d_key_gain: float32 [2048], P(('dp', 'ctx'))
The draws below stay inside these ranges and needn't reach their ends.
Inputs may be any that keep to these rules, and one draw needn't show every extreme that they name: `routes`: within the rows of one device (aligned blocks of 128 rows) no expert is named more than 67 times, a bound that some block reaches. `lengths`: in every micro-batch some slot is full. `block_order`: each block number appears once.
All inputs are finite; a program needn't handle non-finite values.
Results may differ from the reference program's by a relative error of at most 0.02.
Values may be sent and summed in bfloat16 or wider, within the bound.
A program may use at most 448 MiB of HBM per device.

```python
import math
import jax
import jax.numpy as jnp
import numpy as np
from jax import lax

D = 2048
HEADS = 16
HEAD = 128
FFE = 1024
TOP = 8
TOK_DEV = 128
MB = 2
EXPERTS = 16
SLOTS = 4
SLOT = 1024
BLOCKS = 16
CAP = 67
N_CTX = 8


def draw_lengths(key, part):
    drawn = jax.random.randint(key, (MB, SLOTS), SLOT // 4, SLOT + 1)
    chosen = jax.random.randint(jax.random.fold_in(key, 7), (MB,), 0, SLOTS)
    full_slot = jnp.arange(SLOTS, dtype=jnp.int32)[None, :] == chosen[:, None]
    return jnp.where(full_slot, SLOT, drawn).astype(jnp.int32)


def shard_levels(rng, shape, split, low, top_value):
    level, own = 1.0, jax.random.fold_in(rng, 6)
    for dim, parts in split:
        heights = jnp.exp(jax.random.uniform(jax.random.fold_in(own, dim), (parts,), jnp.float32, low / len(split), top_value / len(split)))
        level = level * jnp.repeat(heights, shape[dim] // parts).reshape([-1 if axis == dim else 1 for axis in range(len(shape))])
    return level


def shared_out(key, own, number, rows, number_of, top, reach, lean):
    order = jax.random.permutation(key, number_of)
    heavy_load, common = shares(number_of, rows * top, reach, lean, True), shares(number_of, rows * top, reach, lean, False)
    places = jnp.arange(number_of)

    def named(sizes, rotation):
        used = int((sizes > 0).sum())
        fixed = max(1, used // 4)
        passed = fixed + (places - fixed + rotation * (used - fixed)) % max(1, number_of - fixed)
        return jnp.zeros((number_of,), jnp.int32).at[order[jnp.where(places < fixed, places, passed)]].set(jnp.asarray(sizes, jnp.int32))

    sizes = jnp.where(number % 4 == 0, named(heavy_load, number // 4), named(common, number - number // 4 - 1))
    mixed = jax.random.permutation(jax.random.fold_in(own, 3), number_of)
    source_of, taker = mixed[0:number_of // 2 * 2:2], mixed[1:number_of // 2 * 2:2]
    slack = jnp.minimum(sizes[source_of] - 1, reach - sizes[taker]) // 2
    slack = jnp.where((source_of == order[0]) | (taker == order[0]) | (sizes[taker] == 0), 0, jnp.maximum(slack, 0))
    passed = jax.random.randint(jax.random.fold_in(own, 4), (number_of // 2,), 0, 1 << 20) % (slack + 1)
    sizes = sizes.at[source_of].add(-passed).at[taker].add(passed)
    members = jnp.searchsorted(jnp.cumsum(sizes), jnp.arange(rows * top), side="right").astype(jnp.int32)
    table = members.reshape(top, rows).T
    table = table[jax.random.permutation(jax.random.fold_in(own, 1), rows)]
    rotation = jax.random.randint(jax.random.fold_in(own, 2), (rows, 1), 0, top)
    return jnp.take_along_axis(table, (jnp.arange(top)[None, :] + rotation) % top, axis=1)


def shares(number_of, total, most, slope, full):
    weights = [(1 << 20) // math.isqrt(standing ** slope) + 1 for standing in range(1, number_of + 1)]
    largest = most if full else min(most, max(-(-total // number_of), total * weights[0] // sum(weights)))
    least = 1 if total - largest >= number_of - 1 else 0
    given, spare = [largest] + [least] * (number_of - 1), total - largest - least * (number_of - 1)
    while spare > 0:
        free = [i for i in range(1, number_of) if given[i] < largest] or [i for i in range(1, number_of) if given[i] < most]
        mass, remaining = sum([weights[i] for i in free]), spare
        for i in free:
            addition = min(most - given[i], max(1, remaining * weights[i] // mass), spare)
            given[i] = given[i] + addition
            spare = spare - addition
    return np.array(given)


def bell_draw(stream_key, extent, deviation, most, split=(), held_as=jnp.bfloat16):
    loudness = shard_levels(stream_key, extent, split, -0.22, 0.18) if split else 1.0
    values = jax.random.normal(stream_key, extent, jnp.float32) * deviation * loudness
    return jnp.minimum(jnp.maximum(values, -most), most).astype(held_as)


def setup_inputs(seed: int = 0) -> dict:
    arg_keys = jax.random.split(jax.random.key(seed), 18)
    tokens = bell_draw(arg_keys[0], (MB, SLOTS, SLOT, D), 1.0, 6.0, ((1, 4), (2, 8)))
    cotangent = bell_draw(arg_keys[1], (MB, SLOTS, SLOT, D), 1.0, 6.0, ((1, 4), (2, 8)))
    routes_keys = jax.random.split(jax.random.fold_in(arg_keys[2], 1), MB * SLOTS * SLOT // TOK_DEV)
    routes_turns = jax.random.permutation(jax.random.fold_in(arg_keys[2], 3), MB * SLOTS * SLOT // TOK_DEV)
    routes = jax.vmap(lambda own, number: shared_out(jax.random.fold_in(arg_keys[2], 2), own, number, TOK_DEV, EXPERTS, TOP, CAP, 1))(routes_keys, routes_turns).reshape((MB, SLOTS, SLOT, TOP))
    lengths = draw_lengths(jax.random.fold_in(arg_keys[17], 71), 0)
    block_order = jax.random.permutation(arg_keys[4], BLOCKS).astype(jnp.int32)
    w_query = bell_draw(arg_keys[5], (D, D), D ** -0.5, 0.125, ((0, 32),))
    w_key = bell_draw(arg_keys[6], (D, D), D ** -0.5, 0.125, ((0, 32),))
    w_value = bell_draw(arg_keys[7], (D, D), D ** -0.5, 0.125, ((0, 32),))
    w_out = bell_draw(arg_keys[8], (D, D), (max(1, D // (SLOT // 4))) ** -0.5, 2.0, ((0, 32),))
    w_router = bell_draw(arg_keys[9], (D, EXPERTS), (4 * D) ** -0.5, 0.0625, ((0, 32),))
    w_gate = bell_draw(arg_keys[10], (EXPERTS, D, FFE), D ** -0.5, 0.125, ((0, 8), (1, 4)))
    w_up = bell_draw(arg_keys[11], (EXPERTS, D, FFE), D ** -0.5, 0.125, ((0, 8), (1, 4)))
    w_down = bell_draw(arg_keys[12], (EXPERTS, FFE, D), (max(1, FFE // 256)) ** -0.5, 3.0, ((0, 8), (1, 4)))
    attn_gain = jnp.clip(1.0 + 0.18 * jax.random.normal(arg_keys[13], (D,), jnp.float32), 0.099609375, 1.8984375).astype(jnp.bfloat16)
    mlp_gain = jnp.clip(1.0 + 0.18 * jax.random.normal(arg_keys[14], (D,), jnp.float32), 0.099609375, 1.8984375).astype(jnp.bfloat16)
    query_gain = jnp.clip(1.0 + 0.18 * jax.random.normal(arg_keys[15], (D,), jnp.float32), 0.099609375, 1.8984375).astype(jnp.bfloat16)
    key_gain = jnp.clip(1.0 + 0.18 * jax.random.normal(arg_keys[16], (D,), jnp.float32), 0.099609375, 1.8984375).astype(jnp.bfloat16)
    return {"tokens": tokens, "cotangent": cotangent, "routes": routes, "lengths": lengths, "block_order": block_order, "w_query": w_query, "w_key": w_key, "w_value": w_value, "w_out": w_out, "w_router": w_router, "w_gate": w_gate, "w_up": w_up, "w_down": w_down, "attn_gain": attn_gain, "mlp_gain": mlp_gain, "query_gain": query_gain, "key_gain": key_gain}


EPSILON = 1e-05
ROPE_BASE = 10000.0
MASKED = -1e+30

@jax.custom_vjp
def low(v):
    return lax.optimization_barrier(v.astype(jnp.bfloat16)).astype(jnp.float32)

@jax.custom_vjp
def low_back(v):
    return v

def low_keep(v):
    return (low(v), None)

def low_pass(kept, grad):
    return (grad,)

def back_keep(v):
    return (v, None)

def back_low(kept, grad):
    return (low(grad),)
low.defvjp(low_keep, low_pass)
low_back.defvjp(back_keep, back_low)

def matmul_high(left, right):
    return jnp.einsum('...d,df->...f', left, right, precision=lax.Precision.HIGHEST)

def rms_norm(values, gain_vec):
    return values * lax.rsqrt(lax.optimization_barrier(jnp.mean(values * values, axis=-1, keepdims=True)) + EPSILON) * gain_vec

def angles(places, head_width):
    index = jnp.arange(head_width // 2, dtype=jnp.float32)
    freqs = jnp.power(ROPE_BASE, -2.0 * index / head_width)
    turning = places.astype(jnp.float32)[:, None] * freqs[None, :]
    turning = jnp.concatenate([turning, turning], axis=1)
    return (jnp.cos(turning)[:, None, :], jnp.sin(turning)[:, None, :])

def rotate(values, cosine, sine):
    half_size = values.shape[-1] // 2
    turned = jnp.concatenate([-values[..., half_size:], values[..., :half_size]], axis=-1)
    return values * cosine + turned * sine

def attend(query, key_all, value_all, length, places):
    block_rows = math.gcd(SLOT, 512)
    count = SLOT // block_rows
    factor = 1.0 / math.sqrt(HEAD)
    query_blocks = query.reshape(count, block_rows, HEADS, HEAD)
    place_blocks = places.reshape(count, block_rows)

    def one_block(inputs):
        query_part, place_part = inputs
        scores = low_back(jnp.einsum('qhd,khd->hqk', query_part, key_all, precision=lax.Precision.HIGHEST) * factor)
        allowed = (places[None, :] <= place_part[:, None]) & (places[None, :] < length)
        scores = jnp.where(allowed[None], scores, MASKED)
        probs = low(jax.nn.softmax(scores, axis=-1))
        return jnp.einsum('hqk,khd->qhd', probs, value_all, precision=lax.Precision.HIGHEST)
    result = lax.map(jax.checkpoint(one_block), (query_blocks, place_blocks))
    return result.reshape(SLOT, HEADS, HEAD)

def experts_sum(mixed_flat, gates_flat, routes_batch, w_gate, w_up, w_down):
    blocks = SLOTS * N_CTX
    per_block = TOK_DEV * TOP
    expert_ids = routes_batch.reshape(blocks, per_block)
    match_marks = (expert_ids[:, :, None] == jnp.arange(EXPERTS, dtype=jnp.int32)[None, None, :]).astype(jnp.int32)
    slot_rank = lax.optimization_barrier(jnp.sum((jnp.cumsum(match_marks, axis=1) - 1) * match_marks, axis=2))
    slot_index = expert_ids * CAP + slot_rank
    block_index = jnp.broadcast_to(jnp.arange(blocks, dtype=jnp.int32)[:, None], (blocks, per_block))
    entry_number = jnp.broadcast_to(jnp.arange(per_block, dtype=jnp.int32)[None, :] + 1, (blocks, per_block))
    slot_table = jnp.zeros((blocks, EXPERTS * CAP), jnp.int32).at[block_index, slot_index].set(entry_number)
    slot_table = slot_table.reshape(blocks, EXPERTS, CAP).transpose(1, 0, 2).reshape(EXPERTS, blocks * CAP)
    starts = jnp.broadcast_to((jnp.arange(blocks, dtype=jnp.int32) * per_block)[:, None], (blocks, CAP)).reshape(blocks * CAP)
    live_slots = slot_table > 0
    assign = jnp.where(live_slots, starts[None, :] + slot_table - 1, 0)

    def expert_step(summed, inputs):
        gate_weight, up_weight, down_weight, picked, slot_live = inputs
        gathered = jnp.where(slot_live[:, None], mixed_flat[picked // TOP], 0.0)
        gathered = low_back(gathered)
        gate_pre = low_back(matmul_high(gathered, gate_weight))
        up_pre = low_back(matmul_high(gathered, up_weight))
        hidden = low(jax.nn.silu(gate_pre) * up_pre)
        result = low(low_back(matmul_high(hidden, down_weight)))
        weight = jnp.where(slot_live, gates_flat[picked], 0.0)
        return (summed.at[picked // TOP].add(weight[:, None] * result), None)
    start_sum = jnp.zeros((SLOTS * SLOT, D), jnp.float32)
    summed, _ = lax.scan(jax.checkpoint(expert_step), start_sum, (w_gate, w_up, w_down, assign, live_slots))
    return summed

def layer(inputs, w_query, w_key, w_value, w_out, w_router, w_gate, w_up, w_down, attn_gain, mlp_gain, query_gain, key_gain, routes_batch, lengths_batch, places):
    act = low(rms_norm(inputs, attn_gain))
    query_n = rms_norm(low_back(matmul_high(act, w_query)), query_gain)
    key_n = rms_norm(low_back(matmul_high(act, w_key)), key_gain)
    values = low(low_back(matmul_high(act, w_value)))
    cosine, sine = angles(places, HEAD)
    query = low(rotate(query_n.reshape(SLOTS, SLOT, HEADS, HEAD), cosine, sine))
    key_rot = low(rotate(key_n.reshape(SLOTS, SLOT, HEADS, HEAD), cosine, sine))
    values = values.reshape(SLOTS, SLOT, HEADS, HEAD)
    attended = jax.vmap(attend, in_axes=(0, 0, 0, 0, None))(query, key_rot, values, lengths_batch, places)
    attended = low(low_back(attended.reshape(SLOTS, SLOT, D)))
    x_mid = inputs + low_back(matmul_high(attended, w_out))
    mixed_in = low(rms_norm(x_mid, mlp_gain))
    router = jax.nn.softmax(low_back(matmul_high(mixed_in, w_router)), axis=-1)
    gates = jnp.take_along_axis(router, routes_batch, axis=-1)
    moe_sum = experts_sum(mixed_in.reshape(SLOTS * SLOT, D), gates.reshape(SLOTS * SLOT * TOP), routes_batch, w_gate, w_up, w_down)
    return x_mid + moe_sum.reshape(SLOTS, SLOT, D)

def reference(tokens, cotangent, routes, lengths, block_order, w_query, w_key, w_value, w_out, w_router, w_gate, w_up, w_down, attn_gain, mlp_gain, query_gain, key_gain):
    stored = jnp.arange(SLOT, dtype=jnp.int32)
    half_size = TOK_DEV // 2
    places = block_order[stored // half_size] * half_size + stored % half_size
    params = tuple((item.astype(jnp.float32) for item in (w_query, w_key, w_value, w_out, w_router, w_gate, w_up, w_down, attn_gain, mlp_gain, query_gain, key_gain)))
    outputs = []
    input_grads = []
    param_grads = [jnp.zeros(item.shape, jnp.float32) for item in params]
    for batch_index in range(MB):
        routes_batch = routes[batch_index]
        lengths_batch = lengths[batch_index]

        def forward(inputs, *weights):
            return layer(inputs, *weights, routes_batch, lengths_batch, places)
        result, pullback = jax.vjp(forward, tokens[batch_index].astype(jnp.float32), *params)
        grads = pullback(cotangent[batch_index].astype(jnp.float32))
        outputs.append(result.astype(jnp.bfloat16))
        input_grads.append(grads[0])
        param_grads = [total + part for total, part in zip(param_grads, grads[1:])]
    return (jnp.stack(outputs), jnp.stack(input_grads), param_grads[0], param_grads[1], param_grads[2], param_grads[3], param_grads[4], param_grads[5], param_grads[6], param_grads[7], param_grads[8], param_grads[9], param_grads[10], param_grads[11])
```

```python
import math

import jax
import jax.numpy as jnp
from jax import lax
from jax.sharding import Mesh
from jax.sharding import PartitionSpec as P

HEAD = 128
EPSILON = 1e-05
ROPE_BASE = 10000.0
MASKED = -1e30
BF = jnp.bfloat16
F32 = jnp.float32
DP = ("half", "lane")
CTX = ("quad", "pair")
ALL = DP + CTX


def dot(spec, left, right):
    return jnp.einsum(spec, left, right, preferred_element_type=F32)


def inv_rms(values):
    return lax.rsqrt(jnp.mean(values * values, axis=-1, keepdims=True) + EPSILON)


def norm_back(values, inv_root, gain_vec, grad_in):
    weighted = grad_in * gain_vec
    inner = jnp.mean(weighted * values, axis=-1, keepdims=True)
    grad_values = inv_root * weighted - values * (inv_root * inv_root * inv_root) * inner
    return (grad_values, jnp.sum(grad_in * values * inv_root, axis=0))


def angles(places, head_width):
    index = jnp.arange(head_width // 2, dtype=F32)
    freqs = jnp.power(ROPE_BASE, -2.0 * index / head_width)
    turning = places.astype(F32)[:, None] * freqs[None, :]
    turning = jnp.concatenate([turning, turning], axis=1)
    return (jnp.cos(turning)[:, None, :], jnp.sin(turning)[:, None, :])


def rotate(values, cosine, sine):
    half_size = values.shape[-1] // 2
    turned = jnp.concatenate([-values[..., half_size:], values[..., :half_size]], axis=-1)
    return values * cosine + turned * sine


def rotate_back(grad_in, cosine, sine):
    half_size = grad_in.shape[-1] // 2
    moved = grad_in * sine
    return grad_in * cosine + jnp.concatenate(
        [moved[..., half_size:], -moved[..., :half_size]], axis=-1
    )


def swap(values, axis):
    return lax.ppermute(values, axis, [(0, 1), (1, 0)])


def exchange(blocks, axes):
    return lax.all_to_all(blocks, axes, split_axis=0, concat_axis=0, tiled=True)


def spread(values, axes):
    count = lax.axis_size(axes)
    return exchange(jnp.broadcast_to(values[None], (count,) + values.shape), axes)


def gather_ctx(rows):
    own = spread(rows, "quad")
    return jnp.stack([own, swap(own, "pair")])


def scatter_ctx(own_part, other_part):
    merged = own_part.astype(F32) + swap(other_part.astype(BF), "pair").astype(F32)
    received = exchange(merged.astype(BF), "quad")
    return jnp.sum(received.astype(F32), axis=0)


def relative(blocks):
    split = blocks.reshape((-1, 2) + blocks.shape[1:]).swapaxes(0, 1)
    return jnp.where(lax.axis_index("pair") == 0, split, split[::-1])


def absolute(blocks):
    split = jnp.where(lax.axis_index("pair") == 0, blocks, blocks[::-1])
    return split.swapaxes(0, 1).reshape((-1,) + blocks.shape[2:])


def sum_ctx(values):
    values = values + swap(values, "pair")[:, ::-1]
    count = lax.axis_size("quad")
    step = 1
    while step < count:
        values = values + lax.ppermute(values, "quad", [(i, i ^ step) for i in range(count)])
        step *= 2
    return values


def gather_lane(values):
    if lax.axis_size("lane") == 2:
        other = swap(values, "lane")
        first = lax.axis_index("lane") == 0
        return jnp.stack([jnp.where(first, values, other), jnp.where(first, other, values)])
    return lax.all_gather(values, "lane", axis=0, tiled=False)


def scatter_lane(values):
    count = lax.axis_size("lane")
    here = lax.axis_index("lane")
    own = lax.dynamic_index_in_dim(values, here, 0, keepdims=False)
    if count == 2:
        other = lax.dynamic_index_in_dim(values, 1 - here, 0, keepdims=False)
        return own + swap(other.astype(BF), "lane").astype(F32)
    return lax.psum_scatter(values.astype(BF), "lane", scatter_dimension=0, tiled=False).astype(F32)


def reduce_small(values):
    over_ctx = jnp.sum(exchange(values.swapaxes(0, 1), CTX), axis=0)
    return jnp.sum(exchange(over_ctx, DP), axis=0)


def on_device(
    tokens,
    cotangent,
    routes,
    lengths,
    block_order,
    w_query,
    w_key,
    w_value,
    w_out,
    w_router,
    w_gate,
    w_up,
    w_down,
    attn_gain,
    mlp_gain,
    query_gain,
    key_gain,
):
    batches, _, rows, width = tokens.shape
    dp_size = lax.axis_size(DP)
    ctx_size = lax.axis_size(CTX)
    quads = lax.axis_size("quad")
    lanes = lax.axis_size("lane")
    slot_len = rows * ctx_size
    block_rows = rows // 2
    head_width = width // ctx_size
    heads = head_width // HEAD
    shard = w_query.shape[0]
    expert_count = w_router.shape[1]
    local_experts = w_gate.shape[0]
    hidden_units = w_gate.shape[2]
    hidden_half = hidden_units // 2
    depth_part = w_gate.shape[1]
    factor = 1.0 / math.sqrt(HEAD)
    half = lax.axis_index("half")
    pair = lax.axis_index("pair")

    small = jnp.concatenate(
        [attn_gain, mlp_gain, query_gain, key_gain, w_router.reshape(shard * expert_count)]
    )
    small = spread(spread(small, CTX), DP).reshape(dp_size * ctx_size, -1)
    gain_attn = small[:, :shard].reshape(width).astype(F32)
    gain_mlp = small[:, shard : 2 * shard].reshape(width).astype(F32)
    gain_query = small[:, 2 * shard : 3 * shard].reshape(ctx_size, head_width)
    gain_key = small[:, 3 * shard : 4 * shard].reshape(ctx_size, head_width)
    router_w = small[:, 4 * shard :].reshape(width, expert_count)
    here = lax.axis_index(CTX)
    gain_query = lax.dynamic_index_in_dim(gain_query, here, 0, keepdims=False).astype(F32)
    gain_key = lax.dynamic_index_in_dim(gain_key, here, 0, keepdims=False).astype(F32)

    qkv = jnp.stack([w_query, w_key, w_value], axis=1).reshape(shard, 3, ctx_size, head_width)
    qkv = exchange(
        qkv.transpose(2, 0, 1, 3).reshape(ctx_size, shard, 3 * head_width), CTX
    ).reshape(ctx_size * shard, 3 * head_width)
    qkv_w = lax.all_gather(qkv, DP, axis=0, tiled=True)
    out_w = lax.all_gather(w_out, ALL, axis=0, tiled=True)

    def gather_depth(weights):
        split = weights.reshape(local_experts, depth_part, 2, hidden_half)
        own = lax.dynamic_index_in_dim(split, half, 2, keepdims=False)
        other = swap(lax.dynamic_index_in_dim(split, 1 - half, 2, keepdims=False), "half")
        first = half == 0
        both = jnp.stack([jnp.where(first, own, other), jnp.where(first, other, own)])
        gathered = gather_lane(both)
        return gathered.transpose(2, 1, 0, 3, 4).reshape(local_experts, width, hidden_half)

    down_w = gather_lane(w_down).transpose(1, 0, 2, 3).reshape(local_experts, hidden_half, width)
    gate_w = gather_depth(w_gate)
    up_w = gather_depth(w_up)

    def places_of(device):
        stored = device * rows + jnp.arange(rows, dtype=jnp.int32)
        match_marks = (stored // block_rows)[:, None] == jnp.arange(
            block_order.shape[0], dtype=jnp.int32
        )[None, :]
        first_place = jnp.sum(jnp.where(match_marks, block_order[None, :], 0), axis=1)
        return first_place * block_rows + stored % block_rows

    places = jnp.concatenate(
        [places_of(quad * 2 + (pair ^ other)) for other in range(2) for quad in range(quads)]
    )
    cosine, sine = angles(places, HEAD)
    expert_range = jnp.arange(expert_count, dtype=jnp.int32)

    saved = []
    for m in range(batches):
        inputs = tokens[m, 0].astype(F32)
        attn_root = inv_rms(inputs)
        act_own = (inputs * attn_root * gain_attn).astype(BF)
        act = gather_ctx(act_own).reshape(slot_len, width)
        pre = dot("td,de->te", act, qkv_w)
        query_pre = pre[:, :head_width]
        key_pre = pre[:, head_width : 2 * head_width]
        value = pre[:, 2 * head_width :].astype(BF).reshape(slot_len, heads, HEAD)
        squares = jnp.stack(
            [jnp.sum(query_pre * query_pre, axis=1), jnp.sum(key_pre * key_pre, axis=1)]
        ).reshape(2, 2, slot_len // 2)
        squares = sum_ctx(squares).reshape(2, slot_len, 1)
        query_root = lax.rsqrt(squares[0] / width + EPSILON)
        key_root = lax.rsqrt(squares[1] / width + EPSILON)
        query = rotate(
            (query_pre * query_root * gain_query).reshape(slot_len, heads, HEAD), cosine, sine
        ).astype(BF)
        key = rotate(
            (key_pre * key_root * gain_key).reshape(slot_len, heads, HEAD), cosine, sine
        ).astype(BF)
        allowed = (places[None, :] <= places[:, None]) & (places[None, :] < lengths[m, 0])
        scores = dot("qhd,khd->hqk", query, key) * factor
        scores = jnp.where(allowed[None], scores, MASKED)
        expo = jnp.exp(scores - jnp.max(scores, axis=-1, keepdims=True))
        probs = expo / jnp.sum(expo, axis=-1, keepdims=True)
        probs_low = probs.astype(BF)
        attended = dot("hqk,khd->qhd", probs_low, value).astype(BF)
        attended = exchange(absolute(attended.reshape(2, quads, rows, head_width)), CTX)
        attended = attended.transpose(1, 0, 2).reshape(rows, width)
        x_mid = inputs + dot("td,de->te", attended, out_w)
        mlp_root = inv_rms(x_mid)
        mixed_in = (x_mid * mlp_root * gain_mlp).astype(BF)
        router = jax.nn.softmax(dot("td,de->te", mixed_in, router_w), axis=-1)
        routed = jnp.any(routes[m, 0][:, :, None] == expert_range[None, None, :], axis=1)
        routed = routed.astype(F32)
        gates = (router * routed).T.reshape(ctx_size, local_experts, rows)
        gates = relative(exchange(gates, CTX))
        gates = gates.transpose(0, 1, 3, 2).reshape(2, slot_len // 2, local_experts)
        grad_low = cotangent[m, 0]
        chunks = []
        for rows_in, grad_in, gate_in in (
            (swap(mixed_in, "half"), swap(grad_low, "half"), swap(gates, "half")),
            (mixed_in, grad_low, gates),
        ):
            chunks.append(
                (
                    gather_ctx(rows_in).reshape(slot_len, width),
                    gather_ctx(grad_in).reshape(slot_len, width),
                    gate_in.reshape(slot_len, local_experts),
                )
            )
        saved.append(
            dict(
                inputs=inputs, attn_root=attn_root, act=act, query_pre=query_pre,
                key_pre=key_pre, query_root=query_root, key_root=key_root, query=query, key=key,
                value=value, probs=probs, probs_low=probs_low, attended=attended, x_mid=x_mid,
                mlp_root=mlp_root, mixed_in=mixed_in, router=router, routed=routed,
                grad_low=grad_low, chunks=chunks,
            )
        )

    outputs = []
    input_grads = []
    x_list, g_list, hid_list, dgate_list, dup_list = [], [], [], [], []
    part_mlp_gain = part_attn_gain = part_query_gain = part_key_gain = 0.0
    for m in range(batches):
        s = saved[m]
        sums = []
        for x_rows, g_rows, gate in s["chunks"]:
            gate = gate[:, :, None]
            gate_pre = dot("td,edf->tef", x_rows, gate_w)
            up_pre = dot("td,edf->tef", x_rows, up_w)
            d_hidden = dot("td,efd->tef", g_rows, down_w)
            sigma = jax.nn.sigmoid(gate_pre)
            hidden = gate_pre * sigma * up_pre
            d_gates = jnp.sum(hidden * d_hidden, axis=2)
            scaled = (hidden * gate).astype(BF)
            d_hidden = d_hidden * gate
            d_gate_pre = (d_hidden * up_pre * sigma * (1.0 + gate_pre * (1.0 - sigma))).astype(BF)
            d_up_pre = (d_hidden * gate_pre * sigma).astype(BF)
            moe = dot("tef,efd->td", scaled, down_w).astype(BF)
            d_rows = dot("tef,edf->td", d_gate_pre, gate_w)
            d_rows = (d_rows + dot("tef,edf->td", d_up_pre, up_w)).astype(BF)
            moe = moe.reshape(2, quads, rows, width)
            d_rows = d_rows.reshape(2, quads, rows, width)
            sums.append((scatter_ctx(moe[0], moe[1]), scatter_ctx(d_rows[0], d_rows[1]), d_gates))
            x_list.append(x_rows)
            g_list.append(g_rows)
            hid_list.append(scaled)
            dgate_list.append(d_gate_pre)
            dup_list.append(d_up_pre)
        partner, own = sums
        moe_sum = own[0] + swap(partner[0].astype(BF), "half").astype(F32)
        d_mixed = own[1] + swap(partner[1].astype(BF), "half").astype(F32)
        d_gates = own[2] + swap(partner[2], "half")
        d_gates = d_gates.reshape(2, quads, rows, local_experts).swapaxes(2, 3)
        d_router = exchange(absolute(d_gates), CTX).reshape(expert_count, rows).T * s["routed"]
        outputs.append((s["x_mid"] + moe_sum).astype(BF))
        router = s["router"]
        d_logits = (
            router * (d_router - jnp.sum(router * d_router, axis=-1, keepdims=True))
        ).astype(BF)
        s["d_logits"] = d_logits
        d_mixed = d_mixed + dot("te,de->td", d_logits, router_w)
        d_mid, gain_part = norm_back(s["x_mid"], s["mlp_root"], gain_mlp, d_mixed)
        part_mlp_gain = part_mlp_gain + gain_part
        d_mid = d_mid + s["grad_low"].astype(F32)
        d_att_out = d_mid.astype(BF)
        s["d_att_out"] = d_att_out
        d_attended = dot("te,de->td", d_att_out, out_w).astype(BF)
        d_attended = exchange(
            d_attended.reshape(rows, ctx_size, head_width).swapaxes(0, 1), CTX
        )
        d_attended = relative(d_attended).reshape(slot_len, heads, HEAD)
        probs, query, key = s["probs"], s["query"], s["key"]
        d_probs = dot("qhd,khd->hqk", d_attended, s["value"])
        inner = jnp.sum(probs * d_probs, axis=-1, keepdims=True)
        d_scores = (probs * (d_probs - inner)).astype(BF)
        d_query = dot("hqk,khd->qhd", d_scores, key) * factor
        d_key = dot("hqk,qhd->khd", d_scores, query) * factor
        d_value = dot("hqk,qhd->khd", s["probs_low"], d_attended)
        d_query = rotate_back(d_query, cosine, sine).reshape(slot_len, head_width)
        d_key = rotate_back(d_key, cosine, sine).reshape(slot_len, head_width)
        query_pre, key_pre = s["query_pre"], s["key_pre"]
        query_root, key_root = s["query_root"], s["key_root"]
        inners = jnp.stack(
            [
                jnp.sum(d_query * gain_query * query_pre, axis=1),
                jnp.sum(d_key * gain_key * key_pre, axis=1),
            ]
        ).reshape(2, 2, slot_len // 2)
        inners = sum_ctx(inners).reshape(2, slot_len, 1) / width
        d_query_pre = query_root * (d_query * gain_query) - query_pre * query_root**3 * inners[0]
        d_key_pre = key_root * (d_key * gain_key) - key_pre * key_root**3 * inners[1]
        part_query_gain = part_query_gain + jnp.sum(d_query * query_pre * query_root, axis=0)
        part_key_gain = part_key_gain + jnp.sum(d_key * key_pre * key_root, axis=0)
        d_pre = jnp.concatenate(
            [
                d_query_pre.astype(BF),
                d_key_pre.astype(BF),
                d_value.reshape(slot_len, head_width).astype(BF),
            ],
            axis=1,
        )
        s["d_pre"] = d_pre
        d_act = dot("te,de->td", d_pre, qkv_w).astype(BF).reshape(2, quads, rows, width)
        d_act = scatter_ctx(d_act[0], d_act[1])
        d_inputs, gain_part = norm_back(s["inputs"], s["attn_root"], gain_attn, d_act)
        part_attn_gain = part_attn_gain + gain_part
        input_grads.append(d_inputs + d_mid)

    def both(name):
        return jnp.concatenate([s[name] for s in saved], axis=0)

    x_all = jnp.concatenate(x_list, axis=0)
    g_all = jnp.concatenate(g_list, axis=0)
    grad_down = dot("tef,td->efd", jnp.concatenate(hid_list, axis=0), g_all)
    grad_down = grad_down.reshape(local_experts, lanes, -1, width).swapaxes(0, 1)
    grad_down = scatter_lane(grad_down)

    def scatter_depth(parts):
        grad = dot("td,tef->edf", x_all, jnp.concatenate(parts, axis=0))
        grad = grad.reshape(local_experts, 2, lanes, depth_part, hidden_half)
        grad = scatter_lane(grad.transpose(2, 1, 0, 3, 4)).astype(BF)
        own = lax.dynamic_index_in_dim(grad, half, 0, keepdims=False)
        other = swap(lax.dynamic_index_in_dim(grad, 1 - half, 0, keepdims=False), "half")
        first = half == 0
        return jnp.concatenate(
            [jnp.where(first, own, other), jnp.where(first, other, own)], axis=2
        ).astype(F32)

    grad_gate = scatter_depth(dgate_list)
    grad_up = scatter_depth(dup_list)

    grad_out = dot("td,te->de", both("attended"), both("d_att_out")).astype(BF)
    grad_out = lax.psum_scatter(grad_out, ALL, scatter_dimension=0, tiled=True).astype(F32)
    grad_qkv = dot("td,te->de", both("act"), both("d_pre")).astype(BF)
    grad_qkv = lax.psum_scatter(grad_qkv, DP, scatter_dimension=0, tiled=True)
    grad_qkv = exchange(grad_qkv.reshape(ctx_size, shard, 3 * head_width), CTX).astype(F32)
    grad_qkv = grad_qkv.reshape(ctx_size, shard, 3, head_width).transpose(2, 1, 0, 3)
    grad_qkv = grad_qkv.reshape(3, shard, width)

    grad_router = dot("td,te->de", both("mixed_in"), both("d_logits"))
    columns = jnp.arange(ctx_size, dtype=jnp.int32)[:, None] == here

    def placed(part):
        return jnp.where(columns, part[None, :], 0.0).reshape(width)

    gains = jnp.stack(
        [part_attn_gain, part_mlp_gain, placed(part_query_gain), placed(part_key_gain)]
    )
    gains = gains.reshape(4, dp_size, ctx_size, shard).transpose(1, 2, 0, 3)
    packed = jnp.concatenate(
        [
            gains.reshape(dp_size, ctx_size, 4 * shard),
            grad_router.reshape(dp_size, ctx_size, shard * expert_count),
        ],
        axis=2,
    )
    packed = reduce_small(packed)
    return (
        jnp.stack(outputs).reshape(batches, 1, rows, width),
        jnp.stack(input_grads).reshape(batches, 1, rows, width),
        grad_qkv[0],
        grad_qkv[1],
        grad_qkv[2],
        grad_out,
        packed[4 * shard :].reshape(shard, expert_count),
        grad_gate,
        grad_up,
        grad_down,
        packed[:shard],
        packed[shard : 2 * shard],
        packed[2 * shard : 3 * shard],
        packed[3 * shard : 4 * shard],
    )


def solution(mesh):
    dp_size, ctx_size = mesh.shape["dp"], mesh.shape["ctx"]
    grid = Mesh(mesh.devices.reshape(2, dp_size // 2, ctx_size // 2, 2), ALL)
    rows = P(None, DP, CTX, None)
    dense = P(ALL, None)
    expert = P(CTX, DP, None)
    vector = P(ALL)
    return jax.shard_map(
        on_device,
        mesh=grid,
        in_specs=(rows, rows, rows, P(None, DP), P())
        + (dense,) * 5
        + (expert,) * 3
        + (vector,) * 4,
        out_specs=(rows, rows) + (dense,) * 5 + (expert,) * 3 + (vector,) * 4,
        check_vma=False,
    )
```

```python
import functools
import math

import jax
import jax.numpy as jnp
from jax import lax
from jax.experimental import pallas as pl
from jax.experimental.pallas import tpu as pltpu
from jax.sharding import Mesh
from jax.sharding import PartitionSpec as P

HEAD = 128
EPSILON = 1e-05
ROPE_BASE = 10000.0
MASKED = -1e30
BF = jnp.bfloat16
F32 = jnp.float32
DP = ("half", "lane")
CTX = ("quad", "pair")
ALL = DP + CTX
MESH = pl.DeviceIdType.MESH


def dot(spec, left, right):
    return jnp.einsum(spec, left, right, preferred_element_type=F32)


def inv_rms(values):
    return lax.rsqrt(jnp.mean(values * values, axis=-1, keepdims=True) + EPSILON)


def norm_back(values, inv_root, gain_vec, grad_in):
    weighted = grad_in * gain_vec
    inner = jnp.mean(weighted * values, axis=-1, keepdims=True)
    grad_values = inv_root * weighted - values * (inv_root * inv_root * inv_root) * inner
    return (grad_values, jnp.sum(grad_in * values * inv_root, axis=0))


def angles(places, head_width):
    index = jnp.arange(head_width // 2, dtype=F32)
    freqs = jnp.power(ROPE_BASE, -2.0 * index / head_width)
    turning = places.astype(F32)[:, None] * freqs[None, :]
    turning = jnp.concatenate([turning, turning], axis=1)
    return (jnp.cos(turning)[:, None, :], jnp.sin(turning)[:, None, :])


def rotate(values, cosine, sine):
    half_size = values.shape[-1] // 2
    turned = jnp.concatenate([-values[..., half_size:], values[..., :half_size]], axis=-1)
    return values * cosine + turned * sine


def rotate_back(grad_in, cosine, sine):
    half_size = grad_in.shape[-1] // 2
    moved = grad_in * sine
    return grad_in * cosine + jnp.concatenate(
        [moved[..., half_size:], -moved[..., :half_size]], axis=-1
    )


def swap(values, axis):
    return lax.ppermute(values, axis, [(0, 1), (1, 0)])


def exchange(blocks, axes):
    return lax.all_to_all(blocks, axes, split_axis=0, concat_axis=0, tiled=True)


def spread(values, axes):
    count = lax.axis_size(axes)
    return exchange(jnp.broadcast_to(values[None], (count,) + values.shape), axes)


def from_relative(blocks):
    quads = blocks.shape[1]
    pair, quad = lax.axis_index("pair"), lax.axis_index("quad")
    cores = jnp.where(pair == 0, blocks, blocks[::-1])
    step = 1
    while step < quads:
        split = cores.reshape((2, quads // (2 * step), 2, step) + blocks.shape[2:])
        flipped = split[:, :, ::-1].reshape(blocks.shape)
        cores = jnp.where((quad & step) == 0, cores, flipped)
        step *= 2
    return cores.swapaxes(0, 1).reshape((2 * quads,) + blocks.shape[2:])


def to_relative(blocks):
    split = blocks.reshape((-1, 2) + blocks.shape[1:]).swapaxes(0, 1)
    again = from_relative(split)
    return again.reshape((-1, 2) + blocks.shape[1:]).swapaxes(0, 1)


def sum_ctx(values):
    values = values + swap(values, "pair")[:, ::-1]
    kinds, _, quads = values.shape[:3]
    step = 1
    while step < quads:
        moved = lax.ppermute(values, "quad", [(i, i ^ step) for i in range(quads)])
        split = moved.reshape((kinds, 2, quads // (2 * step), 2, step, -1))
        values = values + split[:, :, :, ::-1].reshape(values.shape)
        step *= 2
    return values


def gather_lane(values):
    if lax.axis_size("lane") == 2:
        other = swap(values, "lane")
        first = lax.axis_index("lane") == 0
        return jnp.stack([jnp.where(first, values, other), jnp.where(first, other, values)])
    return lax.all_gather(values, "lane", axis=0, tiled=False)


def scatter_lane(values):
    count = lax.axis_size("lane")
    here = lax.axis_index("lane")
    if count == 2:
        own = jnp.where(here == 0, values[0], values[1])
        other = jnp.where(here == 0, values[1], values[0]).astype(BF)
        return own + swap(other, "lane").astype(F32)
    return lax.psum_scatter(values.astype(BF), "lane", scatter_dimension=0, tiled=False).astype(F32)


def reduce_small(values):
    over_ctx = jnp.sum(exchange(values.swapaxes(0, 1), CTX), axis=0)
    return jnp.sum(exchange(over_ctx, DP), axis=0)


def toggled(index, bits):
    step = 1
    while step <= bits:
        if bits & step:
            index = index + step - 2 * step * ((index // step) % 2)
        step *= 2
    return index


def greet(peers):
    barrier = pltpu.get_barrier_semaphore()
    for peer in peers:
        pl.semaphore_signal(barrier, inc=1, device_id=peer, device_id_type=MESH)
    pl.semaphore_wait(barrier, len(peers))


def gather_sems(quads, count, partner):
    return count * (2 if partner else 1) * (13 if quads == 4 else 2 * quads - 1) + (count if partner else 0)


def gather_body(quads, count, partner, x_ref, own_ref, other_ref, *rest):
    if partner:
        keep_ref, local, send, recv = rest
    else:
        keep_ref = None
        local, send, recv = rest
    rows = x_ref.shape[1]
    half = rows // 2
    first, second = pl.ds(0, half), pl.ds(half, half)
    quad = lax.axis_index("quad")
    to_quad = [{"quad": toggled(quad, k)} for k in range(quads)]
    sibling = {"pair": 1 - lax.axis_index("pair")}
    peers = to_quad[1:] + [sibling]
    if partner:
        across = {"half": 1 - lax.axis_index("half")}
        peers = peers + [across]
    greet(peers)
    number = iter(range(send.shape[0]))

    def copy(src, dst, device):
        i = next(number)
        return pltpu.make_async_remote_copy(
            src_ref=src, dst_ref=dst, send_sem=send.at[i], recv_sem=recv.at[i],
            device_id=device, device_id_type=MESH)

    finish = []

    def go(*copies):
        for c in copies:
            c.start()
            finish.append(c)

    def at(ref, k, s, part=None):
        view = ref.at[k, s]
        return view if part is None else view.at[part]

    def plan(src, s):
        p = {}
        p["o0"] = copy(src, at(other_ref, 0, s), sibling)
        if quads == 4:
            for k in (1, 2):
                for name, part in (("a", first), ("b", second)):
                    p[f"s{k}{name}"] = copy(src.at[part], at(own_ref, k, s, part), to_quad[k])
            p["f3a"] = copy(at(own_ref, 1, s, first), at(own_ref, 3, s, first), to_quad[2])
            p["f3b"] = copy(at(own_ref, 2, s, second), at(own_ref, 3, s, second), to_quad[1])
            for k in (1, 2, 3):
                for name, part in (("a", first), ("b", second)):
                    p[f"o{k}{name}"] = copy(
                        at(own_ref, k, s, part), at(other_ref, k, s, part), sibling)
        else:
            for k in range(1, quads):
                p[f"s{k}"] = copy(src, at(own_ref, k, s), to_quad[k])
                p[f"o{k}"] = copy(at(own_ref, k, s), at(other_ref, k, s), sibling)
        return p

    def begin(p):
        if quads == 4:
            go(p["s1a"], p["s2b"], p["s1b"], p["s2a"], p["o0"])
        else:
            go(*[p[f"s{k}"] for k in range(1, quads)], p["o0"])

    def forward(p):
        if quads == 4:
            p["s1a"].wait_recv(); go(p["f3a"], p["o1a"])
            p["s2b"].wait_recv(); go(p["f3b"], p["o2b"])
            p["s1b"].wait_recv(); go(p["o1b"])
            p["s2a"].wait_recv(); go(p["o2a"])
        else:
            for k in range(1, quads):
                p[f"s{k}"].wait_recv(); go(p[f"o{k}"])

    def last(p):
        if quads == 4:
            p["f3a"].wait_recv(); go(p["o3a"])
            p["f3b"].wait_recv(); go(p["o3b"])

    def done(p):
        for name, c in p.items():
            if name[0] == "o":
                c.wait_recv()

    locals_ = []
    plans = []
    zs = []
    if partner:
        for s in range(count):
            z = copy(x_ref.at[s], keep_ref.at[s], across)
            go(z)
            zs.append(z)
    for s in range(count):
        p = plan(x_ref.at[s], s)
        begin(p)
        plans.append(p)
        c = pltpu.make_async_copy(x_ref.at[s], own_ref.at[0, s], local.at[s])
        c.start()
        locals_.append(c)
    for p in plans:
        forward(p)
    for p in plans:
        last(p)
    if partner:
        later = []
        for s in range(count):
            zs[s].wait_recv()
            p = plan(keep_ref.at[s], count + s)
            begin(p)
            later.append(p)
            c = pltpu.make_async_copy(keep_ref.at[s], own_ref.at[0, count + s], local.at[count + s])
            c.start()
            locals_.append(c)
        for p in later:
            forward(p)
        for p in later:
            last(p)
        plans += later
    for p in plans:
        done(p)
    for c in finish:
        c.wait_send()
    for c in locals_:
        c.wait()


def gather_rows(x, partner, name, cid):
    count, rows, width = x.shape
    quads = lax.axis_size("quad")
    total = count * (2 if partner else 1)
    sems = gather_sems(quads, count, partner)
    shape = jax.ShapeDtypeStruct((quads, total, rows, width), x.dtype)
    scratch = [pltpu.VMEM((count, rows, width), x.dtype)] if partner else []
    return pl.pallas_call(
        functools.partial(gather_body, quads, count, partner),
        out_shape=(shape, shape),
        in_specs=[pl.BlockSpec(memory_space=pltpu.VMEM)],
        out_specs=(pl.BlockSpec(memory_space=pl.ANY),) * 2,
        scratch_shapes=scratch + [
            pltpu.SemaphoreType.DMA((total,)),
            pltpu.SemaphoreType.DMA((sems,)),
            pltpu.SemaphoreType.DMA((sems,)),
        ],
        compiler_params=pltpu.CompilerParams(collective_id=cid, has_side_effects=True),
        name=name,
    )(x)


def scatter_sems(quads, total, partner):
    per = quads + (6 if quads == 4 else quads - 1)
    return total * per + (total // 2 if partner else 0)


def add_rows(out_ref, *refs):
    rows = out_ref.shape[0]
    step = 16

    @pl.loop(0, rows // step)
    def _(i):
        part = pl.ds(pl.multiple_of(i * step, step), step)
        total = refs[0][part].astype(F32)
        for ref in refs[1:]:
            total = total + ref[part].astype(F32)
        out_ref[part] = total.astype(out_ref.dtype)


def scatter_body(quads, count, partner, own_ref, other_ref, out_ref, *rest):
    if partner:
        mine, theirs, merged, relay, arrived, summed, back, local, send, recv = rest
    else:
        mine, theirs, merged, relay, arrived, local, send, recv = rest
        summed = back = None
    total, rows = own_ref.shape[1:3]
    half = rows // 2
    first, second = pl.ds(0, half), pl.ds(half, half)
    quad = lax.axis_index("quad")
    to_quad = [{"quad": toggled(quad, k)} for k in range(quads)]
    sibling = {"pair": 1 - lax.axis_index("pair")}
    peers = to_quad[1:] + [sibling]
    if partner:
        across = {"half": 1 - lax.axis_index("half")}
        peers = peers + [across]
    greet(peers)
    number = iter(range(send.shape[0]))

    def copy(src, dst, device):
        i = next(number)
        return pltpu.make_async_remote_copy(
            src_ref=src, dst_ref=dst, send_sem=send.at[i], recv_sem=recv.at[i],
            device_id=device, device_id_type=MESH)

    finish = []

    def go(c):
        c.start()
        finish.append(c)
        return c

    order = list(range(count, total)) + list(range(count))
    ks = [3, 1, 2, 0] if quads == 4 else list(range(quads - 1, -1, -1))
    sib, loc = {}, {}
    for s in order:
        for k in ks:
            sib[s, k] = go(copy(other_ref.at[k, s], theirs.at[s, k], sibling))
            loc[s, k] = pltpu.make_async_copy(own_ref.at[k, s], mine.at[s, k], local.at[s * quads + k])
            loc[s, k].start()
    sends = {}
    for s in order:
        for k in ks:
            sib[s, k].wait_recv()
            loc[s, k].wait()
            add_rows(merged.at[s, k], mine.at[s, k], theirs.at[s, k])
            if quads == 4:
                if k == 3:
                    sends[s, "3a"] = go(copy(merged.at[s, 3, first], relay.at[s, 0], to_quad[2]))
                    sends[s, "3b"] = go(copy(merged.at[s, 3, second], relay.at[s, 1], to_quad[1]))
                elif k == 1:
                    sends[s, "1b"] = go(copy(merged.at[s, 1, second], arrived.at[s, 0, second], to_quad[1]))
                elif k == 2:
                    sends[s, "2a"] = go(copy(merged.at[s, 2, first], arrived.at[s, 1, first], to_quad[2]))
            elif k:
                sends[s, k] = go(copy(merged.at[s, k], arrived.at[s, k - 1], to_quad[k]))
        if quads == 4:
            sends[s, "3a"].wait_recv()
            add_rows(mine.at[s, 1, first], merged.at[s, 1, first], relay.at[s, 0])
            sends[s, "1a"] = go(copy(mine.at[s, 1, first], arrived.at[s, 0, first], to_quad[1]))
            sends[s, "3b"].wait_recv()
            add_rows(mine.at[s, 2, second], merged.at[s, 2, second], relay.at[s, 1])
            sends[s, "2b"] = go(copy(mine.at[s, 2, second], arrived.at[s, 1, second], to_quad[2]))
    backs = {}
    for s in order:
        if quads == 4:
            for name in ("1b", "2a", "1a", "2b"):
                sends[s, name].wait_recv()
        else:
            for k in range(1, quads):
                sends[s, k].wait_recv()
        parts = [merged.at[s, 0]] + [arrived.at[s, i] for i in range(arrived.shape[1])]
        if s >= count:
            add_rows(summed.at[s - count], *parts)
            backs[s] = go(copy(summed.at[s - count], back.at[s - count], across))
        else:
            if partner:
                backs[s + count].wait_recv()
                parts.append(back.at[s])
            add_rows(out_ref.at[s], *parts)
    for c in finish:
        c.wait_send()


def scatter_rows(own, other, partner, name, cid):
    quads, total, rows, width = own.shape
    count = total // 2 if partner else total
    sems = scatter_sems(quads, total, partner)
    incoming = 2 if quads == 4 else quads - 1
    def buf(*lead):
        return pltpu.VMEM(lead + (rows, width), BF)
    scratch = [buf(total, quads), buf(total, quads), buf(total, quads),
               pltpu.VMEM((total, 2, rows // 2, width), BF), buf(total, incoming)]
    if partner:
        scratch += [buf(count), buf(count)]
    return pl.pallas_call(
        functools.partial(scatter_body, quads, count, partner),
        out_shape=jax.ShapeDtypeStruct((count, rows, width), F32),
        in_specs=[pl.BlockSpec(memory_space=pl.ANY)] * 2,
        out_specs=pl.BlockSpec(memory_space=pltpu.VMEM),
        scratch_shapes=scratch + [
            pltpu.SemaphoreType.DMA((total * quads,)),
            pltpu.SemaphoreType.DMA((sems,)),
            pltpu.SemaphoreType.DMA((sems,)),
        ],
        compiler_params=pltpu.CompilerParams(collective_id=cid, has_side_effects=True, vmem_limit_bytes=60 << 20),
        name=name,
    )(own, other)


def scatter_all(own, other, partner, name, number):
    if own.shape[0] == 4:
        return scatter_rows(own, other, partner, name, number)
    count = own.shape[1] // 2 if partner else own.shape[1]
    return jnp.concatenate(
        [
            scatter_rows(own[:, m::count], other[:, m::count], partner, name, number)
            for m in range(count)
        ]
    )


def on_device(
    tokens,
    cotangent,
    routes,
    lengths,
    block_order,
    w_query,
    w_key,
    w_value,
    w_out,
    w_router,
    w_gate,
    w_up,
    w_down,
    attn_gain,
    mlp_gain,
    query_gain,
    key_gain,
):
    batches, _, rows, width = tokens.shape
    dp_size = lax.axis_size(DP)
    ctx_size = lax.axis_size(CTX)
    quads = lax.axis_size("quad")
    lanes = lax.axis_size("lane")
    slot_len = rows * ctx_size
    block_rows = rows // 2
    head_width = width // ctx_size
    heads = head_width // HEAD
    shard = w_query.shape[0]
    expert_count = w_router.shape[1]
    local_experts = w_gate.shape[0]
    hidden_units = w_gate.shape[2]
    hidden_half = hidden_units // 2
    depth_part = w_gate.shape[1]
    factor = 1.0 / math.sqrt(HEAD)
    pair = lax.axis_index("pair")

    small = jnp.concatenate(
        [attn_gain, mlp_gain, query_gain, key_gain, w_router.reshape(shard * expert_count)]
    )
    small = spread(spread(small, CTX), DP).reshape(dp_size * ctx_size, -1)
    gain_attn = small[:, :shard].reshape(width).astype(F32)
    gain_mlp = small[:, shard : 2 * shard].reshape(width).astype(F32)
    gain_query = small[:, 2 * shard : 3 * shard].reshape(ctx_size, head_width)
    gain_key = small[:, 3 * shard : 4 * shard].reshape(ctx_size, head_width)
    router_w = small[:, 4 * shard :].reshape(width, expert_count)
    here = lax.axis_index(CTX)
    gain_query = lax.dynamic_index_in_dim(gain_query, here, 0, keepdims=False).astype(F32)
    gain_key = lax.dynamic_index_in_dim(gain_key, here, 0, keepdims=False).astype(F32)

    qkv = jnp.stack([w_query, w_key, w_value], axis=1).reshape(shard, 3, ctx_size, head_width)
    qkv = exchange(
        qkv.transpose(2, 0, 1, 3).reshape(ctx_size, shard, 3 * head_width), CTX
    ).reshape(ctx_size * shard, 3 * head_width)
    qkv_w = lax.all_gather(qkv, DP, axis=0, tiled=True)
    out_w = lax.all_gather(w_out, ALL, axis=0, tiled=True)

    def gather_depth(weights):
        halves = jnp.stack([weights[:, :, :hidden_half], weights[:, :, hidden_half:]])
        blocks = exchange(jnp.repeat(halves, lanes, axis=0), DP)
        return blocks.swapaxes(0, 1).reshape(local_experts, width, hidden_half)

    gate_w = gather_depth(w_gate)
    up_w = gather_depth(w_up)
    down_w = gather_lane(w_down).swapaxes(0, 1).reshape(local_experts, hidden_half, width)

    def places_of(device):
        stored = device * rows + jnp.arange(rows, dtype=jnp.int32)
        match_marks = (stored // block_rows)[:, None] == jnp.arange(
            block_order.shape[0], dtype=jnp.int32
        )[None, :]
        first_place = jnp.sum(jnp.where(match_marks, block_order[None, :], 0), axis=1)
        return first_place * block_rows + stored % block_rows

    places = jnp.concatenate(
        [
            places_of((lax.axis_index("quad") ^ k) * 2 + (pair ^ other))
            for other in range(2)
            for k in range(quads)
        ]
    )
    cosine, sine = angles(places, HEAD)
    expert_range = jnp.arange(expert_count, dtype=jnp.int32)

    inputs = tokens[:, 0].astype(F32)
    attn_root = inv_rms(inputs)
    act = gather_rows((inputs * attn_root * gain_attn).astype(BF), False, "gather_act", 0)
    grad_low = cotangent[:, 0]
    g_rows = gather_rows(grad_low, True, "gather_cotangent", 1)
    pre = [
        dot("td,de->te", part.reshape(-1, width), qkv_w).reshape(quads, batches, rows, -1)
        for part in act
    ]
    pre = jnp.stack(pre)

    saved = []
    attended_all = []
    for m in range(batches):
        pre_m = pre[:, :, m].reshape(slot_len, 3 * head_width)
        query_pre = pre_m[:, :head_width]
        key_pre = pre_m[:, head_width : 2 * head_width]
        value = pre_m[:, 2 * head_width :].astype(BF).reshape(slot_len, heads, HEAD)
        squares = jnp.stack(
            [jnp.sum(query_pre * query_pre, axis=1), jnp.sum(key_pre * key_pre, axis=1)]
        ).reshape(2, 2, quads, rows)
        squares = sum_ctx(squares).reshape(2, slot_len, 1)
        query_root = lax.rsqrt(squares[0] / width + EPSILON)
        key_root = lax.rsqrt(squares[1] / width + EPSILON)
        query = rotate(
            (query_pre * query_root * gain_query).reshape(slot_len, heads, HEAD), cosine, sine
        ).astype(BF)
        key = rotate(
            (key_pre * key_root * gain_key).reshape(slot_len, heads, HEAD), cosine, sine
        ).astype(BF)
        allowed = (places[None, :] <= places[:, None]) & (places[None, :] < lengths[m, 0])
        scores = dot("qhd,khd->hqk", query, key) * factor
        scores = jnp.where(allowed[None], scores, MASKED)
        expo = jnp.exp(scores - jnp.max(scores, axis=-1, keepdims=True))
        probs = expo / jnp.sum(expo, axis=-1, keepdims=True)
        probs_low = probs.astype(BF)
        attended = dot("hqk,khd->qhd", probs_low, value).astype(BF)
        attended_all.append(attended.reshape(2, quads, rows, head_width))
        saved.append(
            dict(
                query_pre=query_pre, key_pre=key_pre, query_root=query_root, key_root=key_root,
                query=query, key=key, value=value, probs=probs, probs_low=probs_low,
            )
        )
    attended = exchange(from_relative(jnp.stack(attended_all, axis=2)), CTX)
    attended = attended.transpose(1, 2, 0, 3).reshape(batches, rows, width)
    x_mid = inputs + dot("mtd,de->mte", attended, out_w)
    mlp_root = inv_rms(x_mid)
    mixed_in = (x_mid * mlp_root * gain_mlp).astype(BF)
    router = jax.nn.softmax(dot("mtd,de->mte", mixed_in, router_w), axis=-1)
    routed = jnp.any(routes[:, 0, :, :, None] == expert_range, axis=2).astype(F32)
    gates = (router * routed).transpose(2, 0, 1).reshape(ctx_size, local_experts, batches, rows)
    gates = to_relative(exchange(gates, CTX))
    gates = jnp.concatenate([gates, swap(gates, "half")], axis=3)
    gates = gates.transpose(0, 1, 3, 4, 2).reshape(2, -1, local_experts, 1)
    x_rows = gather_rows(mixed_in, True, "gather_mixed", 2)
    x_rows = [part.reshape(-1, width) for part in x_rows]
    g_rows = [part.reshape(-1, width) for part in g_rows]

    moe_list, d_list, d_gates_list, hid_list, dgate_list, dup_list = [], [], [], [], [], []
    shards = (quads, 2 * batches, rows)
    for x_part, g_part, gate in zip(x_rows, g_rows, (gates[0], gates[1])):
        gate_pre = dot("td,edf->tef", x_part, gate_w)
        up_pre = dot("td,edf->tef", x_part, up_w)
        d_hidden = dot("td,efd->tef", g_part, down_w)
        sigma = jax.nn.sigmoid(gate_pre)
        hidden = gate_pre * sigma * up_pre
        d_gates_list.append(jnp.sum(hidden * d_hidden, axis=2).reshape(shards + (local_experts,)))
        scaled = (hidden * gate).astype(BF)
        d_hidden = d_hidden * gate
        d_gate_pre = (d_hidden * up_pre * sigma * (1.0 + gate_pre * (1.0 - sigma))).astype(BF)
        d_up_pre = (d_hidden * gate_pre * sigma).astype(BF)
        moe_list.append(dot("tef,efd->td", scaled, down_w).astype(BF).reshape(shards + (width,)))
        d_part = dot("tef,edf->td", d_gate_pre, gate_w)
        d_part = (d_part + dot("tef,edf->td", d_up_pre, up_w)).astype(BF)
        d_list.append(d_part.reshape(shards + (width,)))
        hid_list.append(scaled)
        dgate_list.append(d_gate_pre)
        dup_list.append(d_up_pre)
    d_mixed = scatter_all(d_list[0], d_list[1], True, "scatter_mixed", 3)
    d_gates = jnp.stack(d_gates_list).transpose(0, 1, 4, 2, 3)
    d_gates = d_gates[:, :, :, :batches] + swap(d_gates[:, :, :, batches:], "half")
    d_router = exchange(from_relative(d_gates), CTX).reshape(expert_count, batches, rows)
    d_router = d_router.transpose(1, 2, 0) * routed
    d_logits = (
        router * (d_router - jnp.sum(router * d_router, axis=-1, keepdims=True))
    ).astype(BF)
    d_mixed = d_mixed + dot("mte,de->mtd", d_logits, router_w)

    def norm_back_all(values, root, gain, grad):
        d_values, d_gain = norm_back(values, root, gain, grad)
        return d_values, jnp.sum(d_gain, axis=0)

    d_mid, part_mlp_gain = norm_back_all(x_mid, mlp_root, gain_mlp, d_mixed)
    d_mid = d_mid + grad_low.astype(F32)
    d_att_out = d_mid.astype(BF)
    d_attended = dot("mte,de->mtd", d_att_out, out_w).astype(BF)
    d_attended = d_attended.reshape(batches, rows, ctx_size, head_width).transpose(2, 0, 1, 3)
    d_attended = to_relative(exchange(d_attended, CTX))
    part_query_gain = part_key_gain = 0.0
    d_pre_all = []
    for m in range(batches):
        s = saved[m]
        d_att = d_attended[:, :, m].reshape(slot_len, heads, HEAD)
        probs, query, key = s["probs"], s["query"], s["key"]
        d_probs = dot("qhd,khd->hqk", d_att, s["value"])
        inner = jnp.sum(probs * d_probs, axis=-1, keepdims=True)
        d_scores = (probs * (d_probs - inner)).astype(BF)
        d_query = dot("hqk,khd->qhd", d_scores, key) * factor
        d_key = dot("hqk,qhd->khd", d_scores, query) * factor
        d_value = dot("hqk,qhd->khd", s["probs_low"], d_att)
        d_query = rotate_back(d_query, cosine, sine).reshape(slot_len, head_width)
        d_key = rotate_back(d_key, cosine, sine).reshape(slot_len, head_width)
        query_pre, key_pre = s["query_pre"], s["key_pre"]
        query_root, key_root = s["query_root"], s["key_root"]
        inners = jnp.stack(
            [
                jnp.sum(d_query * gain_query * query_pre, axis=1),
                jnp.sum(d_key * gain_key * key_pre, axis=1),
            ]
        ).reshape(2, 2, quads, rows)
        inners = sum_ctx(inners).reshape(2, slot_len, 1) / width
        d_query_pre = query_root * (d_query * gain_query) - query_pre * query_root**3 * inners[0]
        d_key_pre = key_root * (d_key * gain_key) - key_pre * key_root**3 * inners[1]
        part_query_gain = part_query_gain + jnp.sum(d_query * query_pre * query_root, axis=0)
        part_key_gain = part_key_gain + jnp.sum(d_key * key_pre * key_root, axis=0)
        d_pre = jnp.concatenate(
            [
                d_query_pre.astype(BF),
                d_key_pre.astype(BF),
                d_value.reshape(slot_len, head_width).astype(BF),
            ],
            axis=1,
        )
        d_pre_all.append(d_pre.reshape(2, quads, rows, 3 * head_width))
    d_pre = jnp.stack(d_pre_all, axis=2).reshape(2, -1, 3 * head_width)
    d_act = [
        dot("te,de->td", d_pre[i], qkv_w).astype(BF).reshape(quads, batches, rows, width)
        for i in range(2)
    ]
    d_act = scatter_all(d_act[0], d_act[1], False, "scatter_act", 4)
    d_inputs, part_attn_gain = norm_back_all(inputs, attn_root, gain_attn, d_act)
    moe_sum = scatter_all(moe_list[0], moe_list[1], True, "scatter_moe", 5)
    mixed = (x_mid + moe_sum).astype(BF)

    def total(spec, left, right):
        return sum(dot(spec, x, y) for x, y in zip(left, right))

    grad_down = total("tef,td->efd", hid_list, g_rows)
    grad_down = grad_down.reshape(local_experts, lanes, -1, width).swapaxes(0, 1)
    grad_down = scatter_lane(grad_down)

    def scatter_depth(parts):
        grad = total("td,tef->edf", x_rows, parts).astype(BF)
        grad = grad.reshape(local_experts, dp_size, depth_part, hidden_half).swapaxes(0, 1)
        grad = exchange(grad, DP).astype(F32)
        grad = grad.reshape(2, lanes, local_experts, depth_part, hidden_half).sum(axis=1)
        return grad.transpose(1, 2, 0, 3).reshape(local_experts, depth_part, hidden_units)

    grad_gate = scatter_depth(dgate_list)
    grad_up = scatter_depth(dup_list)

    grad_out = dot("mtd,mte->de", attended, d_att_out).astype(BF)
    grad_out = lax.psum_scatter(grad_out, ALL, scatter_dimension=0, tiled=True).astype(F32)
    acts = [part.reshape(-1, width) for part in act]
    grad_qkv = total("td,te->de", acts, d_pre).astype(BF)
    grad_qkv = lax.psum_scatter(grad_qkv, DP, scatter_dimension=0, tiled=True)
    grad_qkv = exchange(grad_qkv.reshape(ctx_size, shard, 3 * head_width), CTX).astype(F32)
    grad_qkv = grad_qkv.reshape(ctx_size, shard, 3, head_width).transpose(2, 1, 0, 3)
    grad_qkv = grad_qkv.reshape(3, shard, width)

    grad_router = dot("mtd,mte->de", mixed_in, d_logits)
    columns = jnp.arange(ctx_size, dtype=jnp.int32)[:, None] == here

    def placed(part):
        return jnp.where(columns, part[None, :], 0.0).reshape(width)

    gains = jnp.stack(
        [part_attn_gain, part_mlp_gain, placed(part_query_gain), placed(part_key_gain)]
    )
    gains = gains.reshape(4, dp_size, ctx_size, shard).transpose(1, 2, 0, 3)
    packed = jnp.concatenate(
        [
            gains.reshape(dp_size, ctx_size, 4 * shard),
            grad_router.reshape(dp_size, ctx_size, shard * expert_count),
        ],
        axis=2,
    )
    packed = reduce_small(packed)
    return (
        mixed[:, None],
        (d_inputs + d_mid)[:, None],
        grad_qkv[0],
        grad_qkv[1],
        grad_qkv[2],
        grad_out,
        packed[4 * shard :].reshape(shard, expert_count),
        grad_gate,
        grad_up,
        grad_down,
        packed[:shard],
        packed[shard : 2 * shard],
        packed[2 * shard : 3 * shard],
        packed[3 * shard : 4 * shard],
    )


def solution(mesh):
    dp_size, ctx_size = mesh.shape["dp"], mesh.shape["ctx"]
    grid = Mesh(mesh.devices.reshape(2, dp_size // 2, ctx_size // 2, 2), ALL)
    rows = P(None, DP, CTX, None)
    dense = P(ALL, None)
    expert = P(CTX, DP, None)
    vector = P(ALL)
    return jax.shard_map(
        on_device,
        mesh=grid,
        in_specs=(rows, rows, rows, P(None, DP), P())
        + (dense,) * 5
        + (expert,) * 3
        + (vector,) * 4,
        out_specs=(rows, rows) + (dense,) * 5 + (expert,) * 3 + (vector,) * 4,
        check_vma=False,
    )
```

```python
import functools
import math

import jax
import jax.numpy as jnp
from jax import lax
from jax.experimental import pallas as pl
from jax.experimental.pallas import tpu as pltpu
from jax.sharding import Mesh
from jax.sharding import PartitionSpec as P

HEAD = 128
EPSILON = 1e-05
ROPE_BASE = 10000.0
MASKED = -1e30
BF = jnp.bfloat16
F32 = jnp.float32
DP = ("half", "lane")
CTX = ("quad", "pair")
ALL = DP + CTX
MESH = pl.DeviceIdType.MESH


def dot(spec, left, right):
    return jnp.einsum(spec, left, right, preferred_element_type=F32)


def inv_rms(values):
    return lax.rsqrt(jnp.mean(values * values, axis=-1, keepdims=True) + EPSILON)


def norm_back(values, inv_root, gain_vec, grad_in):
    weighted = grad_in * gain_vec
    inner = jnp.mean(weighted * values, axis=-1, keepdims=True)
    grad_values = inv_root * weighted - values * (inv_root * inv_root * inv_root) * inner
    return (grad_values, jnp.sum(grad_in * values * inv_root, axis=0))


def angles(places, head_width):
    index = jnp.arange(head_width // 2, dtype=F32)
    freqs = jnp.power(ROPE_BASE, -2.0 * index / head_width)
    turning = places.astype(F32)[:, None] * freqs[None, :]
    turning = jnp.concatenate([turning, turning], axis=1)
    return (jnp.cos(turning)[:, None, :], jnp.sin(turning)[:, None, :])


def rotate(values, cosine, sine):
    half_size = values.shape[-1] // 2
    turned = jnp.concatenate([-values[..., half_size:], values[..., :half_size]], axis=-1)
    return values * cosine + turned * sine


def rotate_back(grad_in, cosine, sine):
    half_size = grad_in.shape[-1] // 2
    moved = grad_in * sine
    return grad_in * cosine + jnp.concatenate(
        [moved[..., half_size:], -moved[..., :half_size]], axis=-1
    )


def swap(values, axis):
    return lax.ppermute(values, axis, [(0, 1), (1, 0)])


def exchange(blocks, axes):
    return lax.all_to_all(blocks, axes, split_axis=0, concat_axis=0, tiled=True)


def lane_parts(values):
    if lax.axis_size("lane") == 2:
        return swap(values, "lane")
    return lax.all_gather(values, "lane", axis=0, tiled=False)


def gather_lane(values, parts):
    if lax.axis_size("lane") == 2:
        first = lax.axis_index("lane") == 0
        return jnp.stack([jnp.where(first, values, parts), jnp.where(first, parts, values)])
    return parts


def reduce_small(values):
    return jnp.sum(exchange_rows(values, "all", "small_gradients", 15), axis=(0, 1))


def toggled(index, bits):
    step = 1
    while step <= bits:
        if bits & step:
            index = index + step - 2 * step * ((index // step) % 2)
        step *= 2
    return index


def greet(peers):
    barrier = pltpu.get_barrier_semaphore()
    for peer in peers:
        pl.semaphore_signal(barrier, inc=1, device_id=peer, device_id_type=MESH)
    pl.semaphore_wait(barrier, len(peers))


class Mover:
    def __init__(self, send, recv, local):
        self.send, self.recv, self.local = send, recv, local
        self.number, self.local_number = 0, 0
        self.sent, self.kept = [], []

    def copy(self, src, dst, device):
        i = self.number
        self.number += 1
        return pltpu.make_async_remote_copy(
            src_ref=src, dst_ref=dst, send_sem=self.send.at[i], recv_sem=self.recv.at[i],
            device_id=device, device_id_type=MESH,
        )

    def go(self, *copies):
        for c in copies:
            c.start()
            self.sent.append(c)

    def keep(self, src, dst):
        c = pltpu.make_async_copy(src, dst, self.local.at[self.local_number])
        self.local_number += 1
        c.start()
        self.kept.append(c)
        return c

    def finish(self):
        for c in self.sent:
            c.wait_send()
        for c in self.kept:
            c.wait()


class Spread:
    def __init__(self, mover, quads, src, slot):
        self.mover, self.quads = mover, quads
        quad = lax.axis_index("quad")
        to_quad = [{"quad": toggled(quad, k)} for k in range(quads)]
        sibling = {"pair": 1 - lax.axis_index("pair")}
        rows = src.shape[0]
        halves = (("a", pl.ds(0, rows // 2)), ("b", pl.ds(rows // 2, rows // 2)))
        p = {"o0": mover.copy(src, slot(1, 0, 0), sibling)}
        if quads == 4:
            for k in (1, 2):
                for name, part in halves:
                    p[f"s{k}{name}"] = mover.copy(
                        src.at[part], slot(0, k, 0).at[part], to_quad[k]
                    )
            for k, (name, part) in zip((1, 2), halves):
                p[f"f3{name}"] = mover.copy(
                    slot(0, k, k).at[part], slot(0, 3, k).at[part], to_quad[3 - k]
                )
            for k in (1, 2, 3):
                for name, part in halves:
                    p[f"o{k}{name}"] = mover.copy(
                        slot(0, k, k).at[part], slot(1, k, k).at[part], sibling
                    )
        else:
            for k in range(1, quads):
                p[f"s{k}"] = mover.copy(src, slot(0, k, 0), to_quad[k])
                p[f"o{k}"] = mover.copy(slot(0, k, k), slot(1, k, k), sibling)
        self.copies = p

    @staticmethod
    def count(quads):
        return 13 if quads == 4 else 2 * quads - 1

    def begin(self):
        names = [f"s{k}" for k in range(1, self.quads)]
        if self.quads == 4:
            names = ["s1a", "s2b", "s1b", "s2a"]
        self.mover.go(*[self.copies[name] for name in names + ["o0"]])

    def forward(self):
        p = self.copies
        steps = [(f"s{k}", (f"o{k}",)) for k in range(1, self.quads)]
        if self.quads == 4:
            steps = [
                ("s1a", ("f3a", "o1a")), ("s2b", ("f3b", "o2b")), ("s1b", ("o1b",)),
                ("s2a", ("o2a",)), ("f3a", ("o3a",)), ("f3b", ("o3b",)),
            ]
        for name, then in steps:
            p[name].wait_recv()
            self.mover.go(*[p[t] for t in then])

    def arrive(self):
        for name, c in self.copies.items():
            if name[0] == "o":
                c.wait_recv()


def relative_slots(own_ref, other_ref, s):
    return lambda core, kr, km: (other_ref if core else own_ref).at[kr, s]


def ctx_peers(quads):
    return [ctx_at(quads, n)[0] for n in range(1, 2 * quads)]


def planes_of(lanes):
    half, lane = lax.axis_index("half"), lax.axis_index("lane")
    result = []
    for n in range(1, 2 * lanes):
        h, l = toggled(half, n // lanes), toggled(lane, n % lanes)
        result.append(({"half": h, "lane": l}, h * lanes + l))
    return half * lanes + lane, result


def gather_body(quads, lanes, partners, *refs):
    inputs = refs[: len(partners)]
    blocks_ref = refs[len(partners)]
    refs = refs[len(partners) + 1 :]
    outputs = [(refs[2 * i], refs[2 * i + 1]) for i in range(len(partners))]
    blocks_out, held = refs[2 * len(partners) : 2 * len(partners) + 2]
    refs = refs[2 * len(partners) + 2 :]
    keeps = {}
    for i, partner in enumerate(partners):
        if partner:
            keeps[i], refs = refs[0], refs[1:]
    local, send, recv = refs
    mover = Mover(send, recv, local)
    across = {"half": 1 - lax.axis_index("half")}
    quad = lax.axis_index("quad")
    peers = [{"quad": toggled(quad, k)} for k in range(1, quads)]
    peers.append({"pair": 1 - lax.axis_index("pair")})
    me, planes = planes_of(lanes)
    greet(peers + [device for device, _ in planes])

    def add(sources, i, offset):
        plans = []
        for s, src in enumerate(sources):
            p = Spread(mover, quads, src, relative_slots(*outputs[i], offset + s))
            p.begin()
            plans.append(p)
            mover.keep(src, outputs[i][0].at[0, offset + s])
        return plans

    crossing = {}
    for i, keep in keeps.items():
        crossing[i] = [
            mover.copy(inputs[i].at[s], keep.at[s], across) for s in range(inputs[i].shape[0])
        ]
        mover.go(*crossing[i])
    plans = []
    for i, ref in enumerate(inputs):
        plans += add([ref.at[s] for s in range(ref.shape[0])], i, 0)
    blocks = [
        mover.copy(blocks_ref.at[place // lanes], blocks_out.at[me], device)
        for device, place in planes
    ]
    mover.go(*blocks)
    into = mover.keep(blocks_ref.at[me // lanes], held)
    plans[0].forward()
    into.wait()
    mover.kept = [c for c in mover.kept if c is not into]
    mover.keep(held, blocks_out.at[me])
    for p in plans[1:]:
        p.forward()
    late = []
    for i, keep in keeps.items():
        for c in crossing[i]:
            c.wait_recv()
        late += add([keep.at[s] for s in range(keep.shape[0])], i, keep.shape[0])
    for p in late:
        p.forward()
    for p in plans + late:
        p.arrive()
    for c in blocks:
        c.wait_recv()
    mover.finish()


def gather_rows(sources, partners, blocks, name, number):
    quads, lanes = lax.axis_size("quad"), lax.axis_size("lane")
    shapes, keeps = [], []
    sems = total = 0
    for x, partner in zip(sources, partners):
        count = x.shape[0] * (2 if partner else 1)
        total += count
        sems += count * Spread.count(quads) + (x.shape[0] if partner else 0)
        shapes += [jax.ShapeDtypeStruct((quads, count) + x.shape[1:], x.dtype)] * 2
        if partner:
            keeps.append(pltpu.VMEM(x.shape, x.dtype))
    shapes.append(jax.ShapeDtypeStruct((2 * lanes,) + blocks.shape[1:], blocks.dtype))
    sems += 2 * lanes - 1
    out = pl.pallas_call(
        functools.partial(gather_body, quads, lanes, partners),
        out_shape=shapes,
        in_specs=[pl.BlockSpec(memory_space=pltpu.VMEM)] * len(sources)
        + [pl.BlockSpec(memory_space=pl.ANY)],
        out_specs=[pl.BlockSpec(memory_space=pl.ANY)] * len(shapes),
        scratch_shapes=[pltpu.VMEM(blocks.shape[1:], blocks.dtype)]
        + keeps
        + [
            pltpu.SemaphoreType.DMA((total + 2,)),
            pltpu.SemaphoreType.DMA((sems,)),
            pltpu.SemaphoreType.DMA((sems,)),
        ],
        compiler_params=pltpu.CompilerParams(collective_id=number, has_side_effects=True),
        name=name,
    )(*sources, blocks)
    return [(out[2 * i], out[2 * i + 1]) for i in range(len(sources))], out[-1]


def start_body(
    quads, lanes, tok_ref, qkv_ref, small_ref, wout_ref,
    tok_own, tok_other, qkv_out, small_out, wout_out, local, send, recv,
):
    mover = Mover(send, recv, local)
    half, lane = lax.axis_index("half"), lax.axis_index("lane")
    plane, here = half * lanes + lane, ctx_place()
    partner = (1 - half) * lanes + lane
    across = {"half": 1 - half}
    devices = 4 * lanes * quads
    others = [all_at(lanes, quads, n)[0] for n in range(1, devices)]
    greet(others)
    mine = mover.keep(small_ref, small_out.at[plane * 2 * quads + here])
    shared = [mover.copy(small_ref, small_out.at[plane * 2 * quads + here], d) for d in others]
    mover.go(*shared)

    def planes(src, view):
        first = mover.copy(src, view(plane), across)
        rest = [
            mover.copy(src, view(plane), {"lane": toggled(lane, d)}) for d in range(1, lanes)
        ]
        then = [
            mover.copy(view(partner), view(partner), {"lane": toggled(lane, d)})
            for d in range(1, lanes)
        ]
        mover.go(first, *rest)
        return first, rest, then

    mover.keep(wout_ref, wout_out.at[plane, here])
    w_first, w_rest, w_then = planes(wout_ref, lambda p: wout_out.at[p, here])
    kept = mover.keep(qkv_ref.at[here], qkv_out.at[plane, here])
    columns = []
    for n in range(1, 2 * quads):
        device, place = ctx_at(quads, n)
        columns.append(mover.copy(qkv_ref.at[place], qkv_out.at[plane, here], device))
    mover.go(*columns)
    tokens = []
    for s in range(tok_ref.shape[0]):
        p = Spread(mover, quads, tok_ref.at[s], relative_slots(tok_own, tok_other, s))
        p.begin()
        tokens.append(p)
        mover.keep(tok_ref.at[s], tok_own.at[0, s])
    for c in columns:
        c.wait_recv()
    kept.wait()
    mover.kept = [c for c in mover.kept if c is not kept]
    q_first, q_rest, q_then = planes(qkv_out.at[plane], lambda p: qkv_out.at[p])
    w_first.wait_recv()
    mover.go(*w_then)

    def wout_slots(p):
        pair = lax.axis_index("pair")
        quad = lax.axis_index("quad")
        return lambda core, kr, km: wout_out.at[p, toggled(quad, km) * 2 + pair]

    weights = [Spread(mover, quads, wout_ref, wout_slots(plane))]
    weights[0].begin()
    tokens[0].forward()
    for c in w_rest:
        c.wait_recv()
    for c in w_then:
        c.wait_recv()
    for n in range(1, 2 * lanes):
        p = toggled(half, n // lanes) * lanes + toggled(lane, n % lanes)
        weights.append(Spread(mover, quads, wout_out.at[p, here], wout_slots(p)))
        weights[-1].begin()
    q_first.wait_recv()
    mover.go(*q_then)
    for p in tokens[1:] + weights:
        p.forward()
    for p in tokens + weights:
        p.arrive()
    for c in shared + q_rest + q_then:
        c.wait_recv()
    mover.finish()


def start_gather(tokens, qkv, small, w_out):
    quads, lanes = lax.axis_size("quad"), lax.axis_size("lane")
    count = tokens.shape[0]
    planes, devices = 2 * lanes, 4 * lanes * quads

    def like(lead, x, dtype=BF):
        return jax.ShapeDtypeStruct(lead + x.shape, dtype)

    sems = (devices - 1) + 2 * (2 * lanes - 1) + (2 * quads - 1)
    sems += Spread.count(quads) * (count + planes)
    return pl.pallas_call(
        functools.partial(start_body, quads, lanes),
        out_shape=[like((quads,), tokens)] * 2
        + [like((planes,), qkv), like((devices,), small)]
        + [like((planes, 2 * quads), w_out)],
        in_specs=[pl.BlockSpec(memory_space=pltpu.VMEM)] * 4,
        out_specs=[pl.BlockSpec(memory_space=pl.ANY)] * 5,
        scratch_shapes=[
            pltpu.SemaphoreType.DMA((3 + count,)),
            pltpu.SemaphoreType.DMA((sems,)),
            pltpu.SemaphoreType.DMA((sems,)),
        ],
        compiler_params=pltpu.CompilerParams(collective_id=0, has_side_effects=True),
        name="start_gather",
    )(tokens, qkv, small, w_out)


def add_rows(out_ref, *refs):
    rows = out_ref.shape[0]
    step = 16

    @pl.loop(0, rows // step)
    def _(i):
        part = pl.ds(pl.multiple_of(i * step, step), step)
        total = refs[0][part].astype(F32)
        for ref in refs[1:]:
            total = total + ref[part].astype(F32)
        out_ref[part] = total.astype(out_ref.dtype)


def scatter_body(quads, lanes, kinds, count, partner, extra, *refs):
    inputs = [(refs[2 * i], refs[2 * i + 1]) for i in range(kinds)]
    refs = refs[2 * kinds :]
    if extra:
        blocks_ref, down_ref, *refs = refs
    outputs, refs = refs[:kinds], refs[kinds:]
    if extra:
        blocks_out, down_out, held, *refs = refs
    mine, theirs, relay, arrived, *rest = refs
    if partner:
        summed, back, *rest = rest
    local, send, recv = rest
    mover = Mover(send, recv, local)
    mover.local_number = local.shape[0] - 2
    total, rows = inputs[0][0].shape[1:3]
    first, second = pl.ds(0, rows // 2), pl.ds(rows // 2, rows // 2)
    quad = lax.axis_index("quad")
    to_quad = [{"quad": toggled(quad, k)} for k in range(quads)]
    sibling = {"pair": 1 - lax.axis_index("pair")}
    across = {"half": 1 - lax.axis_index("half")}
    peers = to_quad[1:] + [sibling]
    if extra:
        me, planes = planes_of(lanes)
        peers += [device for device, _ in planes]
    elif partner:
        peers.append(across)
    greet(peers)

    def go(src, dst, device):
        c = mover.copy(src, dst, device)
        mover.go(c)
        return c

    order = [(i, s) for i in range(kinds) for s in range(count, total)]
    order += [(i, s) for i in range(kinds) for s in range(count)]
    ks = [3, 1, 2, 0] if quads == 4 else list(range(quads - 1, -1, -1))
    sib, loc = {}, {}
    for n, (i, s) in enumerate(order):
        for k in ks:
            sib[n, k] = go(inputs[i][1].at[k, s], theirs.at[n, k], sibling)
            loc[n, k] = pltpu.make_async_copy(
                inputs[i][0].at[k, s], mine.at[n, k], local.at[n * quads + k]
            )
            loc[n, k].start()
    sends = {}

    def merge(n):
        for k in ks:
            sib[n, k].wait_recv()
            loc[n, k].wait()
            add_rows(mine.at[n, k], mine.at[n, k], theirs.at[n, k])
            if quads == 4:
                if k == 3:
                    sends[n, "3a"] = go(mine.at[n, 3, first], relay.at[n, 0], to_quad[2])
                    sends[n, "3b"] = go(mine.at[n, 3, second], relay.at[n, 1], to_quad[1])
                elif k == 1:
                    sends[n, "1b"] = go(mine.at[n, 1, second], arrived.at[n, 0, second], to_quad[1])
                elif k == 2:
                    sends[n, "2a"] = go(mine.at[n, 2, first], arrived.at[n, 1, first], to_quad[2])
            elif k:
                sends[n, k] = go(mine.at[n, k], arrived.at[n, k - 1], to_quad[k])

    def pass_on(n):
        if quads == 4:
            sends[n, "3a"].wait_recv()
            add_rows(mine.at[n, 1, first], mine.at[n, 1, first], relay.at[n, 0])
            sends[n, "1a"] = go(mine.at[n, 1, first], arrived.at[n, 0, first], to_quad[1])
            sends[n, "3b"].wait_recv()
            add_rows(mine.at[n, 2, second], mine.at[n, 2, second], relay.at[n, 1])
            sends[n, "2b"] = go(mine.at[n, 2, second], arrived.at[n, 1, second], to_quad[2])

    backs = {}

    def total_of(n):
        i, s = order[n]
        for name in ("1b", "2a", "1a", "2b") if quads == 4 else range(1, quads):
            sends[n, name].wait_recv()
        parts = [mine.at[n, 0]] + [arrived.at[n, j] for j in range(arrived.shape[1])]
        if s >= count:
            slot = i * count + s - count
            add_rows(summed.at[slot], *parts)
            backs[slot] = go(summed.at[slot], back.at[slot], across)
        else:
            if partner:
                backs[i * count + s].wait_recv()
                parts.append(back.at[i * count + s])
            add_rows(outputs[i].at[s], *parts)

    ahead = 2
    exchanged = []

    def exchange_grads():
        lane = lax.axis_index("lane")
        part = down_ref.shape[1] // lanes
        for e in range(down_ref.shape[0]):
            for d in range(1, lanes):
                to = toggled(lane, d)
                src = down_ref.at[e, pl.ds(pl.multiple_of(to * part, part), part)]
                exchanged.append(go(src, down_out.at[d - 1, e], {"lane": to}))
        for device, place in planes:
            exchanged.append(go(blocks_ref.at[place], blocks_out.at[me], device))

    if extra:
        into = mover.keep(blocks_ref.at[me], held)
    for n in range(len(order) + 2 * ahead):
        if extra and n == kinds * count + 2 * ahead:
            exchange_grads()
            into.wait()
            mover.kept = [c for c in mover.kept if c is not into]
            mover.keep(held, blocks_out.at[me])
        if n < len(order):
            merge(n)
        if 0 <= n - 1 < len(order):
            pass_on(n - 1)
        if 0 <= n - 2 * ahead < len(order):
            total_of(n - 2 * ahead)
    for c in exchanged:
        c.wait_recv()
    mover.finish()


def scatter_rows(pairs, partner, name, number, extra=()):
    lanes = lax.axis_size("lane")
    quads, total, rows, width = pairs[0][0].shape
    count = total // 2 if partner else total
    kinds = len(pairs)
    shards = kinds * total
    incoming = 2 if quads == 4 else quads - 1
    sems = shards * (quads + (6 if quads == 4 else quads - 1)) + (kinds * count if partner else 0)

    def buf(*lead):
        return pltpu.VMEM(lead + (rows, width), BF)

    scratch = [buf(shards, quads), buf(shards, quads)]
    scratch += [pltpu.VMEM((shards, 2, rows // 2, width), BF), buf(shards, incoming)]
    if partner:
        scratch += [buf(kinds * count), buf(kinds * count)]
    shapes = [jax.ShapeDtypeStruct((count, rows, width), F32)] * kinds
    specs = [pl.BlockSpec(memory_space=pltpu.VMEM)] * kinds
    anywhere = pl.BlockSpec(memory_space=pl.ANY)
    if extra:
        blocks, down = extra
        n_exp, hidden = down.shape[:2]
        shapes = shapes + [
            jax.ShapeDtypeStruct(blocks.shape, BF),
            jax.ShapeDtypeStruct((lanes - 1, n_exp, hidden // lanes, width), BF),
        ]
        specs = specs + [anywhere] * 2
        scratch = [pltpu.VMEM(blocks.shape[1:], BF)] + scratch
        sems += 2 * lanes - 1 + n_exp * (lanes - 1)
    return pl.pallas_call(
        functools.partial(scatter_body, quads, lanes, kinds, count, partner, bool(extra)),
        out_shape=shapes,
        in_specs=[anywhere] * (2 * kinds + len(extra)),
        out_specs=specs,
        scratch_shapes=scratch
        + [
            pltpu.SemaphoreType.DMA((shards * quads + 2,)),
            pltpu.SemaphoreType.DMA((sems,)),
            pltpu.SemaphoreType.DMA((sems,)),
        ],
        compiler_params=pltpu.CompilerParams(
            collective_id=number, has_side_effects=True, vmem_limit_bytes=60 << 20
        ),
        name=name,
    )(*[ref for pair in pairs for ref in pair], *extra)


def ctx_place():
    return lax.axis_index("quad") * 2 + lax.axis_index("pair")


def ctx_at(quads, number):
    core, distance = number // quads, number % quads
    quad = toggled(lax.axis_index("quad"), distance)
    pair = toggled(lax.axis_index("pair"), core)
    return {"quad": quad, "pair": pair}, quad * 2 + pair


def all_at(lanes, quads, number):
    half = toggled(lax.axis_index("half"), number // (lanes * 2 * quads))
    lane = toggled(lax.axis_index("lane"), number // (2 * quads) % lanes)
    device, place = ctx_at(quads, number % (2 * quads))
    return {"half": half, "lane": lane, **device}, (half * lanes + lane) * 2 * quads + place


def exchange_body(mode, lanes, quads, halves, x_ref, out_ref, local, send, recv):
    copies = []
    peers = []
    if mode in ("shared", "all"):
        me = (lax.axis_index("half") * lanes + lax.axis_index("lane")) * 2 * quads + ctx_place()
        for n in range(2 * lanes * 2 * quads):
            device, place = all_at(lanes, quads, n)
            copies.append((x_ref if mode == "shared" else x_ref.at[place], out_ref.at[me], device))
    else:
        for h in range(halves):
            for n in range(2 * quads):
                device, place = ctx_at(quads, n)
                if halves == 2:
                    device = {"half": toggled(lax.axis_index("half"), h), **device}
                if mode == "inward":
                    pair = (x_ref.at[h, n], out_ref.at[h, ctx_place()])
                elif mode == "outward":
                    pair = (x_ref.at[place], out_ref.at[h, n])
                else:
                    pair = (x_ref.at[place], out_ref.at[ctx_place()])
                copies.append(pair + (device,))
    own = pltpu.make_async_copy(copies[0][0], copies[0][1], local)
    own.start()
    greet([device for _, _, device in copies[1:]])
    started = []
    for i, (src, dst, device) in enumerate(copies[1:]):
        c = pltpu.make_async_remote_copy(
            src_ref=src, dst_ref=dst, send_sem=send.at[i], recv_sem=recv.at[i],
            device_id=device, device_id_type=MESH,
        )
        c.start()
        started.append(c)
    own.wait()
    for c in started:
        c.wait_recv()
    for c in started:
        c.wait_send()


def exchange_rows(x, mode, name, number, halves=1):
    quads, lanes = lax.axis_size("quad"), lax.axis_size("lane")
    count = halves * 2 * quads - 1
    shape = x.shape
    if mode == "outward":
        shape = (halves, 2 * quads) + x.shape[1:]
    elif mode in ("shared", "all"):
        count = 4 * lanes * quads - 1
        if mode == "shared":
            shape = (count + 1,) + x.shape
    return pl.pallas_call(
        functools.partial(exchange_body, mode, lanes, quads, halves),
        out_shape=jax.ShapeDtypeStruct(shape, x.dtype),
        in_specs=[pl.BlockSpec(memory_space=pltpu.VMEM)],
        out_specs=pl.BlockSpec(memory_space=pltpu.VMEM),
        scratch_shapes=[
            pltpu.SemaphoreType.DMA,
            pltpu.SemaphoreType.DMA((count,)),
            pltpu.SemaphoreType.DMA((count,)),
        ],
        compiler_params=pltpu.CompilerParams(collective_id=number, has_side_effects=True),
        name=name,
    )(x)


def sum_body(quads, x_ref, out_ref, landed, send, recv):
    count = 2 * quads
    greet([ctx_at(quads, n)[0] for n in range(1, count)])
    started = []
    for n in range(1, count):
        c = pltpu.make_async_remote_copy(
            src_ref=x_ref, dst_ref=landed.at[n - 1], send_sem=send.at[n - 1],
            recv_sem=recv.at[n - 1], device_id=ctx_at(quads, n)[0], device_id_type=MESH,
        )
        c.start()
        started.append(c)
    for c in started:
        c.wait_recv()
    for j in range(count):
        total = x_ref[j]
        for n in range(1, count):
            total = total + landed[n - 1, j ^ n]
        out_ref[j] = total
    for c in started:
        c.wait_send()


def sum_ctx(x, name, number):
    quads = lax.axis_size("quad")
    count = 2 * quads - 1
    return pl.pallas_call(
        functools.partial(sum_body, quads),
        out_shape=jax.ShapeDtypeStruct(x.shape, x.dtype),
        in_specs=[pl.BlockSpec(memory_space=pltpu.VMEM)],
        out_specs=pl.BlockSpec(memory_space=pltpu.VMEM),
        scratch_shapes=[
            pltpu.VMEM((count,) + x.shape, x.dtype),
            pltpu.SemaphoreType.DMA((count,)),
            pltpu.SemaphoreType.DMA((count,)),
        ],
        compiler_params=pltpu.CompilerParams(collective_id=number, has_side_effects=True),
        name=name,
    )(x)


def nn(left, right):
    return lax.dot_general(left, right, (((1,), (0,)), ((), ())), preferred_element_type=F32)


def nt(left, right):
    return lax.dot_general(left, right, (((1,), (1,)), ((), ())), preferred_element_type=F32)


def tn(left, right):
    return lax.dot_general(left, right, (((0,), (0,)), ((), ())), preferred_element_type=F32)


def expert_body(quads, before, gate_ref, xo_ref, xt_ref, goo_ref, got_ref, gpo_ref, gpt_ref, both_ref,
                down_ref, *refs):
    sums = refs[:4] if before else None
    mo_ref, mt_ref, do_ref, dt_ref, dgate_ref, hid_ref, dg_ref, du_ref = refs[-8:]
    t = pl.program_id(0)
    core_other = t >= 2 * quads
    partner = t % 2 == 1
    hidden, width = down_ref.shape
    x = jnp.where(core_other, xt_ref[0], xo_ref[0]).reshape(-1, width)
    g_own = jnp.where(partner, gpo_ref[0], goo_ref[0])
    g_other = jnp.where(partner, gpt_ref[0], got_ref[0])
    g = jnp.where(core_other, g_other, g_own).reshape(-1, width)
    gate = gate_ref[0]
    wg = both_ref[:, 0].reshape(width, hidden)
    wu = both_ref[:, 1].reshape(width, hidden)
    wd = down_ref[...]
    gate_pre = nn(x, wg)
    up_pre = nn(x, wu)
    d_hidden = nt(g, wd)
    sigma = 1.0 / (1.0 + jnp.exp(-gate_pre))
    silu = gate_pre * sigma
    hid = silu * up_pre
    dgate_ref[0] = jnp.sum(hid * d_hidden, axis=1, keepdims=True)
    d_hidden = d_hidden * gate
    scaled = (hid * gate).astype(BF)
    d_gate_pre = (d_hidden * up_pre * (sigma + silu * (1.0 - sigma))).astype(BF)
    d_up_pre = (d_hidden * silu).astype(BF)
    hid_ref[0] = scaled
    dg_ref[0] = d_gate_pre
    du_ref[0] = d_up_pre
    moe = nn(scaled, wd).reshape(mo_ref.shape[1:])
    d_rows = (nt(d_gate_pre, wg) + nt(d_up_pre, wu)).reshape(mo_ref.shape[1:])
    if before:
        moe = moe + jnp.where(core_other, sums[1][0], sums[0][0]).astype(F32)
        d_rows = d_rows + jnp.where(core_other, sums[3][0], sums[2][0]).astype(F32)
    moe, d_rows = moe.astype(BF), d_rows.astype(BF)

    @pl.when(jnp.logical_not(core_other))
    def _():
        mo_ref[0] = moe
        do_ref[0] = d_rows

    @pl.when(core_other)
    def _():
        mt_ref[0] = moe
        dt_ref[0] = d_rows


def expert(gates, x_rows, g_rows, both, down, before, name):
    quads, shards, rows, width = x_rows[0].shape
    batches = shards // 2
    hidden = down.shape[0]
    tiles = 4 * quads
    tile = batches * rows

    def own(t):
        return (jnp.minimum(t, 2 * quads - 1) // 2, jnp.minimum(t, 2 * quads - 1) % 2, 0, 0)

    def other(t):
        u = jnp.maximum(t - 2 * quads, 0)
        return (u // 2, u % 2, 0, 0)

    def own_g(t):
        return (jnp.minimum(t // 2, quads - 1), 0, 0, 0)

    def other_g(t):
        return (jnp.maximum(t // 2 - quads, 0), 0, 0, 0)

    shard_block = (1, batches, rows, width)
    saved_spec = pl.BlockSpec((1, tile, hidden), lambda t: (t, 0, 0))
    saved = jax.ShapeDtypeStruct((tiles, tile, hidden), BF)
    rows_shape = jax.ShapeDtypeStruct(x_rows[0].shape, BF)
    fixed = dict(pipeline_mode=pl.Buffered(1))
    sums_specs = [
        pl.BlockSpec(shard_block, own), pl.BlockSpec(shard_block, other),
        pl.BlockSpec(shard_block, own), pl.BlockSpec(shard_block, other),
    ]
    return pl.pallas_call(
        functools.partial(expert_body, quads, bool(before)),
        out_shape=(rows_shape,) * 4
        + (jax.ShapeDtypeStruct((tiles, tile, 1), F32), saved, saved, saved),
        grid_spec=pl.GridSpec(
            grid=(tiles,),
            in_specs=[
                pl.BlockSpec((1, tile, 1), lambda t: (t, 0, 0)),
                pl.BlockSpec(shard_block, own),
                pl.BlockSpec(shard_block, other),
                pl.BlockSpec(shard_block, own_g), pl.BlockSpec(shard_block, other_g),
                pl.BlockSpec(shard_block, own_g), pl.BlockSpec(shard_block, other_g),
                pl.BlockSpec(both.shape, lambda t: (0, 0, 0, 0), **fixed),
                pl.BlockSpec(down.shape, lambda t: (0, 0), **fixed),
            ]
            + (sums_specs if before else []),
            out_specs=sums_specs
            + [pl.BlockSpec((1, tile, 1), lambda t: (t, 0, 0)), saved_spec, saved_spec, saved_spec],
        ),
        input_output_aliases={9 + i: i for i in range(4)} if before else {},
        compiler_params=pltpu.CompilerParams(
            dimension_semantics=("arbitrary",), vmem_limit_bytes=60 << 20
        ),
        name=name,
    )(gates, *x_rows, *g_rows, both, down, *before)


def grads_body(quads, xo_ref, xt_ref, goo_ref, got_ref, gpo_ref, gpt_ref, hid_ref, dg_ref, du_ref, both_ref, down_ref,
               gate_acc, up_acc, down_acc):
    t = pl.program_id(0)
    width = down_acc.shape[1]
    hidden = down_acc.shape[0]

    @pl.when(t == 0)
    def _():
        gate_acc[...] = jnp.zeros_like(gate_acc)
        up_acc[...] = jnp.zeros_like(up_acc)
        down_acc[...] = jnp.zeros_like(down_acc)

    x = jnp.where(t >= quads, xt_ref[0], xo_ref[0]).reshape(-1, width)
    g_own = jnp.where(t >= quads, got_ref[0], goo_ref[0]).reshape(-1, width)
    g_partner = jnp.where(t >= quads, gpt_ref[0], gpo_ref[0]).reshape(-1, width)
    g = jnp.concatenate([g_own, g_partner], axis=0)
    gate_acc[...] += tn(x, dg_ref[...].reshape(-1, hidden))
    up_acc[...] += tn(x, du_ref[...].reshape(-1, hidden))
    down_acc[...] += tn(hid_ref[...].reshape(-1, hidden), g)

    @pl.when(t == pl.num_programs(0) - 1)
    def _():
        part = both_ref.shape[0]
        both_ref[:, 0] = gate_acc[...].astype(BF).reshape(part, -1, hidden)
        both_ref[:, 1] = up_acc[...].astype(BF).reshape(part, -1, hidden)
        down_ref[...] = down_acc[...].astype(BF)


def expert_grads(x_rows, g_rows, hid, dg, du, dp, name):
    quads, shards, rows, width = x_rows[0].shape
    batches = shards // 2
    tiles, tile, hidden = hid.shape

    saved = pl.BlockSpec((2, tile, hidden), lambda t: (t, 0, 0))

    def own(t):
        return (jnp.minimum(t, quads - 1), 0, 0, 0)

    def other(t):
        return (jnp.maximum(t - quads, 0), 0, 0, 0)

    g_block = (1, batches, rows, width)
    return pl.pallas_call(
        functools.partial(grads_body, quads),
        out_shape=(
            jax.ShapeDtypeStruct((dp, 2, width // dp, hidden), BF),
            jax.ShapeDtypeStruct((hidden, width), BF),
        ),
        grid_spec=pl.GridSpec(
            grid=(tiles // 2,),
            in_specs=[
                pl.BlockSpec((1, shards, rows, width), own),
                pl.BlockSpec((1, shards, rows, width), other),
                pl.BlockSpec(g_block, own), pl.BlockSpec(g_block, other),
                pl.BlockSpec(g_block, own), pl.BlockSpec(g_block, other),
                saved, saved, saved,
            ],
            out_specs=[
                pl.BlockSpec((dp, 2, width // dp, hidden), lambda t: (0, 0, 0, 0)),
                pl.BlockSpec((hidden, width), lambda t: (0, 0)),
            ],
            scratch_shapes=[pltpu.VMEM((width, hidden), F32), pltpu.VMEM((width, hidden), F32),
                            pltpu.VMEM((hidden, width), F32)],
        ),
        compiler_params=pltpu.CompilerParams(
            dimension_semantics=("arbitrary",), vmem_limit_bytes=60 << 20
        ),
        name=name,
    )(*x_rows, *g_rows, hid, dg, du)


def scatter_all(pairs, partner, name, number, extra=()):
    if pairs[0][0].shape[0] == 4:
        return scatter_rows(pairs, partner, name, number, extra)
    total = pairs[0][0].shape[1]
    count = total // 2 if partner else total
    sums = [
        jnp.concatenate(
            [
                scatter_rows([(own[:, m::count], other[:, m::count])], partner, name, number)[0]
                for m in range(count)
            ]
        )
        for own, other in pairs
    ]
    if not extra:
        return sums
    blocks, down = extra
    lanes, lane = lax.axis_size("lane"), lax.axis_index("lane")
    down = down.reshape(down.shape[0], lanes, -1, down.shape[2]).swapaxes(0, 1)
    moved = [
        lax.ppermute(
            lax.dynamic_index_in_dim(down, lane ^ d, 0, keepdims=False),
            "lane", [(i, i ^ d) for i in range(lanes)],
        )
        for d in range(1, lanes)
    ]
    return sums + [exchange(blocks, DP), jnp.stack(moved)]


def on_device(
    tokens,
    cotangent,
    routes,
    lengths,
    block_order,
    w_query,
    w_key,
    w_value,
    w_out,
    w_router,
    w_gate,
    w_up,
    w_down,
    attn_gain,
    mlp_gain,
    query_gain,
    key_gain,
):
    batches, _, rows, width = tokens.shape
    dp_size = lax.axis_size(DP)
    ctx_size = lax.axis_size(CTX)
    quads = lax.axis_size("quad")
    lanes = lax.axis_size("lane")
    slot_len = rows * ctx_size
    block_rows = rows // 2
    head_width = width // ctx_size
    heads = head_width // HEAD
    shard = w_query.shape[0]
    expert_count = w_router.shape[1]
    local_experts = w_gate.shape[0]
    hidden_units = w_gate.shape[2]
    hidden_half = hidden_units // 2
    depth_part = w_gate.shape[1]
    factor = 1.0 / math.sqrt(HEAD)
    pair = lax.axis_index("pair")

    qkv = jnp.stack([w_query, w_key, w_value], axis=1).reshape(shard, 3, ctx_size, head_width)
    qkv = qkv.transpose(2, 0, 1, 3).reshape(ctx_size, shard, 3 * head_width)
    small = jnp.concatenate(
        [attn_gain, mlp_gain, query_gain, key_gain, w_router.reshape(shard * expert_count)]
    )
    grad_low = cotangent[:, 0]
    tok_own, tok_other, qkv_w, small, out_w = start_gather(
        tokens[:, 0], qkv, small.reshape(1, -1), w_out
    )
    token_rows = (tok_own, tok_other)
    qkv_w = qkv_w.reshape(width, 3 * head_width)
    out_w = out_w.reshape(width, width)
    small = small.reshape(dp_size * ctx_size, -1)
    gain_attn = small[:, :shard].reshape(width).astype(F32)
    gain_mlp = small[:, shard : 2 * shard].reshape(width).astype(F32)
    gain_query = small[:, 2 * shard : 3 * shard].reshape(ctx_size, head_width)
    gain_key = small[:, 3 * shard : 4 * shard].reshape(ctx_size, head_width)
    router_w = small[:, 4 * shard :].reshape(width, expert_count)
    here = lax.axis_index(CTX)
    gain_query = lax.dynamic_index_in_dim(gain_query, here, 0, keepdims=False).astype(F32)
    gain_key = lax.dynamic_index_in_dim(gain_key, here, 0, keepdims=False).astype(F32)

    w_gate, w_up, w_down, crossing, qkv_w = lax.optimization_barrier(
        (w_gate, w_up, w_down, grad_low, qkv_w)
    )
    halves = [
        jnp.stack(
            [
                jnp.stack([w_gate[e, :, part], w_up[e, :, part]])
                for part in (slice(0, hidden_half), slice(hidden_half, hidden_units))
            ]
        )
        for e in range(local_experts)
    ]
    both_w = [exchange(jnp.repeat(part, lanes, axis=0), DP) for part in halves[:-1]]
    down_parts = lane_parts(w_down)
    cot_cross = swap(crossing, "half")

    def places_of(device):
        stored = device * rows + jnp.arange(rows, dtype=jnp.int32)
        match_marks = (stored // block_rows)[:, None] == jnp.arange(
            block_order.shape[0], dtype=jnp.int32
        )[None, :]
        first_place = jnp.sum(jnp.where(match_marks, block_order[None, :], 0), axis=1)
        return first_place * block_rows + stored % block_rows

    places = jnp.concatenate(
        [
            places_of((lax.axis_index("quad") ^ k) * 2 + (pair ^ other))
            for other in range(2)
            for k in range(quads)
        ]
    )
    cosine, sine = angles(places, HEAD)
    expert_range = jnp.arange(expert_count, dtype=jnp.int32)

    inputs = tokens[:, 0].astype(F32)
    attn_root = inv_rms(inputs)
    act = []
    for part in token_rows:
        values = part.astype(F32)
        act.append((values * inv_rms(values) * gain_attn).astype(BF))
    pre = [
        dot("td,de->te", part.reshape(-1, width), qkv_w).reshape(quads, batches, rows, -1)
        for part in act
    ]
    pre = jnp.stack(pre)

    squares = jnp.stack(
        [
            jnp.sum(part * part, axis=-1)
            for part in (pre[..., :head_width], pre[..., head_width : 2 * head_width])
        ],
        axis=2,
    )
    squares = sum_ctx(squares.reshape(2 * quads, 2 * batches, rows), "sum_squares", 6)
    roots = lax.rsqrt(squares.reshape(2 * quads, 2, batches, rows) / width + EPSILON)

    saved = []
    attended_all = []
    for m in range(batches):
        pre_m = pre[:, :, m].reshape(slot_len, 3 * head_width)
        query_pre = pre_m[:, :head_width]
        key_pre = pre_m[:, head_width : 2 * head_width]
        value = pre_m[:, 2 * head_width :].astype(BF).reshape(slot_len, heads, HEAD)
        query_root = roots[:, 0, m].reshape(slot_len, 1)
        key_root = roots[:, 1, m].reshape(slot_len, 1)
        query = rotate(
            (query_pre * query_root * gain_query).reshape(slot_len, heads, HEAD), cosine, sine
        ).astype(BF)
        key = rotate(
            (key_pre * key_root * gain_key).reshape(slot_len, heads, HEAD), cosine, sine
        ).astype(BF)
        allowed = (places[None, :] <= places[:, None]) & (places[None, :] < lengths[m, 0])
        scores = dot("qhd,khd->hqk", query, key) * factor
        scores = jnp.where(allowed[None], scores, MASKED)
        expo = jnp.exp(scores - jnp.max(scores, axis=-1, keepdims=True))
        probs = expo / jnp.sum(expo, axis=-1, keepdims=True)
        probs_low = probs.astype(BF)
        attended = dot("hqk,khd->qhd", probs_low, value).astype(BF)
        attended_all.append(attended.reshape(2 * quads, rows, head_width))
        saved.append(
            dict(
                query_pre=query_pre, key_pre=key_pre, query_root=query_root, key_root=key_root,
                query=query, key=key, value=value, probs=probs, probs_low=probs_low,
            )
        )
    attended = jnp.stack(attended_all, axis=1)[None]
    attended = exchange_rows(attended, "inward", "attended_to_rows", 7)[0]
    attended = attended.transpose(1, 2, 0, 3).reshape(batches, rows, width)
    x_mid = inputs + dot("mtd,de->mte", attended, out_w)
    mlp_root = inv_rms(x_mid)
    mixed_in = (x_mid * mlp_root * gain_mlp).astype(BF)
    router = jax.nn.softmax(dot("mtd,de->mte", mixed_in, router_w), axis=-1)
    routed = jnp.any(routes[:, 0, :, :, None] == expert_range, axis=2).astype(F32)
    gates = (router * routed).transpose(2, 0, 1).reshape(ctx_size, local_experts, batches, rows)
    gates = exchange_rows(gates, "outward", "gates_to_experts", 8, 2)
    gates = gates.transpose(1, 0, 3, 4, 2).reshape(4 * quads, batches * rows, local_experts)
    (x_rows, cot_rows, cross_rows), last_w = gather_rows(
        [mixed_in, grad_low, cot_cross], (True, False, False), halves[-1], "gather_mixed", 2
    )
    both_w = both_w + [last_w]
    g_rows = cot_rows + cross_rows
    x_rows, both_w, down_parts = lax.optimization_barrier((x_rows, both_w, down_parts))
    down_w = gather_lane(w_down, down_parts).swapaxes(0, 1)
    down_w = down_w.reshape(local_experts, hidden_half, width)

    sums = ()
    d_gates, grads_both, grads_down = [], [], []
    for e in range(local_experts):
        *sums, d_gate, hid, d_gate_pre, d_up_pre = expert(
            gates[..., e : e + 1], x_rows, g_rows, both_w[e], down_w[e], tuple(sums), f"expert_{e}"
        )
        d_gates.append(d_gate)
        grad_both, grad_down = expert_grads(
            x_rows, g_rows, hid, d_gate_pre, d_up_pre, dp_size, f"expert_grads_{e}"
        )
        sums[0], grad_both = lax.optimization_barrier((sums[0], grad_both))
        grads_both.append(exchange(grad_both, DP) if e < local_experts - 1 else grad_both)
        grads_down.append(grad_down)
    moe_own, moe_other, d_own, d_other = sums
    d_own, grads_both, grads_down = lax.optimization_barrier((d_own, grads_both, grads_down))
    grads_down = jnp.stack(grads_down)
    d_mixed, moe_sum, last_both, down_others = scatter_all(
        [(d_own, d_other), (moe_own, moe_other)], True, "scatter_experts", 3,
        (grads_both[-1], grads_down),
    )
    grads_both[-1] = last_both
    d_gates = jnp.concatenate(d_gates, axis=-1)
    d_gates = d_gates.reshape(2 * quads, 2, batches, rows, local_experts)
    d_gates = d_gates.transpose(1, 0, 4, 2, 3)
    d_gates, d_mixed = lax.optimization_barrier((d_gates, d_mixed))
    d_router = exchange_rows(d_gates, "inward", "gate_gradients", 9, 2)
    d_router = jnp.sum(d_router, axis=0).reshape(expert_count, batches, rows)
    d_router = d_router.transpose(1, 2, 0) * routed
    d_logits = (
        router * (d_router - jnp.sum(router * d_router, axis=-1, keepdims=True))
    ).astype(BF)
    d_mixed = d_mixed + dot("mte,de->mtd", d_logits, router_w)

    def norm_back_all(values, root, gain, grad):
        d_values, d_gain = norm_back(values, root, gain, grad)
        return d_values, jnp.sum(d_gain, axis=0)

    d_mid, part_mlp_gain = norm_back_all(x_mid, mlp_root, gain_mlp, d_mixed)
    d_mid = d_mid + grad_low.astype(F32)
    d_att_out = d_mid.astype(BF)
    d_attended = dot("mte,de->mtd", d_att_out, out_w).astype(BF)
    d_attended = d_attended.reshape(batches, rows, ctx_size, head_width).transpose(2, 0, 1, 3)
    d_attended = exchange_rows(d_attended, "outward", "attended_gradients", 10)[0]
    part_query_gain = part_key_gain = 0.0
    parts = []
    inners = []
    for m in range(batches):
        s = saved[m]
        d_att = d_attended[:, m].reshape(slot_len, heads, HEAD)
        probs, query, key = s["probs"], s["query"], s["key"]
        d_probs = dot("qhd,khd->hqk", d_att, s["value"])
        inner = jnp.sum(probs * d_probs, axis=-1, keepdims=True)
        d_scores = (probs * (d_probs - inner)).astype(BF)
        d_query = dot("hqk,khd->qhd", d_scores, key) * factor
        d_key = dot("hqk,qhd->khd", d_scores, query) * factor
        d_value = dot("hqk,qhd->khd", s["probs_low"], d_att)
        d_query = rotate_back(d_query, cosine, sine).reshape(slot_len, head_width)
        d_key = rotate_back(d_key, cosine, sine).reshape(slot_len, head_width)
        parts.append((d_query, d_key, d_value))
        inners += [
            jnp.sum(d_query * gain_query * s["query_pre"], axis=1).reshape(-1, rows),
            jnp.sum(d_key * gain_key * s["key_pre"], axis=1).reshape(-1, rows),
        ]
    inners = sum_ctx(jnp.stack(inners, axis=1), "sum_inner", 11) / width
    d_pre_all = []
    for m in range(batches):
        s = saved[m]
        d_query, d_key, d_value = parts[m]
        query_pre, key_pre = s["query_pre"], s["key_pre"]
        query_root, key_root = s["query_root"], s["key_root"]
        query_inner = inners[:, 2 * m].reshape(slot_len, 1)
        key_inner = inners[:, 2 * m + 1].reshape(slot_len, 1)
        d_query_pre = query_root * (d_query * gain_query) - query_pre * query_root**3 * query_inner
        d_key_pre = key_root * (d_key * gain_key) - key_pre * key_root**3 * key_inner
        part_query_gain = part_query_gain + jnp.sum(d_query * query_pre * query_root, axis=0)
        part_key_gain = part_key_gain + jnp.sum(d_key * key_pre * key_root, axis=0)
        d_pre = jnp.concatenate(
            [
                d_query_pre.astype(BF),
                d_key_pre.astype(BF),
                d_value.reshape(slot_len, head_width).astype(BF),
            ],
            axis=1,
        )
        d_pre_all.append(d_pre.reshape(2, quads, rows, 3 * head_width))
    d_pre = jnp.stack(d_pre_all, axis=2).reshape(2, -1, 3 * head_width)
    d_act = [
        dot("te,de->td", d_pre[i], qkv_w).astype(BF).reshape(quads, batches, rows, width)
        for i in range(2)
    ]
    d_act = scatter_all([(d_act[0], d_act[1])], False, "scatter_act", 4)[0]
    d_inputs, part_attn_gain = norm_back_all(inputs, attn_root, gain_attn, d_act)
    mixed = (x_mid + moe_sum).astype(BF)

    grads_both = jnp.stack(grads_both, axis=2).astype(F32)
    grads_both = grads_both.reshape(2, lanes, 2, local_experts, depth_part, hidden_half).sum(axis=1)
    grads_both = grads_both.transpose(1, 2, 3, 0, 4)
    grad_gate, grad_up = grads_both.reshape(2, local_experts, depth_part, hidden_units)
    grads_down = grads_down.reshape(local_experts, lanes, -1, width)
    grad_down = lax.dynamic_index_in_dim(grads_down, lax.axis_index("lane"), 1, keepdims=False)
    grad_down = grad_down.astype(F32) + jnp.sum(down_others.astype(F32), axis=0)

    grad_out = dot("mtd,mte->de", attended, d_att_out).astype(BF)
    grad_out = lax.psum_scatter(grad_out, ALL, scatter_dimension=0, tiled=True).astype(F32)
    acts = [part.reshape(-1, width) for part in act]
    grad_qkv = sum(dot("td,te->de", x, y) for x, y in zip(acts, d_pre)).astype(BF)
    grad_qkv = lax.psum_scatter(grad_qkv, DP, scatter_dimension=0, tiled=True)
    grad_qkv = grad_qkv.reshape(ctx_size, shard, 3 * head_width)
    grad_qkv = exchange_rows(grad_qkv, "ctx", "qkv_gradients", 14).astype(F32)
    grad_qkv = grad_qkv.reshape(ctx_size, shard, 3, head_width).transpose(2, 1, 0, 3)
    grad_qkv = grad_qkv.reshape(3, shard, width)

    grad_router = dot("mtd,mte->de", mixed_in, d_logits)
    columns = jnp.arange(ctx_size, dtype=jnp.int32)[:, None] == here

    def placed(part):
        return jnp.where(columns, part[None, :], 0.0).reshape(width)

    gains = jnp.stack(
        [part_attn_gain, part_mlp_gain, placed(part_query_gain), placed(part_key_gain)]
    )
    gains = gains.reshape(4, dp_size, ctx_size, shard).transpose(1, 2, 0, 3)
    packed = jnp.concatenate(
        [
            gains.reshape(dp_size * ctx_size, 1, 4 * shard),
            grad_router.reshape(dp_size * ctx_size, 1, shard * expert_count),
        ],
        axis=2,
    )
    packed = reduce_small(packed)
    return (
        mixed[:, None],
        (d_inputs + d_mid)[:, None],
        grad_qkv[0],
        grad_qkv[1],
        grad_qkv[2],
        grad_out,
        packed[4 * shard :].reshape(shard, expert_count),
        grad_gate,
        grad_up,
        grad_down,
        packed[:shard],
        packed[shard : 2 * shard],
        packed[2 * shard : 3 * shard],
        packed[3 * shard : 4 * shard],
    )


def solution(mesh):
    dp_size, ctx_size = mesh.shape["dp"], mesh.shape["ctx"]
    grid = Mesh(mesh.devices.reshape(2, dp_size // 2, ctx_size // 2, 2), ALL)
    rows = P(None, DP, CTX, None)
    dense = P(ALL, None)
    expert = P(CTX, DP, None)
    vector = P(ALL)
    return jax.shard_map(
        on_device,
        mesh=grid,
        in_specs=(rows, rows, rows, P(None, DP), P())
        + (dense,) * 5
        + (expert,) * 3
        + (vector,) * 4,
        out_specs=(rows, rows) + (dense,) * 5 + (expert,) * 3 + (vector,) * 4,
        check_vma=False,
    )
```

```python
import functools
import math

import jax
import jax.numpy as jnp
from jax import lax
from jax.experimental import pallas as pl
from jax.experimental.pallas import tpu as pltpu
from jax.sharding import Mesh
from jax.sharding import PartitionSpec as P

HEAD = 128
EPSILON = 1e-05
ROPE_BASE = 10000.0
MASKED = -1e30
BF = jnp.bfloat16
F32 = jnp.float32
DP = ("half", "lane")
CTX = ("quad", "pair")
ALL = DP + CTX
MESH = pl.DeviceIdType.MESH


def dot(spec, left, right):
    return jnp.einsum(spec, left, right, preferred_element_type=F32)


def inv_rms(values):
    return lax.rsqrt(jnp.mean(values * values, axis=-1, keepdims=True) + EPSILON)


def norm_back(values, inv_root, gain_vec, grad_in):
    weighted = grad_in * gain_vec
    inner = jnp.mean(weighted * values, axis=-1, keepdims=True)
    grad_values = inv_root * weighted - values * (inv_root * inv_root * inv_root) * inner
    return (grad_values, jnp.sum(grad_in * values * inv_root, axis=0))


def angles(places, head_width):
    index = jnp.arange(head_width // 2, dtype=F32)
    freqs = jnp.power(ROPE_BASE, -2.0 * index / head_width)
    turning = places.astype(F32)[:, None] * freqs[None, :]
    turning = jnp.concatenate([turning, turning], axis=1)
    return (jnp.cos(turning)[:, None, :], jnp.sin(turning)[:, None, :])


def rotate(values, cosine, sine):
    half_size = values.shape[-1] // 2
    turned = jnp.concatenate([-values[..., half_size:], values[..., :half_size]], axis=-1)
    return values * cosine + turned * sine


def rotate_back(grad_in, cosine, sine):
    half_size = grad_in.shape[-1] // 2
    moved = grad_in * sine
    return grad_in * cosine + jnp.concatenate(
        [moved[..., half_size:], -moved[..., :half_size]], axis=-1
    )


def swap(values, axis):
    return lax.ppermute(values, axis, [(0, 1), (1, 0)])


def exchange(blocks, axes):
    return lax.all_to_all(blocks, axes, split_axis=0, concat_axis=0, tiled=True)


def lane_parts(values):
    if lax.axis_size("lane") == 2:
        return swap(values, "lane")
    return lax.all_gather(values, "lane", axis=0, tiled=False)


def gather_lane(values, parts):
    if lax.axis_size("lane") == 2:
        first = lax.axis_index("lane") == 0
        return jnp.stack([jnp.where(first, values, parts), jnp.where(first, parts, values)])
    return parts


def reduce_small(values):
    return jnp.sum(exchange_rows(values, "all", "small_gradients", 15), axis=(0, 1))


def toggled(index, bits):
    step = 1
    while step <= bits:
        if bits & step:
            index = index + step - 2 * step * ((index // step) % 2)
        step *= 2
    return index


def greet(peers):
    barrier = pltpu.get_barrier_semaphore()
    for peer in peers:
        pl.semaphore_signal(barrier, inc=1, device_id=peer, device_id_type=MESH)
    pl.semaphore_wait(barrier, len(peers))


class Mover:
    def __init__(self, send, recv, local):
        self.send, self.recv, self.local = send, recv, local
        self.number, self.local_number = 0, 0
        self.sent, self.kept = [], []

    def copy(self, src, dst, device):
        i = self.number
        self.number += 1
        return pltpu.make_async_remote_copy(
            src_ref=src, dst_ref=dst, send_sem=self.send.at[i], recv_sem=self.recv.at[i],
            device_id=device, device_id_type=MESH,
        )

    def go(self, *copies):
        for c in copies:
            c.start()
            self.sent.append(c)

    def keep(self, src, dst):
        c = pltpu.make_async_copy(src, dst, self.local.at[self.local_number])
        self.local_number += 1
        c.start()
        self.kept.append(c)
        return c

    def finish(self):
        for c in self.sent:
            c.wait_send()
        for c in self.kept:
            c.wait()


class Spread:
    def __init__(self, mover, quads, src, slot):
        self.mover, self.quads = mover, quads
        quad = lax.axis_index("quad")
        to_quad = [{"quad": toggled(quad, k)} for k in range(quads)]
        sibling = {"pair": 1 - lax.axis_index("pair")}
        rows = src.shape[0]
        halves = (("a", pl.ds(0, rows // 2)), ("b", pl.ds(rows // 2, rows // 2)))
        p = {"o0": mover.copy(src, slot(1, 0, 0), sibling)}
        if quads == 4:
            for k in (1, 2):
                for name, part in halves:
                    p[f"s{k}{name}"] = mover.copy(
                        src.at[part], slot(0, k, 0).at[part], to_quad[k]
                    )
            for k, (name, part) in zip((1, 2), halves):
                p[f"f3{name}"] = mover.copy(
                    slot(0, k, k).at[part], slot(0, 3, k).at[part], to_quad[3 - k]
                )
            for k in (1, 2, 3):
                for name, part in halves:
                    p[f"o{k}{name}"] = mover.copy(
                        slot(0, k, k).at[part], slot(1, k, k).at[part], sibling
                    )
        else:
            for k in range(1, quads):
                p[f"s{k}"] = mover.copy(src, slot(0, k, 0), to_quad[k])
                p[f"o{k}"] = mover.copy(slot(0, k, k), slot(1, k, k), sibling)
        self.copies = p

    @staticmethod
    def count(quads):
        return 13 if quads == 4 else 2 * quads - 1

    def begin(self):
        names = [f"s{k}" for k in range(1, self.quads)]
        if self.quads == 4:
            names = ["s1a", "s2b", "s1b", "s2a"]
        self.mover.go(*[self.copies[name] for name in names + ["o0"]])

    def forward(self):
        p = self.copies
        steps = [(f"s{k}", (f"o{k}",)) for k in range(1, self.quads)]
        if self.quads == 4:
            steps = [
                ("s1a", ("f3a", "o1a")), ("s2b", ("f3b", "o2b")), ("s1b", ("o1b",)),
                ("s2a", ("o2a",)), ("f3a", ("o3a",)), ("f3b", ("o3b",)),
            ]
        for name, then in steps:
            p[name].wait_recv()
            self.mover.go(*[p[t] for t in then])

    def arrive(self):
        for name, c in self.copies.items():
            if name[0] == "o":
                c.wait_recv()


def relative_slots(own_ref, other_ref, s):
    return lambda core, kr, km: (other_ref if core else own_ref).at[kr, s]


def ctx_peers(quads):
    return [ctx_at(quads, n)[0] for n in range(1, 2 * quads)]


def planes_of(lanes):
    half, lane = lax.axis_index("half"), lax.axis_index("lane")
    result = []
    for n in range(1, 2 * lanes):
        h, l = toggled(half, n // lanes), toggled(lane, n % lanes)
        result.append(({"half": h, "lane": l}, h * lanes + l))
    return half * lanes + lane, result


def gather_body(quads, partners, *refs):
    inputs = refs[: len(partners)]
    refs = refs[len(partners) :]
    outputs = [(refs[2 * i], refs[2 * i + 1]) for i in range(len(partners))]
    refs = refs[2 * len(partners) :]
    keeps = {}
    for i, partner in enumerate(partners):
        if partner:
            keeps[i], refs = refs[0], refs[1:]
    local, send, recv = refs
    mover = Mover(send, recv, local)
    across = {"half": 1 - lax.axis_index("half")}
    quad = lax.axis_index("quad")
    peers = [{"quad": toggled(quad, k)} for k in range(1, quads)]
    peers.append({"pair": 1 - lax.axis_index("pair")})
    greet(peers + ([across] if keeps else []))

    def add(sources, i, offset):
        plans = []
        for s, src in enumerate(sources):
            p = Spread(mover, quads, src, relative_slots(*outputs[i], offset + s))
            p.begin()
            plans.append(p)
            mover.keep(src, outputs[i][0].at[0, offset + s])
        return plans

    crossing = {}
    for i, keep in keeps.items():
        crossing[i] = [
            mover.copy(inputs[i].at[s], keep.at[s], across) for s in range(inputs[i].shape[0])
        ]
        mover.go(*crossing[i])
    plans = []
    for i, ref in enumerate(inputs):
        plans += add([ref.at[s] for s in range(ref.shape[0])], i, 0)
    for p in plans:
        p.forward()
    late = []
    for i, keep in keeps.items():
        for c in crossing[i]:
            c.wait_recv()
        late += add([keep.at[s] for s in range(keep.shape[0])], i, keep.shape[0])
    for p in late:
        p.forward()
    for p in plans + late:
        p.arrive()
    mover.finish()


def gather_rows(sources, partners, name, number):
    quads = lax.axis_size("quad")
    shapes, keeps = [], []
    sems = total = 0
    for x, partner in zip(sources, partners):
        count = x.shape[0] * (2 if partner else 1)
        total += count
        sems += count * Spread.count(quads) + (x.shape[0] if partner else 0)
        shapes += [jax.ShapeDtypeStruct((quads, count) + x.shape[1:], x.dtype)] * 2
        if partner:
            keeps.append(pltpu.VMEM(x.shape, x.dtype))
    out = pl.pallas_call(
        functools.partial(gather_body, quads, partners),
        out_shape=shapes,
        in_specs=[pl.BlockSpec(memory_space=pltpu.VMEM)] * len(sources),
        out_specs=[pl.BlockSpec(memory_space=pl.ANY)] * len(shapes),
        scratch_shapes=keeps
        + [
            pltpu.SemaphoreType.DMA((total,)),
            pltpu.SemaphoreType.DMA((sems,)),
            pltpu.SemaphoreType.DMA((sems,)),
        ],
        compiler_params=pltpu.CompilerParams(collective_id=number, has_side_effects=True),
        name=name,
    )(*sources)
    return [(out[2 * i], out[2 * i + 1]) for i in range(len(sources))]


def start_body(
    quads, lanes, tok_ref, qkv_ref, small_ref, wout_ref,
    tok_own, tok_other, qkv_out, small_out, wout_out, local, send, recv,
):
    mover = Mover(send, recv, local)
    half, lane = lax.axis_index("half"), lax.axis_index("lane")
    plane, here = half * lanes + lane, ctx_place()
    partner = (1 - half) * lanes + lane
    across = {"half": 1 - half}
    devices = 4 * lanes * quads
    others = [all_at(lanes, quads, n)[0] for n in range(1, devices)]
    greet(others)
    mine = mover.keep(small_ref, small_out.at[plane * 2 * quads + here])
    shared = [mover.copy(small_ref, small_out.at[plane * 2 * quads + here], d) for d in others]
    mover.go(*shared)

    def planes(src, view):
        first = mover.copy(src, view(plane), across)
        rest = [
            mover.copy(src, view(plane), {"lane": toggled(lane, d)}) for d in range(1, lanes)
        ]
        then = [
            mover.copy(view(partner), view(partner), {"lane": toggled(lane, d)})
            for d in range(1, lanes)
        ]
        mover.go(first, *rest)
        return first, rest, then

    mover.keep(wout_ref, wout_out.at[plane, here])
    w_first, w_rest, w_then = planes(wout_ref, lambda p: wout_out.at[p, here])
    kept = mover.keep(qkv_ref.at[here], qkv_out.at[plane, here])
    columns = []
    for n in range(1, 2 * quads):
        device, place = ctx_at(quads, n)
        columns.append(mover.copy(qkv_ref.at[place], qkv_out.at[plane, here], device))
    mover.go(*columns)
    tokens = []
    for s in range(tok_ref.shape[0]):
        p = Spread(mover, quads, tok_ref.at[s], relative_slots(tok_own, tok_other, s))
        p.begin()
        tokens.append(p)
        mover.keep(tok_ref.at[s], tok_own.at[0, s])
    for c in columns:
        c.wait_recv()
    kept.wait()
    mover.kept = [c for c in mover.kept if c is not kept]
    q_first, q_rest, q_then = planes(qkv_out.at[plane], lambda p: qkv_out.at[p])
    w_first.wait_recv()
    mover.go(*w_then)

    def wout_slots(p):
        pair = lax.axis_index("pair")
        quad = lax.axis_index("quad")
        return lambda core, kr, km: wout_out.at[p, toggled(quad, km) * 2 + pair]

    weights = [Spread(mover, quads, wout_ref, wout_slots(plane))]
    weights[0].begin()
    tokens[0].forward()
    for c in w_rest:
        c.wait_recv()
    for c in w_then:
        c.wait_recv()
    for n in range(1, 2 * lanes):
        p = toggled(half, n // lanes) * lanes + toggled(lane, n % lanes)
        weights.append(Spread(mover, quads, wout_out.at[p, here], wout_slots(p)))
        weights[-1].begin()
    q_first.wait_recv()
    mover.go(*q_then)
    for p in tokens[1:] + weights:
        p.forward()
    for p in tokens + weights:
        p.arrive()
    for c in shared + q_rest + q_then:
        c.wait_recv()
    mover.finish()


def start_gather(tokens, qkv, small, w_out):
    quads, lanes = lax.axis_size("quad"), lax.axis_size("lane")
    count = tokens.shape[0]
    planes, devices = 2 * lanes, 4 * lanes * quads

    def like(lead, x, dtype=BF):
        return jax.ShapeDtypeStruct(lead + x.shape, dtype)

    sems = (devices - 1) + 2 * (2 * lanes - 1) + (2 * quads - 1)
    sems += Spread.count(quads) * (count + planes)
    return pl.pallas_call(
        functools.partial(start_body, quads, lanes),
        out_shape=[like((quads,), tokens)] * 2
        + [like((planes,), qkv), like((devices,), small)]
        + [like((planes, 2 * quads), w_out)],
        in_specs=[pl.BlockSpec(memory_space=pltpu.VMEM)] * 4,
        out_specs=[pl.BlockSpec(memory_space=pl.ANY)] * 5,
        scratch_shapes=[
            pltpu.SemaphoreType.DMA((3 + count,)),
            pltpu.SemaphoreType.DMA((sems,)),
            pltpu.SemaphoreType.DMA((sems,)),
        ],
        compiler_params=pltpu.CompilerParams(collective_id=0, has_side_effects=True),
        name="start_gather",
    )(tokens, qkv, small, w_out)


def add_rows(out_ref, *refs):
    rows = out_ref.shape[0]
    step = 16

    @pl.loop(0, rows // step)
    def _(i):
        part = pl.ds(pl.multiple_of(i * step, step), step)
        total = refs[0][part].astype(F32)
        for ref in refs[1:]:
            total = total + ref[part].astype(F32)
        out_ref[part] = total.astype(out_ref.dtype)


def scatter_body(quads, lanes, kinds, count, partner, extra, *refs):
    inputs = [(refs[2 * i], refs[2 * i + 1]) for i in range(kinds)]
    refs = refs[2 * kinds :]
    if extra:
        blocks_ref, down_ref, *refs = refs
    outputs, refs = refs[:kinds], refs[kinds:]
    if extra:
        blocks_out, down_out, held, *refs = refs
    mine, theirs, relay, arrived, *rest = refs
    if partner:
        summed, back, *rest = rest
    local, send, recv = rest
    mover = Mover(send, recv, local)
    mover.local_number = local.shape[0] - 2
    total, rows = inputs[0][0].shape[1:3]
    first, second = pl.ds(0, rows // 2), pl.ds(rows // 2, rows // 2)
    quad = lax.axis_index("quad")
    to_quad = [{"quad": toggled(quad, k)} for k in range(quads)]
    sibling = {"pair": 1 - lax.axis_index("pair")}
    across = {"half": 1 - lax.axis_index("half")}
    peers = to_quad[1:] + [sibling]
    if extra:
        me, planes = planes_of(lanes)
        peers += [device for device, _ in planes]
    elif partner:
        peers.append(across)
    greet(peers)

    def go(src, dst, device):
        c = mover.copy(src, dst, device)
        mover.go(c)
        return c

    order = [(i, s) for i in range(kinds) for s in range(count, total)]
    order += [(i, s) for i in range(kinds) for s in range(count)]
    ks = [3, 1, 2, 0] if quads == 4 else list(range(quads - 1, -1, -1))
    sib, loc = {}, {}
    for n, (i, s) in enumerate(order):
        for k in ks:
            sib[n, k] = go(inputs[i][1].at[k, s], theirs.at[n, k], sibling)
            loc[n, k] = pltpu.make_async_copy(
                inputs[i][0].at[k, s], mine.at[n, k], local.at[n * quads + k]
            )
            loc[n, k].start()
    sends = {}

    def merge(n):
        for k in ks:
            sib[n, k].wait_recv()
            loc[n, k].wait()
            add_rows(mine.at[n, k], mine.at[n, k], theirs.at[n, k])
            if quads == 4:
                if k == 3:
                    sends[n, "3a"] = go(mine.at[n, 3, first], relay.at[n, 0], to_quad[2])
                    sends[n, "3b"] = go(mine.at[n, 3, second], relay.at[n, 1], to_quad[1])
                elif k == 1:
                    sends[n, "1b"] = go(mine.at[n, 1, second], arrived.at[n, 0, second], to_quad[1])
                elif k == 2:
                    sends[n, "2a"] = go(mine.at[n, 2, first], arrived.at[n, 1, first], to_quad[2])
            elif k:
                sends[n, k] = go(mine.at[n, k], arrived.at[n, k - 1], to_quad[k])

    def pass_on(n):
        if quads == 4:
            sends[n, "3a"].wait_recv()
            add_rows(mine.at[n, 1, first], mine.at[n, 1, first], relay.at[n, 0])
            sends[n, "1a"] = go(mine.at[n, 1, first], arrived.at[n, 0, first], to_quad[1])
            sends[n, "3b"].wait_recv()
            add_rows(mine.at[n, 2, second], mine.at[n, 2, second], relay.at[n, 1])
            sends[n, "2b"] = go(mine.at[n, 2, second], arrived.at[n, 1, second], to_quad[2])

    backs = {}

    def total_of(n):
        i, s = order[n]
        for name in ("1b", "2a", "1a", "2b") if quads == 4 else range(1, quads):
            sends[n, name].wait_recv()
        parts = [mine.at[n, 0]] + [arrived.at[n, j] for j in range(arrived.shape[1])]
        if s >= count:
            slot = i * count + s - count
            add_rows(summed.at[slot], *parts)
            backs[slot] = go(summed.at[slot], back.at[slot], across)
        else:
            if partner:
                backs[i * count + s].wait_recv()
                parts.append(back.at[i * count + s])
            add_rows(outputs[i].at[s], *parts)

    ahead = 2
    exchanged = []

    def exchange_gate():
        lane = lax.axis_index("lane")
        part = down_ref.shape[1] // lanes
        for e in range(down_ref.shape[0]):
            for d in range(1, lanes):
                to = toggled(lane, d)
                src = down_ref.at[e, pl.ds(pl.multiple_of(to * part, part), part)]
                exchanged.append(go(src, down_out.at[d - 1, e], {"lane": to}))
        for device, place in planes:
            exchanged.append(go(blocks_ref.at[place, 0], blocks_out.at[me, 0], device))

    def exchange_up():
        for device, place in planes:
            exchanged.append(go(blocks_ref.at[place, 1], blocks_out.at[me, 1], device))

    if extra:
        into = mover.keep(blocks_ref.at[me], held)
        exchange_gate()
    for n in range(len(order) + 2 * ahead):
        if extra and n == kinds * count + 2 * ahead:
            exchange_up()
            into.wait()
            mover.kept = [c for c in mover.kept if c is not into]
            mover.keep(held, blocks_out.at[me])
        if n < len(order):
            merge(n)
        if 0 <= n - 1 < len(order):
            pass_on(n - 1)
        if 0 <= n - 2 * ahead < len(order):
            total_of(n - 2 * ahead)
    for c in exchanged:
        c.wait_recv()
    mover.finish()


def scatter_rows(pairs, partner, name, number, extra=()):
    lanes = lax.axis_size("lane")
    quads, total, rows, width = pairs[0][0].shape
    count = total // 2 if partner else total
    kinds = len(pairs)
    shards = kinds * total
    incoming = 2 if quads == 4 else quads - 1
    sems = shards * (quads + (6 if quads == 4 else quads - 1)) + (kinds * count if partner else 0)

    def buf(*lead):
        return pltpu.VMEM(lead + (rows, width), BF)

    scratch = [buf(shards, quads), buf(shards, quads)]
    scratch += [pltpu.VMEM((shards, 2, rows // 2, width), BF), buf(shards, incoming)]
    if partner:
        scratch += [buf(kinds * count), buf(kinds * count)]
    shapes = [jax.ShapeDtypeStruct((count, rows, width), F32)] * kinds
    specs = [pl.BlockSpec(memory_space=pltpu.VMEM)] * kinds
    anywhere = pl.BlockSpec(memory_space=pl.ANY)
    if extra:
        blocks, down = extra
        n_exp, hidden = down.shape[:2]
        shapes = shapes + [
            jax.ShapeDtypeStruct(blocks.shape, BF),
            jax.ShapeDtypeStruct((lanes - 1, n_exp, hidden // lanes, width), BF),
        ]
        specs = specs + [anywhere] * 2
        scratch = [pltpu.VMEM(blocks.shape[1:], BF)] + scratch
        sems += 2 * (2 * lanes - 1) + n_exp * (lanes - 1)
    return pl.pallas_call(
        functools.partial(scatter_body, quads, lanes, kinds, count, partner, bool(extra)),
        out_shape=shapes,
        in_specs=[anywhere] * (2 * kinds + len(extra)),
        out_specs=specs,
        scratch_shapes=scratch
        + [
            pltpu.SemaphoreType.DMA((shards * quads + 2,)),
            pltpu.SemaphoreType.DMA((sems,)),
            pltpu.SemaphoreType.DMA((sems,)),
        ],
        compiler_params=pltpu.CompilerParams(
            collective_id=number, has_side_effects=True, vmem_limit_bytes=60 << 20
        ),
        name=name,
    )(*[ref for pair in pairs for ref in pair], *extra)


def ctx_place():
    return lax.axis_index("quad") * 2 + lax.axis_index("pair")


def ctx_at(quads, number):
    core, distance = number // quads, number % quads
    quad = toggled(lax.axis_index("quad"), distance)
    pair = toggled(lax.axis_index("pair"), core)
    return {"quad": quad, "pair": pair}, quad * 2 + pair


def all_at(lanes, quads, number):
    half = toggled(lax.axis_index("half"), number // (lanes * 2 * quads))
    lane = toggled(lax.axis_index("lane"), number // (2 * quads) % lanes)
    device, place = ctx_at(quads, number % (2 * quads))
    return {"half": half, "lane": lane, **device}, (half * lanes + lane) * 2 * quads + place


def exchange_body(mode, lanes, quads, halves, x_ref, out_ref, local, send, recv):
    copies = []
    peers = []
    if mode in ("shared", "all"):
        me = (lax.axis_index("half") * lanes + lax.axis_index("lane")) * 2 * quads + ctx_place()
        for n in range(2 * lanes * 2 * quads):
            device, place = all_at(lanes, quads, n)
            copies.append((x_ref if mode == "shared" else x_ref.at[place], out_ref.at[me], device))
    else:
        for h in range(halves):
            for n in range(2 * quads):
                device, place = ctx_at(quads, n)
                if halves == 2:
                    device = {"half": toggled(lax.axis_index("half"), h), **device}
                if mode == "inward":
                    pair = (x_ref.at[h, n], out_ref.at[h, ctx_place()])
                elif mode == "outward":
                    pair = (x_ref.at[place], out_ref.at[h, n])
                else:
                    pair = (x_ref.at[place], out_ref.at[ctx_place()])
                copies.append(pair + (device,))
    own = pltpu.make_async_copy(copies[0][0], copies[0][1], local)
    own.start()
    greet([device for _, _, device in copies[1:]])
    started = []
    for i, (src, dst, device) in enumerate(copies[1:]):
        c = pltpu.make_async_remote_copy(
            src_ref=src, dst_ref=dst, send_sem=send.at[i], recv_sem=recv.at[i],
            device_id=device, device_id_type=MESH,
        )
        c.start()
        started.append(c)
    own.wait()
    for c in started:
        c.wait_recv()
    for c in started:
        c.wait_send()


def exchange_rows(x, mode, name, number, halves=1):
    quads, lanes = lax.axis_size("quad"), lax.axis_size("lane")
    count = halves * 2 * quads - 1
    shape = x.shape
    if mode == "outward":
        shape = (halves, 2 * quads) + x.shape[1:]
    elif mode in ("shared", "all"):
        count = 4 * lanes * quads - 1
        if mode == "shared":
            shape = (count + 1,) + x.shape
    return pl.pallas_call(
        functools.partial(exchange_body, mode, lanes, quads, halves),
        out_shape=jax.ShapeDtypeStruct(shape, x.dtype),
        in_specs=[pl.BlockSpec(memory_space=pltpu.VMEM)],
        out_specs=pl.BlockSpec(memory_space=pltpu.VMEM),
        scratch_shapes=[
            pltpu.SemaphoreType.DMA,
            pltpu.SemaphoreType.DMA((count,)),
            pltpu.SemaphoreType.DMA((count,)),
        ],
        compiler_params=pltpu.CompilerParams(collective_id=number, has_side_effects=True),
        name=name,
    )(x)


def sum_body(quads, x_ref, out_ref, landed, send, recv):
    count = 2 * quads
    greet([ctx_at(quads, n)[0] for n in range(1, count)])
    started = []
    for n in range(1, count):
        c = pltpu.make_async_remote_copy(
            src_ref=x_ref, dst_ref=landed.at[n - 1], send_sem=send.at[n - 1],
            recv_sem=recv.at[n - 1], device_id=ctx_at(quads, n)[0], device_id_type=MESH,
        )
        c.start()
        started.append(c)
    for c in started:
        c.wait_recv()
    for j in range(count):
        total = x_ref[j]
        for n in range(1, count):
            total = total + landed[n - 1, j ^ n]
        out_ref[j] = total
    for c in started:
        c.wait_send()


def sum_ctx(x, name, number):
    quads = lax.axis_size("quad")
    count = 2 * quads - 1
    return pl.pallas_call(
        functools.partial(sum_body, quads),
        out_shape=jax.ShapeDtypeStruct(x.shape, x.dtype),
        in_specs=[pl.BlockSpec(memory_space=pltpu.VMEM)],
        out_specs=pl.BlockSpec(memory_space=pltpu.VMEM),
        scratch_shapes=[
            pltpu.VMEM((count,) + x.shape, x.dtype),
            pltpu.SemaphoreType.DMA((count,)),
            pltpu.SemaphoreType.DMA((count,)),
        ],
        compiler_params=pltpu.CompilerParams(collective_id=number, has_side_effects=True),
        name=name,
    )(x)


def nn(left, right):
    return lax.dot_general(left, right, (((1,), (0,)), ((), ())), preferred_element_type=F32)


def nt(left, right):
    return lax.dot_general(left, right, (((1,), (1,)), ((), ())), preferred_element_type=F32)


def tn(left, right):
    return lax.dot_general(left, right, (((0,), (0,)), ((), ())), preferred_element_type=F32)


def expert_body(quads, before, _, gate_ref, xo_ref, xt_ref, go_ref, gp_ref, both_ref, down_ref, *refs):
    sums = refs[:4] if before else None
    mo_ref, mt_ref, do_ref, dt_ref, dgate_ref, hid_ref, dg_ref, du_ref = refs[-8:]
    t = pl.program_id(0)
    core_other = t >= 2 * quads
    partner = t % 2 == 1
    hidden, width = down_ref.shape
    x = jnp.where(core_other, xt_ref[0], xo_ref[0]).reshape(-1, width)
    g = jnp.where(partner, gp_ref[0], go_ref[0]).reshape(-1, width)
    gate = gate_ref[0]
    wg = both_ref[:, 0].reshape(width, hidden)
    wu = both_ref[:, 1].reshape(width, hidden)
    wd = down_ref[...]
    gate_pre = nn(x, wg)
    up_pre = nn(x, wu)
    d_hidden = nt(g, wd)
    sigma = 1.0 / (1.0 + jnp.exp(-gate_pre))
    silu = gate_pre * sigma
    hid = silu * up_pre
    dgate_ref[0] = jnp.sum(hid * d_hidden, axis=1, keepdims=True)
    d_hidden = d_hidden * gate
    scaled = (hid * gate).astype(BF)
    d_gate_pre = (d_hidden * up_pre * (sigma + silu * (1.0 - sigma))).astype(BF)
    d_up_pre = (d_hidden * silu).astype(BF)
    hid_ref[0] = scaled
    dg_ref[0] = d_gate_pre
    du_ref[0] = d_up_pre
    moe = nn(scaled, wd).reshape(mo_ref.shape[1:])
    d_rows = (nt(d_gate_pre, wg) + nt(d_up_pre, wu)).reshape(mo_ref.shape[1:])
    if before:
        moe = moe + jnp.where(core_other, sums[1][0], sums[0][0]).astype(F32)
        d_rows = d_rows + jnp.where(core_other, sums[3][0], sums[2][0]).astype(F32)
    moe, d_rows = moe.astype(BF), d_rows.astype(BF)

    @pl.when(jnp.logical_not(core_other))
    def _():
        mo_ref[0] = moe
        do_ref[0] = d_rows

    @pl.when(core_other)
    def _():
        mt_ref[0] = moe
        dt_ref[0] = d_rows


def expert(place, gates, x_rows, g_rows, both, down, before, name):
    quads, shards, rows, width = x_rows[0].shape
    batches = shards // 2
    hidden = down.shape[0]
    tiles = 4 * quads
    tile = batches * rows

    def own(t, p):
        return (jnp.minimum(t, 2 * quads - 1) // 2, jnp.minimum(t, 2 * quads - 1) % 2, 0, 0)

    def other(t, p):
        u = jnp.maximum(t - 2 * quads, 0)
        return (u // 2, u % 2, 0, 0)

    def cot(t, p):
        return (p[t // 2], 0, 0, 0)

    shard_block = (1, batches, rows, width)
    saved_spec = pl.BlockSpec((1, tile, hidden), lambda t, p: (t, 0, 0))
    saved = jax.ShapeDtypeStruct((tiles, tile, hidden), BF)
    rows_shape = jax.ShapeDtypeStruct(x_rows[0].shape, BF)
    fixed = dict(pipeline_mode=pl.Buffered(1))
    sums_specs = [
        pl.BlockSpec(shard_block, own), pl.BlockSpec(shard_block, other),
        pl.BlockSpec(shard_block, own), pl.BlockSpec(shard_block, other),
    ]
    return pl.pallas_call(
        functools.partial(expert_body, quads, bool(before)),
        out_shape=(rows_shape,) * 4
        + (jax.ShapeDtypeStruct((tiles, tile, 1), F32), saved, saved, saved),
        grid_spec=pltpu.PrefetchScalarGridSpec(
            num_scalar_prefetch=1,
            grid=(tiles,),
            in_specs=[
                pl.BlockSpec((1, tile, 1), lambda t, p: (t, 0, 0)),
                pl.BlockSpec(shard_block, own),
                pl.BlockSpec(shard_block, other),
                pl.BlockSpec(shard_block, cot), pl.BlockSpec(shard_block, cot),
                pl.BlockSpec(both.shape, lambda t, p: (0, 0, 0, 0), **fixed),
                pl.BlockSpec(down.shape, lambda t, p: (0, 0), **fixed),
            ]
            + (sums_specs if before else []),
            out_specs=sums_specs
            + [pl.BlockSpec((1, tile, 1), lambda t, p: (t, 0, 0)), saved_spec, saved_spec, saved_spec],
        ),
        input_output_aliases={8 + i: i for i in range(4)} if before else {},
        compiler_params=pltpu.CompilerParams(
            dimension_semantics=("arbitrary",), vmem_limit_bytes=60 << 20
        ),
        name=name,
    )(place, gates, *x_rows, *g_rows, both, down, *before)


def grads_body(quads, _, xo_ref, xt_ref, go_ref, gp_ref, hid_ref, dg_ref, du_ref, both_ref, down_ref,
               gate_acc, up_acc, down_acc):
    t = pl.program_id(0)
    width = down_acc.shape[1]
    hidden = down_acc.shape[0]

    @pl.when(t == 0)
    def _():
        gate_acc[...] = jnp.zeros_like(gate_acc)
        up_acc[...] = jnp.zeros_like(up_acc)
        down_acc[...] = jnp.zeros_like(down_acc)

    x = jnp.where(t >= quads, xt_ref[0], xo_ref[0]).reshape(-1, width)
    g = jnp.concatenate([go_ref[0].reshape(-1, width), gp_ref[0].reshape(-1, width)], axis=0)
    gate_acc[...] += tn(x, dg_ref[...].reshape(-1, hidden))
    up_acc[...] += tn(x, du_ref[...].reshape(-1, hidden))
    down_acc[...] += tn(hid_ref[...].reshape(-1, hidden), g)

    @pl.when(t == pl.num_programs(0) - 1)
    def _():
        part = both_ref.shape[0]
        both_ref[:, 0] = gate_acc[...].astype(BF).reshape(part, -1, hidden)
        both_ref[:, 1] = up_acc[...].astype(BF).reshape(part, -1, hidden)
        down_ref[...] = down_acc[...].astype(BF)


def expert_grads(place, x_rows, g_rows, hid, dg, du, dp, name):
    quads, shards, rows, width = x_rows[0].shape
    batches = shards // 2
    tiles, tile, hidden = hid.shape

    saved = pl.BlockSpec((2, tile, hidden), lambda t, p: (t, 0, 0))

    def own(t, p):
        return (jnp.minimum(t, quads - 1), 0, 0, 0)

    def other(t, p):
        return (jnp.maximum(t - quads, 0), 0, 0, 0)

    def cot(t, p):
        return (p[t], 0, 0, 0)

    g_block = (1, batches, rows, width)
    return pl.pallas_call(
        functools.partial(grads_body, quads),
        out_shape=(
            jax.ShapeDtypeStruct((dp, 2, width // dp, hidden), BF),
            jax.ShapeDtypeStruct((hidden, width), BF),
        ),
        grid_spec=pltpu.PrefetchScalarGridSpec(
            num_scalar_prefetch=1,
            grid=(tiles // 2,),
            in_specs=[
                pl.BlockSpec((1, shards, rows, width), own),
                pl.BlockSpec((1, shards, rows, width), other),
                pl.BlockSpec(g_block, cot), pl.BlockSpec(g_block, cot),
                saved, saved, saved,
            ],
            out_specs=[
                pl.BlockSpec((dp, 2, width // dp, hidden), lambda t, p: (0, 0, 0, 0)),
                pl.BlockSpec((hidden, width), lambda t, p: (0, 0)),
            ],
            scratch_shapes=[pltpu.VMEM((width, hidden), F32), pltpu.VMEM((width, hidden), F32),
                            pltpu.VMEM((hidden, width), F32)],
        ),
        compiler_params=pltpu.CompilerParams(
            dimension_semantics=("arbitrary",), vmem_limit_bytes=60 << 20
        ),
        name=name,
    )(place, *x_rows, *g_rows, hid, dg, du)


def finish_body(lanes, *refs):
    gate_ref, up_ref = refs[-2:]
    for e, ref in enumerate(refs[:-2]):
        for kind, out_ref in enumerate((gate_ref, up_ref)):
            hidden = ref.shape[3]
            for h in range(2):
                total = ref[h * lanes, kind].astype(F32)
                for l in range(1, lanes):
                    total = total + ref[h * lanes + l, kind].astype(F32)
                out_ref[e, :, h * hidden : (h + 1) * hidden] = total


def finish_grads(parts):
    planes, _, depth, hidden = parts[0].shape
    step = 128
    shape = jax.ShapeDtypeStruct((len(parts), depth, 2 * hidden), F32)
    out_spec = pl.BlockSpec((len(parts), step, 2 * hidden), lambda i: (0, i, 0))
    return pl.pallas_call(
        functools.partial(finish_body, planes // 2),
        out_shape=(shape, shape),
        grid=(depth // step,),
        in_specs=[pl.BlockSpec((planes, 2, step, hidden), lambda i: (0, 0, i, 0))] * len(parts),
        out_specs=(out_spec, out_spec),
        name="finish_gradients",
    )(*parts)


def scatter_all(pairs, partner, name, number, extra=()):
    if pairs[0][0].shape[0] == 4:
        return scatter_rows(pairs, partner, name, number, extra)
    total = pairs[0][0].shape[1]
    count = total // 2 if partner else total
    sums = [
        jnp.concatenate(
            [
                scatter_rows([(own[:, m::count], other[:, m::count])], partner, name, number)[0]
                for m in range(count)
            ]
        )
        for own, other in pairs
    ]
    if not extra:
        return sums
    blocks, down = extra
    lanes, lane = lax.axis_size("lane"), lax.axis_index("lane")
    down = down.reshape(down.shape[0], lanes, -1, down.shape[2]).swapaxes(0, 1)
    moved = [
        lax.ppermute(
            lax.dynamic_index_in_dim(down, lane ^ d, 0, keepdims=False),
            "lane", [(i, i ^ d) for i in range(lanes)],
        )
        for d in range(1, lanes)
    ]
    return sums + [exchange(blocks, DP), jnp.stack(moved)]


def on_device(
    tokens,
    cotangent,
    routes,
    lengths,
    block_order,
    w_query,
    w_key,
    w_value,
    w_out,
    w_router,
    w_gate,
    w_up,
    w_down,
    attn_gain,
    mlp_gain,
    query_gain,
    key_gain,
):
    batches, _, rows, width = tokens.shape
    dp_size = lax.axis_size(DP)
    ctx_size = lax.axis_size(CTX)
    quads = lax.axis_size("quad")
    lanes = lax.axis_size("lane")
    slot_len = rows * ctx_size
    block_rows = rows // 2
    head_width = width // ctx_size
    heads = head_width // HEAD
    shard = w_query.shape[0]
    expert_count = w_router.shape[1]
    local_experts = w_gate.shape[0]
    hidden_units = w_gate.shape[2]
    hidden_half = hidden_units // 2
    depth_part = w_gate.shape[1]
    factor = 1.0 / math.sqrt(HEAD)
    pair = lax.axis_index("pair")

    qkv = jnp.stack([w_query, w_key, w_value], axis=1).reshape(shard, 3, ctx_size, head_width)
    qkv = qkv.transpose(2, 0, 1, 3).reshape(ctx_size, shard, 3 * head_width)
    small = jnp.concatenate(
        [attn_gain, mlp_gain, query_gain, key_gain, w_router.reshape(shard * expert_count)]
    )
    grad_low = cotangent[:, 0]
    tok_own, tok_other, qkv_w, small, out_w = start_gather(
        tokens[:, 0], qkv, small.reshape(1, -1), w_out
    )
    token_rows = (tok_own, tok_other)
    qkv_w = qkv_w.reshape(width, 3 * head_width)
    out_w = out_w.reshape(width, width)
    small = small.reshape(dp_size * ctx_size, -1)
    gain_attn = small[:, :shard].reshape(width).astype(F32)
    gain_mlp = small[:, shard : 2 * shard].reshape(width).astype(F32)
    gain_query = small[:, 2 * shard : 3 * shard].reshape(ctx_size, head_width)
    gain_key = small[:, 3 * shard : 4 * shard].reshape(ctx_size, head_width)
    router_w = small[:, 4 * shard :].reshape(width, expert_count)
    here = lax.axis_index(CTX)
    gain_query = lax.dynamic_index_in_dim(gain_query, here, 0, keepdims=False).astype(F32)
    gain_key = lax.dynamic_index_in_dim(gain_key, here, 0, keepdims=False).astype(F32)

    w_gate, w_up, w_down, crossing, qkv_w = lax.optimization_barrier(
        (w_gate, w_up, w_down, grad_low, qkv_w)
    )
    halves = [
        jnp.stack(
            [
                jnp.stack([w_gate[e, :, part], w_up[e, :, part]])
                for part in (slice(0, hidden_half), slice(hidden_half, hidden_units))
            ]
        )
        for e in range(local_experts)
    ]
    halves = [jnp.repeat(part, lanes, axis=0) for part in halves]
    next_w = exchange(halves[0], DP)
    down_parts = lane_parts(w_down)
    g_rows = [
        lax.all_gather(part, CTX, axis=0, tiled=False)
        for part in (crossing, swap(crossing, "half"))
    ]

    def places_of(device):
        stored = device * rows + jnp.arange(rows, dtype=jnp.int32)
        match_marks = (stored // block_rows)[:, None] == jnp.arange(
            block_order.shape[0], dtype=jnp.int32
        )[None, :]
        first_place = jnp.sum(jnp.where(match_marks, block_order[None, :], 0), axis=1)
        return first_place * block_rows + stored % block_rows

    places = jnp.concatenate(
        [
            places_of((lax.axis_index("quad") ^ k) * 2 + (pair ^ other))
            for other in range(2)
            for k in range(quads)
        ]
    )
    cosine, sine = angles(places, HEAD)
    expert_range = jnp.arange(expert_count, dtype=jnp.int32)

    inputs = tokens[:, 0].astype(F32)
    attn_root = inv_rms(inputs)
    act = []
    for part in token_rows:
        values = part.astype(F32)
        act.append((values * inv_rms(values) * gain_attn).astype(BF))
    pre = [
        dot("td,de->te", part.reshape(-1, width), qkv_w).reshape(quads, batches, rows, -1)
        for part in act
    ]
    pre = jnp.stack(pre)

    squares = jnp.stack(
        [
            jnp.sum(part * part, axis=-1)
            for part in (pre[..., :head_width], pre[..., head_width : 2 * head_width])
        ],
        axis=2,
    )
    squares = sum_ctx(squares.reshape(2 * quads, 2 * batches, rows), "sum_squares", 6)
    roots = lax.rsqrt(squares.reshape(2 * quads, 2, batches, rows) / width + EPSILON)

    saved = []
    attended_all = []
    for m in range(batches):
        pre_m = pre[:, :, m].reshape(slot_len, 3 * head_width)
        query_pre = pre_m[:, :head_width]
        key_pre = pre_m[:, head_width : 2 * head_width]
        value = pre_m[:, 2 * head_width :].astype(BF).reshape(slot_len, heads, HEAD)
        query_root = roots[:, 0, m].reshape(slot_len, 1)
        key_root = roots[:, 1, m].reshape(slot_len, 1)
        query = rotate(
            (query_pre * query_root * gain_query).reshape(slot_len, heads, HEAD), cosine, sine
        ).astype(BF)
        key = rotate(
            (key_pre * key_root * gain_key).reshape(slot_len, heads, HEAD), cosine, sine
        ).astype(BF)
        allowed = (places[None, :] <= places[:, None]) & (places[None, :] < lengths[m, 0])
        scores = dot("qhd,khd->hqk", query, key) * factor
        scores = jnp.where(allowed[None], scores, MASKED)
        expo = jnp.exp(scores - jnp.max(scores, axis=-1, keepdims=True))
        probs = expo / jnp.sum(expo, axis=-1, keepdims=True)
        probs_low = probs.astype(BF)
        attended = dot("hqk,khd->qhd", probs_low, value).astype(BF)
        attended_all.append(attended.reshape(2 * quads, rows, head_width))
        saved.append(
            dict(
                query_pre=query_pre, key_pre=key_pre, query_root=query_root, key_root=key_root,
                query=query, key=key, value=value, probs=probs, probs_low=probs_low,
            )
        )
    attended = jnp.stack(attended_all, axis=1)[None]
    attended = exchange_rows(attended, "inward", "attended_to_rows", 7)[0]
    attended = attended.transpose(1, 2, 0, 3).reshape(batches, rows, width)
    x_mid = inputs + dot("mtd,de->mte", attended, out_w)
    mlp_root = inv_rms(x_mid)
    mixed_in = (x_mid * mlp_root * gain_mlp).astype(BF)
    router = jax.nn.softmax(dot("mtd,de->mte", mixed_in, router_w), axis=-1)
    routed = jnp.any(routes[:, 0, :, :, None] == expert_range, axis=2).astype(F32)
    gates = (router * routed).transpose(2, 0, 1).reshape(ctx_size, local_experts, batches, rows)
    gates = exchange_rows(gates, "outward", "gates_to_experts", 8, 2)
    gates = gates.transpose(1, 0, 3, 4, 2).reshape(4 * quads, batches * rows, local_experts)
    gates, mixed_rows = lax.optimization_barrier((gates, mixed_in))
    x_rows = gather_rows([mixed_rows], (True,), "gather_mixed", 2)[0]
    number = jnp.arange(2 * quads, dtype=jnp.int32)
    place = (lax.axis_index("quad") ^ (number % quads)) * 2 + (pair ^ (number // quads))
    x_rows, next_w, down_parts, halves, gates = lax.optimization_barrier(
        (x_rows, next_w, down_parts, halves, gates)
    )
    down_w = gather_lane(w_down, down_parts).swapaxes(0, 1)
    down_w = down_w.reshape(local_experts, hidden_half, width)

    sums = ()
    d_gates, grads_both, grads_down = [], [], []
    for e in range(local_experts):
        both_w = next_w
        if e < local_experts - 1:
            next_w = exchange(halves[e + 1], DP)
        *sums, d_gate, hid, d_gate_pre, d_up_pre = expert(
            place, gates[..., e : e + 1], x_rows, g_rows, both_w, down_w[e], tuple(sums),
            f"expert_{e}",
        )
        d_gates.append(d_gate)
        grad_both, grad_down = expert_grads(
            place, x_rows, g_rows, hid, d_gate_pre, d_up_pre, dp_size, f"expert_grads_{e}"
        )
        sums[0], grad_both, next_w = lax.optimization_barrier((sums[0], grad_both, next_w))
        grads_both.append(exchange(grad_both, DP) if e < local_experts - 1 else grad_both)
        grads_down.append(grad_down)
    moe_own, moe_other, d_own, d_other = sums
    d_own, grads_both, grads_down = lax.optimization_barrier((d_own, grads_both, grads_down))
    grads_down = jnp.stack(grads_down)
    d_mixed, moe_sum, last_both, down_others = scatter_all(
        [(d_own, d_other), (moe_own, moe_other)], True, "scatter_experts", 3,
        (grads_both[-1], grads_down),
    )
    grads_both[-1] = last_both
    d_gates = jnp.concatenate(d_gates, axis=-1)
    d_gates = d_gates.reshape(2 * quads, 2, batches, rows, local_experts)
    d_gates = d_gates.transpose(1, 0, 4, 2, 3)
    d_gates, d_mixed = lax.optimization_barrier((d_gates, d_mixed))
    d_router = exchange_rows(d_gates, "inward", "gate_gradients", 9, 2)
    d_router = jnp.sum(d_router, axis=0).reshape(expert_count, batches, rows)
    d_router = d_router.transpose(1, 2, 0) * routed
    d_logits = (
        router * (d_router - jnp.sum(router * d_router, axis=-1, keepdims=True))
    ).astype(BF)
    d_mixed = d_mixed + dot("mte,de->mtd", d_logits, router_w)

    def norm_back_all(values, root, gain, grad):
        d_values, d_gain = norm_back(values, root, gain, grad)
        return d_values, jnp.sum(d_gain, axis=0)

    d_mid, part_mlp_gain = norm_back_all(x_mid, mlp_root, gain_mlp, d_mixed)
    d_mid = d_mid + grad_low.astype(F32)
    d_att_out = d_mid.astype(BF)
    grad_out = dot("mtd,mte->de", attended, d_att_out).astype(BF)
    d_attended = dot("mte,de->mtd", d_att_out, out_w).astype(BF)
    d_attended, grad_out = lax.optimization_barrier((d_attended, grad_out))
    grad_out = lax.psum_scatter(grad_out, ALL, scatter_dimension=0, tiled=True).astype(F32)
    d_attended = d_attended.reshape(batches, rows, ctx_size, head_width).transpose(2, 0, 1, 3)
    d_attended = exchange_rows(d_attended, "outward", "attended_gradients", 10)[0]
    part_query_gain = part_key_gain = 0.0
    parts = []
    inners = []
    for m in range(batches):
        s = saved[m]
        d_att = d_attended[:, m].reshape(slot_len, heads, HEAD)
        probs, query, key = s["probs"], s["query"], s["key"]
        d_probs = dot("qhd,khd->hqk", d_att, s["value"])
        inner = jnp.sum(probs * d_probs, axis=-1, keepdims=True)
        d_scores = (probs * (d_probs - inner)).astype(BF)
        d_query = dot("hqk,khd->qhd", d_scores, key) * factor
        d_key = dot("hqk,qhd->khd", d_scores, query) * factor
        d_value = dot("hqk,qhd->khd", s["probs_low"], d_att)
        d_query = rotate_back(d_query, cosine, sine).reshape(slot_len, head_width)
        d_key = rotate_back(d_key, cosine, sine).reshape(slot_len, head_width)
        parts.append((d_query, d_key, d_value))
        inners += [
            jnp.sum(d_query * gain_query * s["query_pre"], axis=1).reshape(-1, rows),
            jnp.sum(d_key * gain_key * s["key_pre"], axis=1).reshape(-1, rows),
        ]
    inners = sum_ctx(jnp.stack(inners, axis=1), "sum_inner", 11) / width
    d_pre_all = []
    for m in range(batches):
        s = saved[m]
        d_query, d_key, d_value = parts[m]
        query_pre, key_pre = s["query_pre"], s["key_pre"]
        query_root, key_root = s["query_root"], s["key_root"]
        query_inner = inners[:, 2 * m].reshape(slot_len, 1)
        key_inner = inners[:, 2 * m + 1].reshape(slot_len, 1)
        d_query_pre = query_root * (d_query * gain_query) - query_pre * query_root**3 * query_inner
        d_key_pre = key_root * (d_key * gain_key) - key_pre * key_root**3 * key_inner
        part_query_gain = part_query_gain + jnp.sum(d_query * query_pre * query_root, axis=0)
        part_key_gain = part_key_gain + jnp.sum(d_key * key_pre * key_root, axis=0)
        d_pre = jnp.concatenate(
            [
                d_query_pre.astype(BF),
                d_key_pre.astype(BF),
                d_value.reshape(slot_len, head_width).astype(BF),
            ],
            axis=1,
        )
        d_pre_all.append(d_pre.reshape(2, quads, rows, 3 * head_width))
    d_pre = jnp.stack(d_pre_all, axis=2).reshape(2, -1, 3 * head_width)
    d_act = [
        dot("te,de->td", d_pre[i], qkv_w).astype(BF).reshape(quads, batches, rows, width)
        for i in range(2)
    ]
    d_act = scatter_all([(d_act[0], d_act[1])], False, "scatter_act", 4)[0]
    d_inputs, part_attn_gain = norm_back_all(inputs, attn_root, gain_attn, d_act)
    mixed = (x_mid + moe_sum).astype(BF)

    grad_gate, grad_up = finish_grads(grads_both)
    grads_down = grads_down.reshape(local_experts, lanes, -1, width)
    grad_down = lax.dynamic_index_in_dim(grads_down, lax.axis_index("lane"), 1, keepdims=False)
    grad_down = grad_down.astype(F32) + jnp.sum(down_others.astype(F32), axis=0)

    acts = [part.reshape(-1, width) for part in act]
    grad_qkv = sum(dot("td,te->de", x, y) for x, y in zip(acts, d_pre)).astype(BF)
    grad_qkv, grad_out = lax.optimization_barrier((grad_qkv, grad_out))
    grad_qkv = lax.psum_scatter(grad_qkv, DP, scatter_dimension=0, tiled=True)
    grad_qkv = grad_qkv.reshape(ctx_size, shard, 3 * head_width)
    grad_qkv = exchange_rows(grad_qkv, "ctx", "qkv_gradients", 14).astype(F32)
    grad_qkv = grad_qkv.reshape(ctx_size, shard, 3, head_width).transpose(2, 1, 0, 3)
    grad_qkv = grad_qkv.reshape(3, shard, width)

    grad_router = dot("mtd,mte->de", mixed_in, d_logits)
    columns = jnp.arange(ctx_size, dtype=jnp.int32)[:, None] == here

    def placed(part):
        return jnp.where(columns, part[None, :], 0.0).reshape(width)

    gains = jnp.stack(
        [part_attn_gain, part_mlp_gain, placed(part_query_gain), placed(part_key_gain)]
    )
    gains = gains.reshape(4, dp_size, ctx_size, shard).transpose(1, 2, 0, 3)
    packed = jnp.concatenate(
        [
            gains.reshape(dp_size * ctx_size, 1, 4 * shard),
            grad_router.reshape(dp_size * ctx_size, 1, shard * expert_count),
        ],
        axis=2,
    )
    packed = reduce_small(packed)
    return (
        mixed[:, None],
        (d_inputs + d_mid)[:, None],
        grad_qkv[0],
        grad_qkv[1],
        grad_qkv[2],
        grad_out,
        packed[4 * shard :].reshape(shard, expert_count),
        grad_gate,
        grad_up,
        grad_down,
        packed[:shard],
        packed[shard : 2 * shard],
        packed[2 * shard : 3 * shard],
        packed[3 * shard : 4 * shard],
    )


def solution(mesh):
    dp_size, ctx_size = mesh.shape["dp"], mesh.shape["ctx"]
    grid = Mesh(mesh.devices.reshape(2, dp_size // 2, ctx_size // 2, 2), ALL)
    rows = P(None, DP, CTX, None)
    dense = P(ALL, None)
    expert = P(CTX, DP, None)
    vector = P(ALL)
    return jax.shard_map(
        on_device,
        mesh=grid,
        in_specs=(rows, rows, rows, P(None, DP), P())
        + (dense,) * 5
        + (expert,) * 3
        + (vector,) * 4,
        out_specs=(rows, rows) + (dense,) * 5 + (expert,) * 3 + (vector,) * 4,
        check_vma=False,
    )
```

```python
import functools
import math

import jax
import jax.numpy as jnp
from jax import lax
from jax.experimental import pallas as pl
from jax.experimental.pallas import tpu as pltpu
from jax.sharding import Mesh
from jax.sharding import PartitionSpec as P

HEAD = 128
EPSILON = 1e-05
ROPE_BASE = 10000.0
MASKED = -1e30
BF = jnp.bfloat16
F32 = jnp.float32
DP = ("half", "lane")
CTX = ("quad", "pair")
ALL = DP + CTX
MESH = pl.DeviceIdType.MESH


def dot(spec, left, right):
    return jnp.einsum(spec, left, right, preferred_element_type=F32)


def inv_rms(values):
    return lax.rsqrt(jnp.mean(values * values, axis=-1, keepdims=True) + EPSILON)


def norm_back(values, inv_root, gain_vec, grad_in):
    weighted = grad_in * gain_vec
    inner = jnp.mean(weighted * values, axis=-1, keepdims=True)
    grad_values = inv_root * weighted - values * (inv_root * inv_root * inv_root) * inner
    return (grad_values, jnp.sum(grad_in * values * inv_root, axis=0))


def angles(places, head_width):
    index = jnp.arange(head_width // 2, dtype=F32)
    freqs = jnp.power(ROPE_BASE, -2.0 * index / head_width)
    turning = places.astype(F32)[:, None] * freqs[None, :]
    turning = jnp.concatenate([turning, turning], axis=1)
    return (jnp.cos(turning)[:, None, :], jnp.sin(turning)[:, None, :])


def swap(values, axis):
    return lax.ppermute(values, axis, [(0, 1), (1, 0)])


def exchange(blocks, axes):
    return lax.all_to_all(blocks, axes, split_axis=0, concat_axis=0, tiled=True)


def lane_parts(values):
    if lax.axis_size("lane") == 2:
        return swap(values, "lane")
    return lax.all_gather(values, "lane", axis=0, tiled=False)


def gather_lane(values, parts):
    if lax.axis_size("lane") == 2:
        first = lax.axis_index("lane") == 0
        return jnp.stack([jnp.where(first, values, parts), jnp.where(first, parts, values)])
    return parts


def reduce_small(values):
    return jnp.sum(exchange_rows(values, "all", "small_gradients", 15), axis=(0, 1))


def toggled(index, bits):
    step = 1
    while step <= bits:
        if bits & step:
            index = index + step - 2 * step * ((index // step) % 2)
        step *= 2
    return index


def greet(peers):
    barrier = pltpu.get_barrier_semaphore()
    for peer in peers:
        pl.semaphore_signal(barrier, inc=1, device_id=peer, device_id_type=MESH)
    pl.semaphore_wait(barrier, len(peers))


class Mover:
    def __init__(self, send, recv, local):
        self.send, self.recv, self.local = send, recv, local
        self.number, self.local_number = 0, 0
        self.sent, self.kept = [], []

    def copy(self, src, dst, device):
        i = self.number
        self.number += 1
        return pltpu.make_async_remote_copy(
            src_ref=src, dst_ref=dst, send_sem=self.send.at[i], recv_sem=self.recv.at[i],
            device_id=device, device_id_type=MESH,
        )

    def go(self, *copies):
        for c in copies:
            c.start()
            self.sent.append(c)

    def keep(self, src, dst):
        c = pltpu.make_async_copy(src, dst, self.local.at[self.local_number])
        self.local_number += 1
        c.start()
        self.kept.append(c)
        return c

    def finish(self):
        for c in self.sent:
            c.wait_send()
        for c in self.kept:
            c.wait()


class Spread:
    def __init__(self, mover, quads, src, slot):
        self.mover, self.quads = mover, quads
        quad = lax.axis_index("quad")
        to_quad = [{"quad": toggled(quad, k)} for k in range(quads)]
        sibling = {"pair": 1 - lax.axis_index("pair")}
        rows = src.shape[0]
        halves = (("a", pl.ds(0, rows // 2)), ("b", pl.ds(rows // 2, rows // 2)))
        p = {"o0": mover.copy(src, slot(1, 0, 0), sibling)}
        if quads == 4:
            for k in (1, 2):
                for name, part in halves:
                    p[f"s{k}{name}"] = mover.copy(
                        src.at[part], slot(0, k, 0).at[part], to_quad[k]
                    )
            for k, (name, part) in zip((1, 2), halves):
                p[f"f3{name}"] = mover.copy(
                    slot(0, k, k).at[part], slot(0, 3, k).at[part], to_quad[3 - k]
                )
            for k in (1, 2, 3):
                for name, part in halves:
                    p[f"o{k}{name}"] = mover.copy(
                        slot(0, k, k).at[part], slot(1, k, k).at[part], sibling
                    )
        else:
            for k in range(1, quads):
                p[f"s{k}"] = mover.copy(src, slot(0, k, 0), to_quad[k])
                p[f"o{k}"] = mover.copy(slot(0, k, k), slot(1, k, k), sibling)
        self.copies = p

    @staticmethod
    def count(quads):
        return 13 if quads == 4 else 2 * quads - 1

    def begin(self):
        names = [f"s{k}" for k in range(1, self.quads)]
        if self.quads == 4:
            names = ["s1a", "s2b", "s1b", "s2a"]
        self.mover.go(*[self.copies[name] for name in names + ["o0"]])

    def forward(self):
        p = self.copies
        steps = [(f"s{k}", (f"o{k}",)) for k in range(1, self.quads)]
        if self.quads == 4:
            steps = [
                ("s1a", ("f3a", "o1a")), ("s2b", ("f3b", "o2b")), ("s1b", ("o1b",)),
                ("s2a", ("o2a",)), ("f3a", ("o3a",)), ("f3b", ("o3b",)),
            ]
        for name, then in steps:
            p[name].wait_recv()
            self.mover.go(*[p[t] for t in then])

    def arrive(self):
        for name, c in self.copies.items():
            if name[0] == "o":
                c.wait_recv()


def relative_slots(own_ref, other_ref, s):
    return lambda core, kr, km: (other_ref if core else own_ref).at[kr, s]


def ctx_peers(quads):
    return [ctx_at(quads, n)[0] for n in range(1, 2 * quads)]


def planes_of(lanes):
    half, lane = lax.axis_index("half"), lax.axis_index("lane")
    result = []
    for n in range(1, 2 * lanes):
        h, l = toggled(half, n // lanes), toggled(lane, n % lanes)
        result.append(({"half": h, "lane": l}, h * lanes + l))
    return half * lanes + lane, result


def gather_body(quads, partners, *refs):
    inputs = refs[: len(partners)]
    refs = refs[len(partners) :]
    outputs = [(refs[2 * i], refs[2 * i + 1]) for i in range(len(partners))]
    refs = refs[2 * len(partners) :]
    keeps = {}
    for i, partner in enumerate(partners):
        if partner != "own":
            keeps[i], refs = refs[0], refs[1:]
    local, send, recv = refs
    mover = Mover(send, recv, local)
    across = {"half": 1 - lax.axis_index("half")}
    quad = lax.axis_index("quad")
    peers = [{"quad": toggled(quad, k)} for k in range(1, quads)]
    peers.append({"pair": 1 - lax.axis_index("pair")})
    greet(peers + ([across] if keeps else []))

    def add(sources, i, offset):
        plans = []
        for s, src in enumerate(sources):
            p = Spread(mover, quads, src, relative_slots(*outputs[i], offset + s))
            p.begin()
            plans.append(p)
            mover.keep(src, outputs[i][0].at[0, offset + s])
        return plans

    crossing = {}
    for i, keep in keeps.items():
        crossing[i] = [
            mover.copy(inputs[i].at[s], keep.at[s], across) for s in range(inputs[i].shape[0])
        ]
        mover.go(*crossing[i])
    plans = []
    for i, ref in enumerate(inputs):
        if partners[i] == "partner":
            continue
        plans += add([ref.at[s] for s in range(ref.shape[0])], i, 0)
    for p in plans:
        p.forward()
    late = []
    for i, keep in keeps.items():
        for c in crossing[i]:
            c.wait_recv()
        offset = keep.shape[0] if partners[i] == "both" else 0
        late += add([keep.at[s] for s in range(keep.shape[0])], i, offset)
    for p in late:
        p.forward()
    for p in plans + late:
        p.arrive()
    mover.finish()


def gather_rows(sources, partners, name, number):
    quads = lax.axis_size("quad")
    shapes, keeps = [], []
    sems = total = 0
    for x, partner in zip(sources, partners):
        count = x.shape[0] * (2 if partner == "both" else 1)
        total += count
        sems += count * Spread.count(quads) + (x.shape[0] if partner != "own" else 0)
        shapes += [jax.ShapeDtypeStruct((quads, count) + x.shape[1:], x.dtype)] * 2
        if partner != "own":
            keeps.append(pltpu.VMEM(x.shape, x.dtype))
    out = pl.pallas_call(
        functools.partial(gather_body, quads, partners),
        out_shape=shapes,
        in_specs=[pl.BlockSpec(memory_space=pltpu.VMEM)] * len(sources),
        out_specs=[pl.BlockSpec(memory_space=pl.ANY)] * len(shapes),
        scratch_shapes=keeps
        + [
            pltpu.SemaphoreType.DMA((total,)),
            pltpu.SemaphoreType.DMA((sems,)),
            pltpu.SemaphoreType.DMA((sems,)),
        ],
        compiler_params=pltpu.CompilerParams(collective_id=number, has_side_effects=True),
        name=name,
    )(*sources)
    return [(out[2 * i], out[2 * i + 1]) for i in range(len(sources))]


def start_body(
    quads, lanes, tok_ref, qkv_ref, small_ref, wout_ref,
    tok_own, tok_other, qkv_out, small_out, wout_out, local, send, recv,
):
    mover = Mover(send, recv, local)
    half, lane = lax.axis_index("half"), lax.axis_index("lane")
    plane, here = half * lanes + lane, ctx_place()
    partner = (1 - half) * lanes + lane
    across = {"half": 1 - half}
    devices = 4 * lanes * quads
    others = [all_at(lanes, quads, n)[0] for n in range(1, devices)]
    greet(others)
    mine = mover.keep(small_ref, small_out.at[plane * 2 * quads + here])
    shared = [mover.copy(small_ref, small_out.at[plane * 2 * quads + here], d) for d in others]
    mover.go(*shared)

    def planes(src, view):
        first = mover.copy(src, view(plane), across)
        rest = [
            mover.copy(src, view(plane), {"lane": toggled(lane, d)}) for d in range(1, lanes)
        ]
        then = [
            mover.copy(view(partner), view(partner), {"lane": toggled(lane, d)})
            for d in range(1, lanes)
        ]
        mover.go(first, *rest)
        return first, rest, then

    mover.keep(wout_ref, wout_out.at[plane])
    w_first, w_rest, w_then = planes(wout_ref, lambda p: wout_out.at[p])
    kept = mover.keep(qkv_ref.at[here], qkv_out.at[plane, here])
    columns = []
    for n in range(1, 2 * quads):
        device, place = ctx_at(quads, n)
        columns.append(mover.copy(qkv_ref.at[place], qkv_out.at[plane, here], device))
    mover.go(*columns)
    tokens = []
    for s in range(tok_ref.shape[0]):
        p = Spread(mover, quads, tok_ref.at[s], relative_slots(tok_own, tok_other, s))
        p.begin()
        tokens.append(p)
        mover.keep(tok_ref.at[s], tok_own.at[0, s])
    for c in columns:
        c.wait_recv()
    kept.wait()
    mover.kept = [c for c in mover.kept if c is not kept]
    q_first, q_rest, q_then = planes(qkv_out.at[plane], lambda p: qkv_out.at[p])
    w_first.wait_recv()
    mover.go(*w_then)
    tokens[0].forward()
    q_first.wait_recv()
    mover.go(*q_then)
    for p in tokens[1:]:
        p.forward()
    for p in tokens:
        p.arrive()
    for c in shared + q_rest + q_then + w_rest + w_then:
        c.wait_recv()
    mover.finish()


def start_gather(tokens, qkv, small, w_out):
    quads, lanes = lax.axis_size("quad"), lax.axis_size("lane")
    count = tokens.shape[0]
    planes, devices = 2 * lanes, 4 * lanes * quads

    def like(lead, x, dtype=BF):
        return jax.ShapeDtypeStruct(lead + x.shape, dtype)

    sems = (devices - 1) + 2 * (2 * lanes - 1) + (2 * quads - 1)
    sems += Spread.count(quads) * count
    return pl.pallas_call(
        functools.partial(start_body, quads, lanes),
        out_shape=[like((quads,), tokens)] * 2
        + [like((planes,), qkv), like((devices,), small), like((planes,), w_out)],
        in_specs=[pl.BlockSpec(memory_space=pltpu.VMEM)] * 4,
        out_specs=[pl.BlockSpec(memory_space=pl.ANY)] * 5,
        scratch_shapes=[
            pltpu.SemaphoreType.DMA((3 + count,)),
            pltpu.SemaphoreType.DMA((sems,)),
            pltpu.SemaphoreType.DMA((sems,)),
        ],
        compiler_params=pltpu.CompilerParams(collective_id=0, has_side_effects=True),
        name="start_gather",
    )(tokens, qkv, small, w_out)


def add_rows(out_ref, *refs):
    rows = out_ref.shape[0]
    step = 16

    @pl.loop(0, rows // step)
    def _(i):
        part = pl.ds(pl.multiple_of(i * step, step), step)
        total = refs[0][part].astype(F32)
        for ref in refs[1:]:
            total = total + ref[part].astype(F32)
        out_ref[part] = total.astype(out_ref.dtype)


def scatter_body(quads, lanes, partners, count, extra, *refs):
    kinds = len(partners)
    inputs = [(refs[2 * i], refs[2 * i + 1]) for i in range(kinds)]
    refs = refs[2 * kinds :]
    if extra:
        blocks_ref, *refs = refs
    outputs, refs = refs[:kinds], refs[kinds:]
    if extra:
        blocks_out, held, *refs = refs
    mine, theirs, relay, arrived, *rest = refs
    if any(partners):
        summed, back, *rest = rest
    local, send, recv = rest
    mover = Mover(send, recv, local)
    mover.local_number = local.shape[0] - 2
    rows = inputs[0][0].shape[2]
    first, second = pl.ds(0, rows // 2), pl.ds(rows // 2, rows // 2)
    quad = lax.axis_index("quad")
    to_quad = [{"quad": toggled(quad, k)} for k in range(quads)]
    sibling = {"pair": 1 - lax.axis_index("pair")}
    across = {"half": 1 - lax.axis_index("half")}
    peers = to_quad[1:] + [sibling]
    if extra:
        me, planes = planes_of(lanes)
        peers += [device for device, _ in planes]
    elif any(partners):
        peers.append(across)
    greet(peers)

    def go(src, dst, device):
        c = mover.copy(src, dst, device)
        mover.go(c)
        return c

    order = [(i, s) for i in range(kinds) if partners[i] for s in range(count, 2 * count)]
    order += [(i, s) for i in range(kinds) for s in range(count)]
    ks = [3, 1, 2, 0] if quads == 4 else list(range(quads - 1, -1, -1))
    sib, loc = {}, {}
    for n, (i, s) in enumerate(order):
        for k in ks:
            sib[n, k] = go(inputs[i][1].at[k, s], theirs.at[n, k], sibling)
            loc[n, k] = pltpu.make_async_copy(
                inputs[i][0].at[k, s], mine.at[n, k], local.at[n * quads + k]
            )
            loc[n, k].start()
    sends = {}

    def merge(n):
        for k in ks:
            sib[n, k].wait_recv()
            loc[n, k].wait()
            add_rows(mine.at[n, k], mine.at[n, k], theirs.at[n, k])
            if quads == 4:
                if k == 3:
                    sends[n, "3a"] = go(mine.at[n, 3, first], relay.at[n, 0], to_quad[2])
                    sends[n, "3b"] = go(mine.at[n, 3, second], relay.at[n, 1], to_quad[1])
                elif k == 1:
                    sends[n, "1b"] = go(mine.at[n, 1, second], arrived.at[n, 0, second], to_quad[1])
                elif k == 2:
                    sends[n, "2a"] = go(mine.at[n, 2, first], arrived.at[n, 1, first], to_quad[2])
            elif k:
                sends[n, k] = go(mine.at[n, k], arrived.at[n, k - 1], to_quad[k])

    def pass_on(n):
        if quads == 4:
            sends[n, "3a"].wait_recv()
            add_rows(mine.at[n, 1, first], mine.at[n, 1, first], relay.at[n, 0])
            sends[n, "1a"] = go(mine.at[n, 1, first], arrived.at[n, 0, first], to_quad[1])
            sends[n, "3b"].wait_recv()
            add_rows(mine.at[n, 2, second], mine.at[n, 2, second], relay.at[n, 1])
            sends[n, "2b"] = go(mine.at[n, 2, second], arrived.at[n, 1, second], to_quad[2])

    backs = {}

    def total_of(n):
        i, s = order[n]
        for name in ("1b", "2a", "1a", "2b") if quads == 4 else range(1, quads):
            sends[n, name].wait_recv()
        parts = [mine.at[n, 0]] + [arrived.at[n, j] for j in range(arrived.shape[1])]
        if s >= count:
            slot = i * count + s - count
            add_rows(summed.at[slot], *parts)
            backs[slot] = go(summed.at[slot], back.at[slot], across)
        else:
            if partners[i]:
                backs[i * count + s].wait_recv()
                parts.append(back.at[i * count + s])
            add_rows(outputs[i].at[s], *parts)

    ahead = 2
    exchanged = []

    if extra:
        into = mover.keep(blocks_ref.at[me], held)
        for device, place in planes:
            exchanged.append(go(blocks_ref.at[place], blocks_out.at[me], device))
    for n in range(len(order) + 2 * ahead):
        if extra and n == 1:
            into.wait()
            mover.kept = [c for c in mover.kept if c is not into]
            mover.keep(held, blocks_out.at[me])
        if n < len(order):
            merge(n)
        if 0 <= n - 1 < len(order):
            pass_on(n - 1)
        if 0 <= n - 2 * ahead < len(order):
            total_of(n - 2 * ahead)
    for c in exchanged:
        c.wait_recv()
    mover.finish()


def scatter_rows(pairs, partners, name, number, extra=()):
    lanes = lax.axis_size("lane")
    quads, _, rows, width = pairs[0][0].shape
    shards = sum(own.shape[1] for own, _ in pairs)
    kinds = len(pairs)
    count = shards // sum(2 if partner else 1 for partner in partners)
    incoming = 2 if quads == 4 else quads - 1
    sems = shards * (quads + (6 if quads == 4 else quads - 1)) + count * sum(partners)

    def buf(*lead):
        return pltpu.VMEM(lead + (rows, width), BF)

    scratch = [buf(shards, quads), buf(shards, quads)]
    scratch += [pltpu.VMEM((shards, 2, rows // 2, width), BF), buf(shards, incoming)]
    if any(partners):
        scratch += [buf(kinds * count), buf(kinds * count)]
    shapes = [jax.ShapeDtypeStruct((count, rows, width), F32)] * kinds
    specs = [pl.BlockSpec(memory_space=pltpu.VMEM)] * kinds
    anywhere = pl.BlockSpec(memory_space=pl.ANY)
    if extra:
        blocks = extra[0]
        shapes = shapes + [jax.ShapeDtypeStruct(blocks.shape, BF)]
        specs = specs + [anywhere]
        scratch = [pltpu.VMEM(blocks.shape[1:], BF)] + scratch
        sems += 2 * lanes - 1
    return pl.pallas_call(
        functools.partial(scatter_body, quads, lanes, partners, count, bool(extra)),
        out_shape=shapes,
        in_specs=[anywhere] * (2 * kinds + len(extra)),
        out_specs=specs,
        scratch_shapes=scratch
        + [
            pltpu.SemaphoreType.DMA((shards * quads + 2,)),
            pltpu.SemaphoreType.DMA((sems,)),
            pltpu.SemaphoreType.DMA((sems,)),
        ],
        compiler_params=pltpu.CompilerParams(
            collective_id=number, has_side_effects=True, vmem_limit_bytes=60 << 20
        ),
        name=name,
    )(*[ref for pair in pairs for ref in pair], *extra)


def ctx_place():
    return lax.axis_index("quad") * 2 + lax.axis_index("pair")


def ctx_at(quads, number):
    core, distance = number // quads, number % quads
    quad = toggled(lax.axis_index("quad"), distance)
    pair = toggled(lax.axis_index("pair"), core)
    return {"quad": quad, "pair": pair}, quad * 2 + pair


def all_at(lanes, quads, number):
    half = toggled(lax.axis_index("half"), number // (lanes * 2 * quads))
    lane = toggled(lax.axis_index("lane"), number // (2 * quads) % lanes)
    device, place = ctx_at(quads, number % (2 * quads))
    return {"half": half, "lane": lane, **device}, (half * lanes + lane) * 2 * quads + place


def exchange_body(mode, lanes, quads, halves, x_ref, out_ref, local, send, recv):
    copies = []
    peers = []
    if mode in ("shared", "all"):
        me = (lax.axis_index("half") * lanes + lax.axis_index("lane")) * 2 * quads + ctx_place()
        for n in range(2 * lanes * 2 * quads):
            device, place = all_at(lanes, quads, n)
            copies.append((x_ref if mode == "shared" else x_ref.at[place], out_ref.at[me], device))
    else:
        for h in range(halves):
            for n in range(2 * quads):
                device, place = ctx_at(quads, n)
                if halves == 2:
                    device = {"half": toggled(lax.axis_index("half"), h), **device}
                if mode == "inward":
                    pair = (x_ref.at[h, n], out_ref.at[h, ctx_place()])
                elif mode == "outward":
                    pair = (x_ref.at[place], out_ref.at[h, n])
                else:
                    pair = (x_ref.at[place], out_ref.at[ctx_place()])
                copies.append(pair + (device,))
    own = pltpu.make_async_copy(copies[0][0], copies[0][1], local)
    own.start()
    greet([device for _, _, device in copies[1:]])
    started = []
    for i, (src, dst, device) in enumerate(copies[1:]):
        c = pltpu.make_async_remote_copy(
            src_ref=src, dst_ref=dst, send_sem=send.at[i], recv_sem=recv.at[i],
            device_id=device, device_id_type=MESH,
        )
        c.start()
        started.append(c)
    own.wait()
    for c in started:
        c.wait_recv()
    for c in started:
        c.wait_send()


def exchange_rows(x, mode, name, number, halves=1):
    quads, lanes = lax.axis_size("quad"), lax.axis_size("lane")
    count = halves * 2 * quads - 1
    shape = x.shape
    if mode == "outward":
        shape = (halves, 2 * quads) + x.shape[1:]
    elif mode in ("shared", "all"):
        count = 4 * lanes * quads - 1
        if mode == "shared":
            shape = (count + 1,) + x.shape
    return pl.pallas_call(
        functools.partial(exchange_body, mode, lanes, quads, halves),
        out_shape=jax.ShapeDtypeStruct(shape, x.dtype),
        in_specs=[pl.BlockSpec(memory_space=pltpu.VMEM)],
        out_specs=pl.BlockSpec(memory_space=pltpu.VMEM),
        scratch_shapes=[
            pltpu.SemaphoreType.DMA,
            pltpu.SemaphoreType.DMA((count,)),
            pltpu.SemaphoreType.DMA((count,)),
        ],
        compiler_params=pltpu.CompilerParams(collective_id=number, has_side_effects=True),
        name=name,
    )(x)


def sum_body(quads, x_ref, out_ref, landed, send, recv):
    count = 2 * quads
    greet([ctx_at(quads, n)[0] for n in range(1, count)])
    started = []
    for n in range(1, count):
        c = pltpu.make_async_remote_copy(
            src_ref=x_ref, dst_ref=landed.at[n - 1], send_sem=send.at[n - 1],
            recv_sem=recv.at[n - 1], device_id=ctx_at(quads, n)[0], device_id_type=MESH,
        )
        c.start()
        started.append(c)
    for c in started:
        c.wait_recv()
    for j in range(count):
        total = x_ref[j]
        for n in range(1, count):
            total = total + landed[n - 1, j ^ n]
        out_ref[j] = total
    for c in started:
        c.wait_send()


def sum_ctx(x, name, number):
    quads = lax.axis_size("quad")
    count = 2 * quads - 1
    return pl.pallas_call(
        functools.partial(sum_body, quads),
        out_shape=jax.ShapeDtypeStruct(x.shape, x.dtype),
        in_specs=[pl.BlockSpec(memory_space=pltpu.VMEM)],
        out_specs=pl.BlockSpec(memory_space=pltpu.VMEM),
        scratch_shapes=[
            pltpu.VMEM((count,) + x.shape, x.dtype),
            pltpu.SemaphoreType.DMA((count,)),
            pltpu.SemaphoreType.DMA((count,)),
        ],
        compiler_params=pltpu.CompilerParams(collective_id=number, has_side_effects=True),
        name=name,
    )(x)


def nn(left, right):
    return lax.dot_general(left, right, (((1,), (0,)), ((), ())), preferred_element_type=F32)


def nt(left, right):
    return lax.dot_general(left, right, (((1,), (1,)), ((), ())), preferred_element_type=F32)


def tn(left, right):
    return lax.dot_general(left, right, (((0,), (0,)), ((), ())), preferred_element_type=F32)


def expert_body(quads, before, _, gate_ref, xo_ref, xt_ref, go_ref, gpo_ref, gpt_ref, both_ref,
                down_ref, *refs):
    sums = refs[:4] if before else None
    mo_ref, mt_ref, do_ref, dt_ref, dgate_ref, hid_ref, dg_ref, du_ref = refs[-8:]
    t = pl.program_id(0)
    core_other = t >= 2 * quads
    partner = t % 2 == 1
    hidden, width = down_ref.shape
    x = jnp.where(core_other, xt_ref[0], xo_ref[0]).reshape(-1, width)
    g_partner = jnp.where(core_other, gpt_ref[0], gpo_ref[0])
    g = jnp.where(partner, g_partner, go_ref[0]).reshape(-1, width)
    gate = gate_ref[0]
    wg = both_ref[:, 0].reshape(width, hidden)
    wu = both_ref[:, 1].reshape(width, hidden)
    wd = down_ref[...]
    gate_pre = nn(x, wg)
    up_pre = nn(x, wu)
    d_hidden = nt(g, wd)
    sigma = 1.0 / (1.0 + jnp.exp(-gate_pre))
    silu = gate_pre * sigma
    hid = silu * up_pre
    dgate_ref[0] = jnp.sum(hid * d_hidden, axis=1, keepdims=True)
    d_hidden = d_hidden * gate
    scaled = (hid * gate).astype(BF)
    d_gate_pre = (d_hidden * up_pre * (sigma + silu * (1.0 - sigma))).astype(BF)
    d_up_pre = (d_hidden * silu).astype(BF)
    hid_ref[0] = scaled
    dg_ref[0] = d_gate_pre
    du_ref[0] = d_up_pre
    moe = nn(scaled, wd).reshape(mo_ref.shape[1:])
    d_rows = (nt(d_gate_pre, wg) + nt(d_up_pre, wu)).reshape(mo_ref.shape[1:])
    if before:
        moe = moe + jnp.where(core_other, sums[1][0], sums[0][0]).astype(F32)
        d_rows = d_rows + jnp.where(core_other, sums[3][0], sums[2][0]).astype(F32)
    moe, d_rows = moe.astype(BF), d_rows.astype(BF)

    @pl.when(jnp.logical_not(core_other))
    def _():
        mo_ref[0] = moe
        do_ref[0] = d_rows

    @pl.when(core_other)
    def _():
        mt_ref[0] = moe
        dt_ref[0] = d_rows


def expert(place, gates, x_rows, g_rows, both, down, before, name):
    quads, shards, rows, width = x_rows[0].shape
    batches = shards // 2
    hidden = down.shape[0]
    tiles = 4 * quads
    tile = batches * rows

    def own(t, p):
        return (jnp.minimum(t, 2 * quads - 1) // 2, jnp.minimum(t, 2 * quads - 1) % 2, 0, 0)

    def other(t, p):
        u = jnp.maximum(t - 2 * quads, 0)
        return (u // 2, u % 2, 0, 0)

    def cot(t, p):
        return (p[t // 2], 0, 0, 0)

    def own_g(t, p):
        return (jnp.minimum(t // 2, quads - 1), 0, 0, 0)

    def other_g(t, p):
        return (jnp.maximum(t // 2 - quads, 0), 0, 0, 0)

    shard_block = (1, batches, rows, width)
    saved_spec = pl.BlockSpec((1, tile, hidden), lambda t, p: (t, 0, 0))
    saved = jax.ShapeDtypeStruct((tiles, tile, hidden), BF)
    rows_shape = jax.ShapeDtypeStruct(x_rows[0].shape, BF)
    fixed = dict(pipeline_mode=pl.Buffered(1))
    sums_specs = [
        pl.BlockSpec(shard_block, own), pl.BlockSpec(shard_block, other),
        pl.BlockSpec(shard_block, own), pl.BlockSpec(shard_block, other),
    ]
    return pl.pallas_call(
        functools.partial(expert_body, quads, bool(before)),
        out_shape=(rows_shape,) * 4
        + (jax.ShapeDtypeStruct((tiles, tile, 1), F32), saved, saved, saved),
        grid_spec=pltpu.PrefetchScalarGridSpec(
            num_scalar_prefetch=1,
            grid=(tiles,),
            in_specs=[
                pl.BlockSpec((1, tile, 1), lambda t, p: (t, 0, 0)),
                pl.BlockSpec(shard_block, own),
                pl.BlockSpec(shard_block, other),
                pl.BlockSpec(shard_block, cot),
                pl.BlockSpec(shard_block, own_g), pl.BlockSpec(shard_block, other_g),
                pl.BlockSpec(both.shape, lambda t, p: (0, 0, 0, 0), **fixed),
                pl.BlockSpec(down.shape, lambda t, p: (0, 0), **fixed),
            ]
            + (sums_specs if before else []),
            out_specs=sums_specs
            + [pl.BlockSpec((1, tile, 1), lambda t, p: (t, 0, 0)), saved_spec, saved_spec, saved_spec],
        ),
        input_output_aliases={9 + i: i for i in range(4)} if before else {},
        compiler_params=pltpu.CompilerParams(
            dimension_semantics=("arbitrary",), vmem_limit_bytes=60 << 20
        ),
        name=name,
    )(place, gates, *x_rows, *g_rows, both, down, *before)


def grads_body(quads, _, xo_ref, xt_ref, go_ref, gpo_ref, gpt_ref, hid_ref, dg_ref, du_ref, both_ref, down_ref,
               gate_acc, up_acc, down_acc):
    t = pl.program_id(0)
    width = down_acc.shape[1]
    hidden = down_acc.shape[0]

    @pl.when(t == 0)
    def _():
        gate_acc[...] = jnp.zeros_like(gate_acc)
        up_acc[...] = jnp.zeros_like(up_acc)
        down_acc[...] = jnp.zeros_like(down_acc)

    x = jnp.where(t >= quads, xt_ref[0], xo_ref[0]).reshape(-1, width)
    g_partner = jnp.where(t >= quads, gpt_ref[0], gpo_ref[0]).reshape(-1, width)
    g = jnp.concatenate([go_ref[0].reshape(-1, width), g_partner], axis=0)
    gate_acc[...] += tn(x, dg_ref[...].reshape(-1, hidden))
    up_acc[...] += tn(x, du_ref[...].reshape(-1, hidden))
    down_acc[...] += tn(hid_ref[...].reshape(-1, hidden), g)

    @pl.when(t == pl.num_programs(0) - 1)
    def _():
        part = both_ref.shape[0]
        both_ref[:, 0] = gate_acc[...].astype(BF).reshape(part, -1, hidden)
        both_ref[:, 1] = up_acc[...].astype(BF).reshape(part, -1, hidden)
        down_ref[...] = down_acc[...].astype(BF)


def expert_grads(place, x_rows, g_rows, hid, dg, du, dp, name):
    quads, shards, rows, width = x_rows[0].shape
    batches = shards // 2
    tiles, tile, hidden = hid.shape

    saved = pl.BlockSpec((2, tile, hidden), lambda t, p: (t, 0, 0))

    def own(t, p):
        return (jnp.minimum(t, quads - 1), 0, 0, 0)

    def other(t, p):
        return (jnp.maximum(t - quads, 0), 0, 0, 0)

    def cot(t, p):
        return (p[t], 0, 0, 0)

    g_block = (1, batches, rows, width)
    return pl.pallas_call(
        functools.partial(grads_body, quads),
        out_shape=(
            jax.ShapeDtypeStruct((dp, 2, width // dp, hidden), BF),
            jax.ShapeDtypeStruct((hidden, width), BF),
        ),
        grid_spec=pltpu.PrefetchScalarGridSpec(
            num_scalar_prefetch=1,
            grid=(tiles // 2,),
            in_specs=[
                pl.BlockSpec((1, shards, rows, width), own),
                pl.BlockSpec((1, shards, rows, width), other),
                pl.BlockSpec(g_block, cot), pl.BlockSpec(g_block, own), pl.BlockSpec(g_block, other),
                saved, saved, saved,
            ],
            out_specs=[
                pl.BlockSpec((dp, 2, width // dp, hidden), lambda t, p: (0, 0, 0, 0)),
                pl.BlockSpec((hidden, width), lambda t, p: (0, 0)),
            ],
            scratch_shapes=[pltpu.VMEM((width, hidden), F32), pltpu.VMEM((width, hidden), F32),
                            pltpu.VMEM((hidden, width), F32)],
        ),
        compiler_params=pltpu.CompilerParams(
            dimension_semantics=("arbitrary",), vmem_limit_bytes=60 << 20
        ),
        name=name,
    )(place, *x_rows, *g_rows, hid, dg, du)


def finish_body(lanes, *refs):
    gate_ref, up_ref = refs[-2:]
    for e, ref in enumerate(refs[:-2]):
        for kind, out_ref in enumerate((gate_ref, up_ref)):
            hidden = ref.shape[3]
            for h in range(2):
                total = ref[h * lanes, kind].astype(F32)
                for l in range(1, lanes):
                    total = total + ref[h * lanes + l, kind].astype(F32)
                out_ref[e, :, h * hidden : (h + 1) * hidden] = total


def finish_grads(parts):
    planes, _, depth, hidden = parts[0].shape
    step = 128
    shape = jax.ShapeDtypeStruct((len(parts), depth, 2 * hidden), F32)
    out_spec = pl.BlockSpec((len(parts), step, 2 * hidden), lambda i: (0, i, 0))
    return pl.pallas_call(
        functools.partial(finish_body, planes // 2),
        out_shape=(shape, shape),
        grid=(depth // step,),
        in_specs=[pl.BlockSpec((planes, 2, step, hidden), lambda i: (0, 0, i, 0))] * len(parts),
        out_specs=(out_spec, out_spec),
        name="finish_gradients",
    )(*parts)


def row_sums(values):
    ones = jnp.ones((8, values.shape[1]), F32)
    sums = lax.dot_general(
        ones, values, (((1,), (1,)), ((), ())), preferred_element_type=F32,
        precision=lax.Precision.HIGHEST,
    )
    return sums[:1]


def columns(values):
    turned = jnp.transpose(values)
    return jnp.concatenate([turned[:, i : i + 1] for i in range(values.shape[0])], axis=0)


def qkv_body(quads, xo_ref, xt_ref, gain_ref, w_ref, ao_ref, at_ref, pre_ref, square_ref):
    n = pl.program_id(0)
    other = n >= quads
    batches, rows, width = xo_ref.shape[1:]
    head_width = w_ref.shape[1] // 3
    x = jnp.where(other, xt_ref[0], xo_ref[0]).astype(F32).reshape(-1, width)
    root = lax.rsqrt(jnp.mean(x * x, axis=1, keepdims=True) + EPSILON)
    act = (x * root * gain_ref[...]).astype(BF)
    pre = nn(act, w_ref[...])
    pre_ref[:, 0] = pre.reshape(batches, rows, -1)
    for kind in range(2):
        part = pre[:, kind * head_width : (kind + 1) * head_width]
        sums = row_sums(part * part)
        for m in range(batches):
            i = kind * batches + m
            square_ref[0, i : i + 1] = sums[:, m * rows : (m + 1) * rows]
    act = act.reshape(batches, rows, width)

    @pl.when(jnp.logical_not(other))
    def _():
        ao_ref[0] = act

    @pl.when(other)
    def _():
        at_ref[0] = act


def own_block(quads):
    return lambda n: (jnp.minimum(n, quads - 1), 0, 0, 0)


def other_block(quads):
    return lambda n: (jnp.maximum(n - quads, 0), 0, 0, 0)


def project(token_rows, gain, weights):
    quads, batches, rows, width = token_rows[0].shape
    total = weights.shape[1]
    block = (1, batches, rows, width)
    fixed = dict(pipeline_mode=pl.Buffered(1))
    own, other = pl.BlockSpec(block, own_block(quads)), pl.BlockSpec(block, other_block(quads))
    return pl.pallas_call(
        functools.partial(qkv_body, quads),
        out_shape=(
            jax.ShapeDtypeStruct(token_rows[0].shape, BF),
            jax.ShapeDtypeStruct(token_rows[0].shape, BF),
            jax.ShapeDtypeStruct((batches, 2 * quads, rows, total), F32),
            jax.ShapeDtypeStruct((2 * quads, 2 * batches, rows), F32),
        ),
        grid=(2 * quads,),
        in_specs=[
            own, other,
            pl.BlockSpec((1, width), lambda n: (0, 0)),
            pl.BlockSpec((width, total), lambda n: (0, 0), **fixed),
        ],
        out_specs=(
            own, other,
            pl.BlockSpec((batches, 1, rows, total), lambda n: (0, n, 0, 0)),
            pl.BlockSpec((1, 2 * batches, rows), lambda n: (n, 0, 0)),
        ),
        compiler_params=pltpu.CompilerParams(vmem_limit_bytes=40 << 20),
        name="project",
    )(*token_rows, gain.reshape(1, width), weights)


def turned(values, cosine, sine):
    return values * cosine + pltpu.roll(values, HEAD // 2, 1) * sine


def turned_back(grad, cosine, sine):
    return grad * cosine - pltpu.roll(grad, HEAD // 2, 1) * sine


def head_probs(query, key, column, row, length):
    scores = nt(query, key) * (1.0 / math.sqrt(HEAD))
    scores = jnp.where((row <= column) & (row < length), scores, MASKED)
    expo = jnp.exp(scores - jnp.max(scores, axis=1, keepdims=True))
    return expo / jnp.sum(expo, axis=1, keepdims=True)


def attend_body(
    step, pre_ref, sum_ref, gain_ref, cos_ref, sin_ref, column_ref, row_ref, length_ref,
    query_ref, key_ref, value_ref, out_ref, att,
):
    m = pl.program_id(0)
    places, rows = pre_ref.shape[1:3]
    slot = places * rows
    head_width = query_ref.shape[2]
    cosine, sine = cos_ref[...], sin_ref[...]
    pre = pre_ref[0].reshape(slot, 3 * head_width)
    for kind, ref in enumerate((query_ref, key_ref)):
        root = lax.rsqrt(columns(sum_ref[0, kind]) / (head_width * places) + EPSILON)
        part = pre[:, kind * head_width : (kind + 1) * head_width] * root * gain_ref[kind]
        for h in range(head_width // HEAD):
            here = slice(h * HEAD, (h + 1) * HEAD)
            ref[0, :, here] = turned(part[:, here], cosine, sine).astype(BF)
    value_ref[0] = pre[:, 2 * head_width :].astype(BF)
    length = length_ref[m]
    row = row_ref[...]
    for h in range(head_width // HEAD):
        here = slice(h * HEAD, (h + 1) * HEAD)

        @pl.loop(0, slot // step)
        def _(i):
            part = pl.ds(pl.multiple_of(i * step, step), step)
            probs = head_probs(query_ref[0, part, here], key_ref[0, :, here], column_ref[part], row, length)
            att[part, here] = nn(probs.astype(BF), value_ref[0, :, here]).astype(BF)

    out_ref[:, 0] = att[...].reshape(places, rows, head_width)


def attend(pre, sums, gains, cosine, sine, column, row, lengths):
    batches, places, rows, total = pre.shape
    head_width, slot = total // 3, places * rows
    saved = jax.ShapeDtypeStruct((batches, slot, head_width), BF)
    saved_spec = pl.BlockSpec((1, slot, head_width), lambda m: (m, 0, 0))
    return pl.pallas_call(
        functools.partial(attend_body, 256),
        out_shape=(saved,) * 3
        + (jax.ShapeDtypeStruct((places, batches, rows, head_width), BF),),
        grid=(batches,),
        in_specs=[
            pl.BlockSpec((1,) + pre.shape[1:], lambda m: (m, 0, 0, 0)),
            pl.BlockSpec((1,) + sums.shape[1:], lambda m: (m, 0, 0, 0)),
            pl.BlockSpec(gains.shape, lambda m: (0, 0, 0)),
            pl.BlockSpec(cosine.shape, lambda m: (0, 0)),
            pl.BlockSpec(sine.shape, lambda m: (0, 0)),
            pl.BlockSpec(column.shape, lambda m: (0, 0)),
            pl.BlockSpec(row.shape, lambda m: (0, 0)),
            pl.BlockSpec(memory_space=pltpu.SMEM),
        ],
        out_specs=(saved_spec,) * 3
        + (pl.BlockSpec((places, 1, rows, head_width), lambda m: (0, m, 0, 0)),),
        scratch_shapes=[pltpu.VMEM((slot, head_width), BF)],
        compiler_params=pltpu.CompilerParams(vmem_limit_bytes=60 << 20),
        name="attend",
    )(pre, sums, gains, cosine, sine, column, row, lengths)


def attend_back_body(
    step, query_ref, key_ref, value_ref, datt_ref, pre_ref, sum_ref, gain_ref, cos_ref, sin_ref,
    column_ref, row_ref, length_ref, dn_ref, dv_ref, inner_ref, dgain_ref, att, dq, dk, dv,
):
    m = pl.program_id(0)
    places, rows = pre_ref.shape[1:3]
    slot = places * rows
    head_width = query_ref.shape[2]
    factor = 1.0 / math.sqrt(HEAD)
    att[...] = datt_ref[:, 0].reshape(slot, head_width)
    length = length_ref[m]
    row = row_ref[...]
    dk[...] = jnp.zeros_like(dk)
    dv[...] = jnp.zeros_like(dv)
    for h in range(head_width // HEAD):
        here = slice(h * HEAD, (h + 1) * HEAD)

        @pl.loop(0, slot // step)
        def _(i):
            part = pl.ds(pl.multiple_of(i * step, step), step)
            query, grad = query_ref[0, part, here], att[part, here]
            probs = head_probs(query, key_ref[0, :, here], column_ref[part], row, length)
            d_probs = nt(grad, value_ref[0, :, here])
            inner = jnp.sum(probs * d_probs, axis=1, keepdims=True)
            d_scores = (probs * (d_probs - inner)).astype(BF)
            dq[part, here] = nn(d_scores, key_ref[0, :, here]) * factor
            dk[:, here] += tn(d_scores, query) * factor
            dv[:, here] += tn(probs.astype(BF), grad)

    dv_ref[0] = dv[...].astype(BF)
    cosine, sine = cos_ref[...], sin_ref[...]
    for kind, ref in enumerate((dq, dk)):
        root = lax.rsqrt(columns(sum_ref[0, kind]) / (head_width * places) + EPSILON)
        for h in range(head_width // HEAD):
            here = slice(h * HEAD, (h + 1) * HEAD)
            ref[:, here] = turned_back(ref[:, here], cosine, sine)
        grad = ref[...]
        pre = pre_ref[0, :, :, kind * head_width : (kind + 1) * head_width].reshape(slot, head_width)
        product = grad * pre
        gain_part = jnp.sum(product * root, axis=0, keepdims=True)
        before = jnp.where(m == 0, jnp.zeros_like(gain_part), dgain_ref[kind])
        dgain_ref[kind] = before + gain_part
        weighted = grad * gain_ref[kind]
        dn_ref[0, kind] = weighted
        sums = row_sums(product * gain_ref[kind])
        for n in range(places):
            inner_ref[0, kind, n : n + 1] = sums[:, n * rows : (n + 1) * rows]


def attend_back(saved, d_att, pre, sums, gains, cosine, sine, column, row, lengths):
    batches, places, rows, total = pre.shape
    head_width, slot = total // 3, places * rows
    saved_spec = pl.BlockSpec((1, slot, head_width), lambda m: (m, 0, 0))
    return pl.pallas_call(
        functools.partial(attend_back_body, 256),
        out_shape=(
            jax.ShapeDtypeStruct((batches, 2, slot, head_width), F32),
            jax.ShapeDtypeStruct((batches, slot, head_width), BF),
            jax.ShapeDtypeStruct(sums.shape, F32),
            jax.ShapeDtypeStruct(gains.shape, F32),
        ),
        grid=(batches,),
        in_specs=[saved_spec] * 3
        + [
            pl.BlockSpec((places, 1, rows, head_width), lambda m: (0, m, 0, 0)),
            pl.BlockSpec((1,) + pre.shape[1:], lambda m: (m, 0, 0, 0)),
            pl.BlockSpec((1,) + sums.shape[1:], lambda m: (m, 0, 0, 0)),
            pl.BlockSpec(gains.shape, lambda m: (0, 0, 0)),
            pl.BlockSpec(cosine.shape, lambda m: (0, 0)),
            pl.BlockSpec(sine.shape, lambda m: (0, 0)),
            pl.BlockSpec(column.shape, lambda m: (0, 0)),
            pl.BlockSpec(row.shape, lambda m: (0, 0)),
            pl.BlockSpec(memory_space=pltpu.SMEM),
        ],
        out_specs=(
            pl.BlockSpec((1, 2, slot, head_width), lambda m: (m, 0, 0, 0)),
            saved_spec,
            pl.BlockSpec((1,) + sums.shape[1:], lambda m: (m, 0, 0, 0)),
            pl.BlockSpec(gains.shape, lambda m: (0, 0, 0)),
        ),
        scratch_shapes=[pltpu.VMEM((slot, head_width), BF)]
        + [pltpu.VMEM((slot, head_width), F32)] * 3,
        compiler_params=pltpu.CompilerParams(vmem_limit_bytes=60 << 20),
        name="attend_back",
    )(*saved, d_att, pre, sums, gains, cosine, sine, column, row, lengths)


def back_body(
    quads, dn_ref, dv_ref, pre_ref, sum_ref, inner_ref, ao_ref, at_ref, w_ref,
    do_ref, dt_ref, dw_ref, dw, cols,
):
    n = pl.program_id(0)
    other = n >= quads
    batches, _, rows, head_width = dn_ref.shape
    width = w_ref.shape[0]
    total = head_width * 2 * quads
    for m in range(batches):
        here = pl.ds(m * rows, rows)
        for kind in range(2):
            root = lax.rsqrt(columns(sum_ref[0, m, kind]) / total + EPSILON)
            inner = columns(inner_ref[0, m, kind]) / total
            part = slice(kind * head_width, (kind + 1) * head_width)
            pre = pre_ref[m, 0, :, part]
            grad = root * dn_ref[m, kind] - pre * (root * root * root) * inner
            cols[here, part] = grad.astype(BF)
        cols[here, 2 * head_width :] = dv_ref[m]
    d_pre = cols[...]
    act = jnp.where(other, at_ref[0], ao_ref[0]).reshape(-1, width)
    d_act = nt(d_pre, w_ref[...]).astype(BF).reshape(batches, rows, width)
    part = tn(act, d_pre)

    @pl.when(n == 0)
    def _():
        dw[...] = part

    @pl.when(n > 0)
    def _():
        dw[...] += part

    @pl.when(n == pl.num_programs(0) - 1)
    def _():
        dw_ref[...] = dw[...].astype(BF)

    @pl.when(jnp.logical_not(other))
    def _():
        do_ref[0] = d_act

    @pl.when(other)
    def _():
        dt_ref[0] = d_act


def project_back(d_norm, d_value, pre, sums, inners, act, weights):
    batches, places, rows, total = pre.shape
    quads, width, head_width = places // 2, weights.shape[0], total // 3
    block = (1, batches, rows, width)
    fixed = dict(pipeline_mode=pl.Buffered(1))
    own, other = pl.BlockSpec(block, own_block(quads)), pl.BlockSpec(block, other_block(quads))
    sums = sums.transpose(2, 0, 1, 3)[:, :, :, None]
    inners = inners[:, :, :, None]
    small = pl.BlockSpec((1, batches, 2, 1, rows), lambda n: (n, 0, 0, 0, 0))
    return pl.pallas_call(
        functools.partial(back_body, quads),
        out_shape=(
            jax.ShapeDtypeStruct(act[0].shape, BF), jax.ShapeDtypeStruct(act[0].shape, BF),
            jax.ShapeDtypeStruct(weights.shape, BF),
        ),
        grid=(places,),
        in_specs=[
            pl.BlockSpec((batches, 2, rows, head_width), lambda n: (0, 0, n, 0)),
            pl.BlockSpec((batches, rows, head_width), lambda n: (0, n, 0)),
            pl.BlockSpec((batches, 1, rows, total), lambda n: (0, n, 0, 0)),
            small, small, own, other,
            pl.BlockSpec(weights.shape, lambda n: (0, 0), **fixed),
        ],
        out_specs=(own, other, pl.BlockSpec(weights.shape, lambda n: (0, 0))),
        scratch_shapes=[
            pltpu.VMEM(weights.shape, F32), pltpu.VMEM((batches * rows, total), BF)
        ],
        compiler_params=pltpu.CompilerParams(vmem_limit_bytes=60 << 20),
        name="project_back",
    )(d_norm, d_value, pre, sums, inners, *act, weights)


def scatter_all(pairs, partners, name, number, extra=()):
    if pairs[0][0].shape[0] == 4:
        return scatter_rows(pairs, partners, name, number, extra)
    sums = []
    for i, ((own, other), partner) in enumerate(zip(pairs, partners)):
        count = own.shape[1] // 2 if partner else own.shape[1]
        parts = [
            scatter_rows(
                [(own[:, m::count], other[:, m::count])], (partner,), name, number + 8 * i
            )[0]
            for m in range(count)
        ]
        sums.append(jnp.concatenate(parts))
    return sums + [exchange(blocks, DP) for blocks in extra]


def on_device(
    tokens,
    cotangent,
    routes,
    lengths,
    block_order,
    w_query,
    w_key,
    w_value,
    w_out,
    w_router,
    w_gate,
    w_up,
    w_down,
    attn_gain,
    mlp_gain,
    query_gain,
    key_gain,
):
    batches, _, rows, width = tokens.shape
    dp_size = lax.axis_size(DP)
    ctx_size = lax.axis_size(CTX)
    quads = lax.axis_size("quad")
    lanes = lax.axis_size("lane")
    slot_len = rows * ctx_size
    block_rows = rows // 2
    head_width = width // ctx_size
    shard = w_query.shape[0]
    expert_count = w_router.shape[1]
    local_experts = w_gate.shape[0]
    hidden_units = w_gate.shape[2]
    hidden_half = hidden_units // 2
    depth_part = w_gate.shape[1]
    pair = lax.axis_index("pair")

    qkv = jnp.stack([w_query, w_key, w_value], axis=1).reshape(shard, 3, ctx_size, head_width)
    qkv = qkv.transpose(2, 0, 1, 3).reshape(ctx_size, shard, 3 * head_width)
    small = jnp.concatenate(
        [attn_gain, mlp_gain, query_gain, key_gain, w_router.reshape(shard * expert_count)]
    )
    grad_low = cotangent[:, 0]
    tok_own, tok_other, qkv_w, small, out_w = start_gather(
        tokens[:, 0], qkv, small.reshape(1, -1), w_out
    )
    out_w = lax.all_gather(out_w, CTX, axis=1, tiled=False).reshape(width, width)
    token_rows = (tok_own, tok_other)
    qkv_w = qkv_w.reshape(width, 3 * head_width)
    small = small.reshape(dp_size * ctx_size, -1)
    gain_attn = small[:, :shard].reshape(width).astype(F32)
    gain_mlp = small[:, shard : 2 * shard].reshape(width).astype(F32)
    gain_query = small[:, 2 * shard : 3 * shard].reshape(ctx_size, head_width)
    gain_key = small[:, 3 * shard : 4 * shard].reshape(ctx_size, head_width)
    router_w = small[:, 4 * shard :].reshape(width, expert_count)
    here = lax.axis_index(CTX)
    gain_query = lax.dynamic_index_in_dim(gain_query, here, 0, keepdims=False).astype(F32)
    gain_key = lax.dynamic_index_in_dim(gain_key, here, 0, keepdims=False).astype(F32)

    w_gate, w_up, w_down, crossing, qkv_w = lax.optimization_barrier(
        (w_gate, w_up, w_down, grad_low, qkv_w)
    )
    halves = [
        jnp.stack(
            [
                jnp.stack([w_gate[e, :, part], w_up[e, :, part]])
                for part in (slice(0, hidden_half), slice(hidden_half, hidden_units))
            ]
        )
        for e in range(local_experts)
    ]
    halves = [jnp.repeat(part, lanes, axis=0) for part in halves]
    next_w = exchange(halves[0], DP)
    down_parts = lane_parts(w_down)
    g_own = lax.all_gather(crossing, CTX, axis=0, tiled=False)

    def places_of(device):
        stored = device * rows + jnp.arange(rows, dtype=jnp.int32)
        match_marks = (stored // block_rows)[:, None] == jnp.arange(
            block_order.shape[0], dtype=jnp.int32
        )[None, :]
        first_place = jnp.sum(jnp.where(match_marks, block_order[None, :], 0), axis=1)
        return first_place * block_rows + stored % block_rows

    places = jnp.concatenate(
        [
            places_of((lax.axis_index("quad") ^ k) * 2 + (pair ^ other))
            for other in range(2)
            for k in range(quads)
        ]
    )
    cosine, sine = angles(places, HEAD)
    expert_range = jnp.arange(expert_count, dtype=jnp.int32)

    inputs = tokens[:, 0].astype(F32)
    attn_root = inv_rms(inputs)
    act_own, act_other, pre, squares = project(token_rows, gain_attn, qkv_w)
    squares = sum_ctx(squares, "sum_squares", 6)
    squares = squares.reshape(2 * quads, 2, batches, rows).transpose(2, 1, 0, 3)
    qk_gains = jnp.stack([gain_query, gain_key])[:, None]
    signed = jnp.where(jnp.arange(HEAD) < HEAD // 2, -sine[:, 0], sine[:, 0])
    context = (pre, squares, qk_gains, cosine[:, 0], signed, places[:, None], places[None, :])
    context = context + (lengths[:, 0],)
    *saved, attended = attend(*context)
    attended = exchange_rows(attended[None], "inward", "attended_to_rows", 7)[0]
    attended, next_w = lax.optimization_barrier((attended, next_w))
    attended = attended.transpose(1, 2, 0, 3).reshape(batches, rows, width)
    x_mid = inputs + dot("mtd,de->mte", attended, out_w)
    mlp_root = inv_rms(x_mid)
    mixed_in = (x_mid * mlp_root * gain_mlp).astype(BF)
    router = jax.nn.softmax(dot("mtd,de->mte", mixed_in, router_w), axis=-1)
    routed = jnp.any(routes[:, 0, :, :, None] == expert_range, axis=2).astype(F32)
    gates = (router * routed).transpose(2, 0, 1).reshape(ctx_size, local_experts, batches, rows)
    x_rows, cross_rows = gather_rows([mixed_in, grad_low], ("both", "partner"), "gather_mixed", 2)
    gates, x_rows = lax.optimization_barrier((gates, x_rows))
    gates = exchange_rows(gates, "outward", "gates_to_experts", 8, 2)
    g_rows = (g_own,) + cross_rows
    gates = gates.transpose(1, 0, 3, 4, 2).reshape(4 * quads, batches * rows, local_experts)
    number = jnp.arange(2 * quads, dtype=jnp.int32)
    place = (lax.axis_index("quad") ^ (number % quads)) * 2 + (pair ^ (number // quads))
    x_rows, next_w, down_parts, halves, gates = lax.optimization_barrier(
        (x_rows, next_w, down_parts, halves, gates)
    )
    down_w = gather_lane(w_down, down_parts).swapaxes(0, 1)
    down_w = down_w.reshape(local_experts, hidden_half, width)

    sums = ()
    d_gates, grads_both, grads_down = [], [], []
    for e in range(local_experts):
        both_w = next_w
        if e < local_experts - 1:
            next_w = exchange(halves[e + 1], DP)
        *sums, d_gate, hid, d_gate_pre, d_up_pre = expert(
            place, gates[..., e : e + 1], x_rows, g_rows, both_w, down_w[e], tuple(sums),
            f"expert_{e}",
        )
        d_gates.append(d_gate)
        grad_both, grad_down = expert_grads(
            place, x_rows, g_rows, hid, d_gate_pre, d_up_pre, dp_size, f"expert_grads_{e}"
        )
        sums[0], grad_both, next_w = lax.optimization_barrier((sums[0], grad_both, next_w))
        grads_both.append(exchange(grad_both, DP) if e < local_experts - 1 else grad_both)
        grads_down.append(grad_down)
    moe_own, moe_other, d_own, d_other = sums
    done, grads_down, d_own = lax.optimization_barrier((grads_both[:-1], grads_down, d_own))
    grads_both[:-1] = done
    grads_down = jnp.stack(grads_down)
    grads_down = grads_down.reshape(local_experts, lanes, -1, width).swapaxes(0, 1)
    lane = lax.axis_index("lane")
    down_others = [
        lax.ppermute(
            lax.dynamic_index_in_dim(grads_down, lane ^ d, 0, keepdims=False),
            "lane", [(i, i ^ d) for i in range(lanes)],
        )
        for d in range(1, lanes)
    ]
    d_mixed, moe_sum = scatter_all(
        [(d_own, d_other), (moe_own, moe_other)], (True, True), "scatter_experts", 24
    )
    d_gates = jnp.concatenate(d_gates, axis=-1)
    d_gates = d_gates.reshape(2 * quads, 2, batches, rows, local_experts)
    d_gates = d_gates.transpose(1, 0, 4, 2, 3)
    d_gates, d_mixed, down_others = lax.optimization_barrier((d_gates, d_mixed, down_others))
    d_router = exchange_rows(d_gates, "inward", "gate_gradients", 9, 2)
    d_router, last_both = lax.optimization_barrier((d_router, grads_both[-1]))
    grads_both[-1] = exchange(last_both, DP)
    d_router = jnp.sum(d_router, axis=0).reshape(expert_count, batches, rows)
    d_router = d_router.transpose(1, 2, 0) * routed
    d_logits = (
        router * (d_router - jnp.sum(router * d_router, axis=-1, keepdims=True))
    ).astype(BF)
    d_mixed = d_mixed + dot("mte,de->mtd", d_logits, router_w)

    def norm_back_all(values, root, gain, grad):
        d_values, d_gain = norm_back(values, root, gain, grad)
        return d_values, jnp.sum(d_gain, axis=0)

    d_mid, part_mlp_gain = norm_back_all(x_mid, mlp_root, gain_mlp, d_mixed)
    d_mid = d_mid + grad_low.astype(F32)
    d_att_out = d_mid.astype(BF)
    grad_out = dot("mtd,mte->de", attended, d_att_out).astype(BF)
    d_attended = dot("mte,de->mtd", d_att_out, out_w).astype(BF)
    d_attended, grad_out = lax.optimization_barrier((d_attended, grad_out))
    grad_out = lax.psum_scatter(grad_out, ALL, scatter_dimension=0, tiled=True).astype(F32)
    d_attended = d_attended.reshape(batches, rows, ctx_size, head_width).transpose(2, 0, 1, 3)
    d_attended = exchange_rows(d_attended, "outward", "attended_gradients", 10)[0]
    d_norm, d_value, inners, d_gains = attend_back(saved, d_attended, *context)
    inners = inners.transpose(2, 0, 1, 3).reshape(2 * quads, 2 * batches, rows)
    inners = sum_ctx(inners, "sum_inner", 11).reshape(2 * quads, batches, 2, rows)
    d_act_own, d_act_other, grad_qkv = project_back(
        d_norm, d_value, pre, squares, inners, (act_own, act_other), qkv_w
    )
    grad_qkv = grad_qkv.reshape(dp_size, -1, 3 * head_width)
    d_act, grad_qkv = scatter_all(
        [(d_act_own, d_act_other)], (False,), "scatter_act", 25, (grad_qkv,)
    )
    d_inputs, part_attn_gain = norm_back_all(inputs, attn_root, gain_attn, d_act)
    mixed = (x_mid + moe_sum).astype(BF)

    grad_gate, grad_up = finish_grads(grads_both)
    grad_down = lax.dynamic_index_in_dim(grads_down, lane, 0, keepdims=False).astype(F32)
    for part in down_others:
        grad_down = grad_down + part.astype(F32)

    grad_qkv = jnp.sum(grad_qkv.astype(F32), axis=0).astype(BF)
    grad_qkv = grad_qkv.reshape(ctx_size, shard, 3 * head_width)
    grad_qkv = exchange_rows(grad_qkv, "ctx", "qkv_gradients", 14).astype(F32)
    grad_qkv = grad_qkv.reshape(ctx_size, shard, 3, head_width).transpose(2, 1, 0, 3)
    grad_qkv = grad_qkv.reshape(3, shard, width)

    grad_router = dot("mtd,mte->de", mixed_in, d_logits)
    columns = jnp.arange(ctx_size, dtype=jnp.int32)[:, None] == here

    def placed(part):
        return jnp.where(columns, part[None, :], 0.0).reshape(width)

    gains = jnp.stack(
        [part_attn_gain, part_mlp_gain, placed(d_gains[0, 0]), placed(d_gains[1, 0])]
    )
    gains = gains.reshape(4, dp_size, ctx_size, shard).transpose(1, 2, 0, 3)
    packed = jnp.concatenate(
        [
            gains.reshape(dp_size * ctx_size, 1, 4 * shard),
            grad_router.reshape(dp_size * ctx_size, 1, shard * expert_count),
        ],
        axis=2,
    )
    packed = reduce_small(packed)
    return (
        mixed[:, None],
        (d_inputs + d_mid)[:, None],
        grad_qkv[0],
        grad_qkv[1],
        grad_qkv[2],
        grad_out,
        packed[4 * shard :].reshape(shard, expert_count),
        grad_gate,
        grad_up,
        grad_down,
        packed[:shard],
        packed[shard : 2 * shard],
        packed[2 * shard : 3 * shard],
        packed[3 * shard : 4 * shard],
    )


def solution(mesh):
    dp_size, ctx_size = mesh.shape["dp"], mesh.shape["ctx"]
    grid = Mesh(mesh.devices.reshape(2, dp_size // 2, ctx_size // 2, 2), ALL)
    rows = P(None, DP, CTX, None)
    dense = P(ALL, None)
    expert = P(CTX, DP, None)
    vector = P(ALL)
    return jax.shard_map(
        on_device,
        mesh=grid,
        in_specs=(rows, rows, rows, P(None, DP), P())
        + (dense,) * 5
        + (expert,) * 3
        + (vector,) * 4,
        out_specs=(rows, rows) + (dense,) * 5 + (expert,) * 3 + (vector,) * 4,
        check_vma=False,
    )
```

```python
import functools
import math

import jax
import jax.numpy as jnp
from jax import lax
from jax.experimental import pallas as pl
from jax.experimental.pallas import tpu as pltpu
from jax.sharding import Mesh
from jax.sharding import PartitionSpec as P

HEAD = 128
EPSILON = 1e-05
ROPE_BASE = 10000.0
MASKED = -1e30
BF = jnp.bfloat16
F32 = jnp.float32
DP = ("half", "lane")
CTX = ("quad", "pair")
ALL = DP + CTX
MESH = pl.DeviceIdType.MESH


def dot(spec, left, right):
    return jnp.einsum(spec, left, right, preferred_element_type=F32)


def inv_rms(values):
    return lax.rsqrt(jnp.mean(values * values, axis=-1, keepdims=True) + EPSILON)


def norm_back(values, inv_root, gain_vec, grad_in):
    weighted = grad_in * gain_vec
    inner = jnp.mean(weighted * values, axis=-1, keepdims=True)
    grad_values = inv_root * weighted - values * (inv_root * inv_root * inv_root) * inner
    return (grad_values, jnp.sum(grad_in * values * inv_root, axis=0))


def angles(places, head_width):
    index = jnp.arange(head_width // 2, dtype=F32)
    freqs = jnp.power(ROPE_BASE, -2.0 * index / head_width)
    turning = places.astype(F32)[:, None] * freqs[None, :]
    turning = jnp.concatenate([turning, turning], axis=1)
    return (jnp.cos(turning)[:, None, :], jnp.sin(turning)[:, None, :])


def swap(values, axis):
    return lax.ppermute(values, axis, [(0, 1), (1, 0)])


def exchange(blocks, axes):
    return lax.all_to_all(blocks, axes, split_axis=0, concat_axis=0, tiled=True)


def lane_parts(values):
    if lax.axis_size("lane") == 2:
        return swap(values, "lane")
    return lax.all_gather(values, "lane", axis=0, tiled=False)


def gather_lane(values, parts):
    if lax.axis_size("lane") == 2:
        first = lax.axis_index("lane") == 0
        return jnp.stack([jnp.where(first, values, parts), jnp.where(first, parts, values)])
    return parts


def toggled(index, bits):
    step = 1
    while step <= bits:
        if bits & step:
            index = index + step - 2 * step * ((index // step) % 2)
        step *= 2
    return index


def greet(peers):
    barrier = pltpu.get_barrier_semaphore()
    for peer in peers:
        pl.semaphore_signal(barrier, inc=1, device_id=peer, device_id_type=MESH)
    pl.semaphore_wait(barrier, len(peers))


class Mover:
    def __init__(self, send, recv, local):
        self.send, self.recv, self.local = send, recv, local
        self.number, self.local_number = 0, 0
        self.sent, self.kept = [], []

    def copy(self, src, dst, device):
        i = self.number
        self.number += 1
        return pltpu.make_async_remote_copy(
            src_ref=src, dst_ref=dst, send_sem=self.send.at[i], recv_sem=self.recv.at[i],
            device_id=device, device_id_type=MESH,
        )

    def go(self, *copies):
        for c in copies:
            c.start()
            self.sent.append(c)

    def keep(self, src, dst):
        c = pltpu.make_async_copy(src, dst, self.local.at[self.local_number])
        self.local_number += 1
        c.start()
        self.kept.append(c)
        return c

    def finish(self):
        for c in self.sent:
            c.wait_send()
        for c in self.kept:
            c.wait()


class Spread:
    def __init__(self, mover, quads, src, slot):
        self.mover, self.quads = mover, quads
        quad = lax.axis_index("quad")
        to_quad = [{"quad": toggled(quad, k)} for k in range(quads)]
        sibling = {"pair": 1 - lax.axis_index("pair")}
        rows = src.shape[0]
        halves = (("a", pl.ds(0, rows // 2)), ("b", pl.ds(rows // 2, rows // 2)))
        p = {"o0": mover.copy(src, slot(1, 0, 0), sibling)}
        if quads == 4:
            for k in (1, 2):
                for name, part in halves:
                    p[f"s{k}{name}"] = mover.copy(
                        src.at[part], slot(0, k, 0).at[part], to_quad[k]
                    )
            for k, (name, part) in zip((1, 2), halves):
                p[f"f3{name}"] = mover.copy(
                    slot(0, k, k).at[part], slot(0, 3, k).at[part], to_quad[3 - k]
                )
            for k in (1, 2, 3):
                for name, part in halves:
                    p[f"o{k}{name}"] = mover.copy(
                        slot(0, k, k).at[part], slot(1, k, k).at[part], sibling
                    )
        else:
            for k in range(1, quads):
                p[f"s{k}"] = mover.copy(src, slot(0, k, 0), to_quad[k])
                p[f"o{k}"] = mover.copy(slot(0, k, k), slot(1, k, k), sibling)
        self.copies = p

    @staticmethod
    def count(quads):
        return 13 if quads == 4 else 2 * quads - 1

    def begin(self):
        names = [f"s{k}" for k in range(1, self.quads)]
        if self.quads == 4:
            names = ["s1a", "s2b", "s1b", "s2a"]
        self.mover.go(*[self.copies[name] for name in names + ["o0"]])

    def forward(self):
        p = self.copies
        steps = [(f"s{k}", (f"o{k}",)) for k in range(1, self.quads)]
        if self.quads == 4:
            steps = [
                ("s1a", ("f3a", "o1a")), ("s2b", ("f3b", "o2b")), ("s1b", ("o1b",)),
                ("s2a", ("o2a",)), ("f3a", ("o3a",)), ("f3b", ("o3b",)),
            ]
        for name, then in steps:
            p[name].wait_recv()
            self.mover.go(*[p[t] for t in then])

    def arrive(self):
        for name, c in self.copies.items():
            if name[0] == "o":
                c.wait_recv()


def relative_slots(ref, s):
    return lambda core, kr, km: ref.at[core, kr, s]


def ctx_peers(quads):
    return [ctx_at(quads, n)[0] for n in range(1, 2 * quads)]


def planes_of(lanes):
    half, lane = lax.axis_index("half"), lax.axis_index("lane")
    result = []
    for n in range(1, 2 * lanes):
        h, l = toggled(half, n // lanes), toggled(lane, n % lanes)
        result.append(({"half": h, "lane": l}, h * lanes + l))
    return half * lanes + lane, result


def gather_body(quads, partners, *refs):
    inputs = refs[: len(partners)]
    refs = refs[len(partners) :]
    outputs = refs[: len(partners)]
    refs = refs[len(partners) :]
    keeps = {}
    for i, partner in enumerate(partners):
        if partner != "own":
            keeps[i], refs = refs[0], refs[1:]
    local, send, recv = refs
    mover = Mover(send, recv, local)
    across = {"half": 1 - lax.axis_index("half")}
    quad = lax.axis_index("quad")
    peers = [{"quad": toggled(quad, k)} for k in range(1, quads)]
    peers.append({"pair": 1 - lax.axis_index("pair")})
    greet(peers + ([across] if keeps else []))

    def add(sources, i, offset):
        plans = []
        for s, src in enumerate(sources):
            p = Spread(mover, quads, src, relative_slots(outputs[i], offset + s))
            p.begin()
            plans.append(p)
            mover.keep(src, outputs[i].at[0, 0, offset + s])
        return plans

    crossing = {}
    for i, keep in keeps.items():
        crossing[i] = [
            mover.copy(inputs[i].at[s], keep.at[s], across) for s in range(inputs[i].shape[0])
        ]
        mover.go(*crossing[i])
    plans = []
    for i, ref in enumerate(inputs):
        if partners[i] == "partner":
            continue
        plans += add([ref.at[s] for s in range(ref.shape[0])], i, 0)
    for p in plans:
        p.forward()
    late = []
    for i, keep in keeps.items():
        for c in crossing[i]:
            c.wait_recv()
        offset = keep.shape[0] if partners[i] == "both" else 0
        added = add([keep.at[s] for s in range(keep.shape[0])], i, offset)
        for p in added:
            p.forward()
        late += added
    for p in plans + late:
        p.arrive()
    mover.finish()


def gather_rows(sources, partners, name, number):
    quads = lax.axis_size("quad")
    shapes, keeps = [], []
    sems = total = 0
    for x, partner in zip(sources, partners):
        count = x.shape[0] * (2 if partner == "both" else 1)
        total += count
        sems += count * Spread.count(quads) + (x.shape[0] if partner != "own" else 0)
        shapes.append(jax.ShapeDtypeStruct((2, quads, count) + x.shape[1:], x.dtype))
        if partner != "own":
            keeps.append(pltpu.VMEM(x.shape, x.dtype))
    return pl.pallas_call(
        functools.partial(gather_body, quads, partners),
        out_shape=shapes,
        in_specs=[pl.BlockSpec(memory_space=pltpu.VMEM)] * len(sources),
        out_specs=[pl.BlockSpec(memory_space=pl.ANY)] * len(shapes),
        scratch_shapes=keeps
        + [
            pltpu.SemaphoreType.DMA((total,)),
            pltpu.SemaphoreType.DMA((sems,)),
            pltpu.SemaphoreType.DMA((sems,)),
        ],
        compiler_params=pltpu.CompilerParams(collective_id=number, has_side_effects=True),
        name=name,
    )(*sources)


def start_body(
    quads, lanes, tok_ref, qkv_ref, small_ref, wout_ref,
    tok_out, qkv_out, small_out, wout_out, local, send, recv,
):
    mover = Mover(send, recv, local)
    half, lane = lax.axis_index("half"), lax.axis_index("lane")
    plane, here = half * lanes + lane, ctx_place()
    partner = (1 - half) * lanes + lane
    across = {"half": 1 - half}
    devices = 4 * lanes * quads
    others = [all_at(lanes, quads, n)[0] for n in range(1, devices)]
    greet(others)
    mine = mover.keep(small_ref, small_out.at[plane * 2 * quads + here])
    shared = [mover.copy(small_ref, small_out.at[plane * 2 * quads + here], d) for d in others]
    mover.go(*shared)

    def planes(src, view):
        first = mover.copy(src, view(plane), across)
        rest = [
            mover.copy(src, view(plane), {"lane": toggled(lane, d)}) for d in range(1, lanes)
        ]
        then = [
            mover.copy(view(partner), view(partner), {"lane": toggled(lane, d)})
            for d in range(1, lanes)
        ]
        mover.go(first, *rest)
        return first, rest, then

    mover.keep(wout_ref, wout_out.at[plane])
    w_first, w_rest, w_then = planes(wout_ref, lambda p: wout_out.at[p])
    kept = mover.keep(qkv_ref.at[here], qkv_out.at[plane, here])
    columns = []
    for n in range(1, 2 * quads):
        device, place = ctx_at(quads, n)
        columns.append(mover.copy(qkv_ref.at[place], qkv_out.at[plane, here], device))
    mover.go(*columns)
    tokens = []
    for s in range(tok_ref.shape[0]):
        p = Spread(mover, quads, tok_ref.at[s], relative_slots(tok_out, s))
        p.begin()
        tokens.append(p)
        mover.keep(tok_ref.at[s], tok_out.at[0, 0, s])
    for c in columns:
        c.wait_recv()
    kept.wait()
    mover.kept = [c for c in mover.kept if c is not kept]
    q_first, q_rest, q_then = planes(qkv_out.at[plane], lambda p: qkv_out.at[p])
    w_first.wait_recv()
    mover.go(*w_then)
    tokens[0].forward()
    q_first.wait_recv()
    mover.go(*q_then)
    for p in tokens[1:]:
        p.forward()
    for p in tokens:
        p.arrive()
    for c in shared + q_rest + q_then + w_rest + w_then:
        c.wait_recv()
    mover.finish()


def start_gather(tokens, qkv, small, w_out):
    quads, lanes = lax.axis_size("quad"), lax.axis_size("lane")
    count = tokens.shape[0]
    planes, devices = 2 * lanes, 4 * lanes * quads

    def like(lead, x, dtype=BF):
        return jax.ShapeDtypeStruct(lead + x.shape, dtype)

    sems = (devices - 1) + 2 * (2 * lanes - 1) + (2 * quads - 1)
    sems += Spread.count(quads) * count
    return pl.pallas_call(
        functools.partial(start_body, quads, lanes),
        out_shape=[like((2, quads), tokens)]
        + [like((planes,), qkv), like((devices,), small), like((planes,), w_out)],
        in_specs=[pl.BlockSpec(memory_space=pltpu.VMEM)] * 4,
        out_specs=[pl.BlockSpec(memory_space=pl.ANY)] * 4,
        scratch_shapes=[
            pltpu.SemaphoreType.DMA((3 + count,)),
            pltpu.SemaphoreType.DMA((sems,)),
            pltpu.SemaphoreType.DMA((sems,)),
        ],
        compiler_params=pltpu.CompilerParams(collective_id=0, has_side_effects=True),
        name="start_gather",
    )(tokens, qkv, small, w_out)


def add_rows(out_ref, *refs):
    rows = out_ref.shape[0]
    step = 16

    @pl.loop(0, rows // step)
    def _(i):
        part = pl.ds(pl.multiple_of(i * step, step), step)
        total = refs[0][part].astype(F32)
        for ref in refs[1:]:
            total = total + ref[part].astype(F32)
        out_ref[part] = total.astype(out_ref.dtype)


def scatter_body(quads, lanes, partners, count, extra, *refs):
    kinds = len(partners)
    inputs, refs = refs[:kinds], refs[kinds:]
    if extra:
        blocks_ref, *refs = refs
    outputs, refs = refs[:kinds], refs[kinds:]
    if extra:
        blocks_out, held, *refs = refs
    mine, theirs, relay, arrived, *rest = refs
    if any(partners):
        summed, back, *rest = rest
    local, send, recv = rest
    mover = Mover(send, recv, local)
    mover.local_number = local.shape[0] - 2
    rows = inputs[0].shape[3]
    first, second = pl.ds(0, rows // 2), pl.ds(rows // 2, rows // 2)
    quad = lax.axis_index("quad")
    to_quad = [{"quad": toggled(quad, k)} for k in range(quads)]
    sibling = {"pair": 1 - lax.axis_index("pair")}
    across = {"half": 1 - lax.axis_index("half")}
    peers = to_quad[1:] + [sibling]
    if extra:
        me, planes = planes_of(lanes)
        peers += [device for device, _ in planes]
    elif any(partners):
        peers.append(across)
    greet(peers)

    def go(src, dst, device):
        c = mover.copy(src, dst, device)
        mover.go(c)
        return c

    order = [(i, s) for i in range(kinds) if partners[i] for s in range(count, 2 * count)]
    order += [(i, s) for i in range(kinds) for s in range(count)]
    ks = [3, 1, 2, 0] if quads == 4 else list(range(quads - 1, -1, -1))
    sib, loc = {}, {}

    def pieces(i, core, k, s):
        if len(inputs[i].shape) == 5:
            return [(inputs[i].at[core, k, s], pl.ds(0, rows))]
        shard = inputs[i].shape[2]
        place = ctx_at(quads, core * quads + k)[1]
        each = rows // shard
        return [
            (inputs[i].at[s * each + j, place], pl.ds(j * shard, shard)) for j in range(each)
        ]

    def load(src, dst, number):
        c = pltpu.make_async_copy(src, dst, local.at[number])
        c.start()
        return c

    for n, (i, s) in enumerate(order):
        for k in ks:
            sib[n, k] = [
                go(src, theirs.at[n, k, part], sibling) for src, part in pieces(i, 1, k, s)
            ]
            loc[n, k] = [
                load(src, mine.at[n, k, part], (n * quads + k) * 2 + j)
                for j, (src, part) in enumerate(pieces(i, 0, k, s))
            ]
    sends = {}

    def merge(n):
        for k in ks:
            for c in sib[n, k]:
                c.wait_recv()
            for c in loc[n, k]:
                c.wait()
            add_rows(mine.at[n, k], mine.at[n, k], theirs.at[n, k])
            if quads == 4:
                if k == 3:
                    sends[n, "3a"] = go(mine.at[n, 3, first], relay.at[n, 0], to_quad[2])
                    sends[n, "3b"] = go(mine.at[n, 3, second], relay.at[n, 1], to_quad[1])
                elif k == 1:
                    sends[n, "1b"] = go(mine.at[n, 1, second], arrived.at[n, 0, second], to_quad[1])
                elif k == 2:
                    sends[n, "2a"] = go(mine.at[n, 2, first], arrived.at[n, 1, first], to_quad[2])
            elif k:
                sends[n, k] = go(mine.at[n, k], arrived.at[n, k - 1], to_quad[k])

    def pass_on(n):
        if quads == 4:
            sends[n, "3a"].wait_recv()
            add_rows(mine.at[n, 1, first], mine.at[n, 1, first], relay.at[n, 0])
            sends[n, "1a"] = go(mine.at[n, 1, first], arrived.at[n, 0, first], to_quad[1])
            sends[n, "3b"].wait_recv()
            add_rows(mine.at[n, 2, second], mine.at[n, 2, second], relay.at[n, 1])
            sends[n, "2b"] = go(mine.at[n, 2, second], arrived.at[n, 1, second], to_quad[2])

    backs = {}

    def total_of(n):
        i, s = order[n]
        for name in ("1b", "2a", "1a", "2b") if quads == 4 else range(1, quads):
            sends[n, name].wait_recv()
        parts = [mine.at[n, 0]] + [arrived.at[n, j] for j in range(arrived.shape[1])]
        if s >= count:
            slot = i * count + s - count
            add_rows(summed.at[slot], *parts)
            backs[slot] = go(summed.at[slot], back.at[slot], across)
        else:
            if partners[i]:
                backs[i * count + s].wait_recv()
                parts.append(back.at[i * count + s])
            add_rows(outputs[i].at[s], *parts)

    ahead = 2
    exchanged = []

    if extra:
        into = mover.keep(blocks_ref.at[me], held)
        for device, place in planes:
            exchanged.append(go(blocks_ref.at[place], blocks_out.at[me], device))
    for n in range(len(order) + 2 * ahead):
        if extra and n == 1:
            into.wait()
            mover.kept = [c for c in mover.kept if c is not into]
            mover.keep(held, blocks_out.at[me])
        if n < len(order):
            merge(n)
        if 0 <= n - 1 < len(order):
            pass_on(n - 1)
        if 0 <= n - 2 * ahead < len(order):
            total_of(n - 2 * ahead)
    for c in exchanged:
        c.wait_recv()
    mover.finish()


def scatter_rows(parts, partners, name, number, extra=()):
    lanes = lax.axis_size("lane")
    _, quads, _, rows, width = parts[0].shape
    shards = sum(
        part.shape[2] if len(part.shape) == 5 else part.shape[0] * part.shape[2] // rows
        for part in parts
    )
    kinds = len(parts)
    count = shards // sum(2 if partner else 1 for partner in partners)
    incoming = 2 if quads == 4 else quads - 1
    sems = shards * (2 * quads + (6 if quads == 4 else quads - 1)) + count * sum(partners)

    def buf(*lead):
        return pltpu.VMEM(lead + (rows, width), BF)

    scratch = [buf(shards, quads), buf(shards, quads)]
    scratch += [pltpu.VMEM((shards, 2, rows // 2, width), BF), buf(shards, incoming)]
    if any(partners):
        scratch += [buf(kinds * count), buf(kinds * count)]
    shapes = [jax.ShapeDtypeStruct((count, rows, width), F32)] * kinds
    specs = [pl.BlockSpec(memory_space=pltpu.VMEM)] * kinds
    anywhere = pl.BlockSpec(memory_space=pl.ANY)
    if extra:
        blocks = extra[0]
        shapes = shapes + [jax.ShapeDtypeStruct(blocks.shape, BF)]
        specs = specs + [anywhere]
        scratch = [pltpu.VMEM(blocks.shape[1:], BF)] + scratch
        sems += 2 * lanes - 1
    return pl.pallas_call(
        functools.partial(scatter_body, quads, lanes, partners, count, bool(extra)),
        out_shape=shapes,
        in_specs=[anywhere] * (kinds + len(extra)),
        out_specs=specs,
        scratch_shapes=scratch
        + [
            pltpu.SemaphoreType.DMA((2 * shards * quads + 2,)),
            pltpu.SemaphoreType.DMA((sems,)),
            pltpu.SemaphoreType.DMA((sems,)),
        ],
        compiler_params=pltpu.CompilerParams(
            collective_id=number, has_side_effects=True, vmem_limit_bytes=60 << 20
        ),
        name=name,
    )(*parts, *extra)


def ctx_place():
    return lax.axis_index("quad") * 2 + lax.axis_index("pair")


def ctx_at(quads, number):
    core, distance = number // quads, number % quads
    quad = toggled(lax.axis_index("quad"), distance)
    pair = toggled(lax.axis_index("pair"), core)
    return {"quad": quad, "pair": pair}, quad * 2 + pair


def all_at(lanes, quads, number):
    half = toggled(lax.axis_index("half"), number // (lanes * 2 * quads))
    lane = toggled(lax.axis_index("lane"), number // (2 * quads) % lanes)
    device, place = ctx_at(quads, number % (2 * quads))
    return {"half": half, "lane": lane, **device}, (half * lanes + lane) * 2 * quads + place


def exchange_body(mode, lanes, quads, halves, x_ref, out_ref, local, send, recv):
    copies = []
    peers = []
    if mode in ("shared", "all"):
        me = (lax.axis_index("half") * lanes + lax.axis_index("lane")) * 2 * quads + ctx_place()
        for n in range(2 * lanes * 2 * quads):
            device, place = all_at(lanes, quads, n)
            copies.append((x_ref if mode == "shared" else x_ref.at[place], out_ref.at[me], device))
    else:
        for h in range(halves):
            for n in range(2 * quads):
                device, place = ctx_at(quads, n)
                if halves == 2:
                    device = {"half": toggled(lax.axis_index("half"), h), **device}
                if mode == "inward":
                    pair = (x_ref.at[h, n], out_ref.at[h, ctx_place()])
                elif mode == "outward":
                    pair = (x_ref.at[place], out_ref.at[h, n])
                else:
                    pair = (x_ref.at[place], out_ref.at[ctx_place()])
                copies.append(pair + (device,))
    own = pltpu.make_async_copy(copies[0][0], copies[0][1], local)
    own.start()
    greet([device for _, _, device in copies[1:]])
    started = []
    for i, (src, dst, device) in enumerate(copies[1:]):
        c = pltpu.make_async_remote_copy(
            src_ref=src, dst_ref=dst, send_sem=send.at[i], recv_sem=recv.at[i],
            device_id=device, device_id_type=MESH,
        )
        c.start()
        started.append(c)
    own.wait()
    for c in started:
        c.wait_recv()
    for c in started:
        c.wait_send()


def exchange_rows(x, mode, name, number, halves=1):
    quads, lanes = lax.axis_size("quad"), lax.axis_size("lane")
    count = halves * 2 * quads - 1
    shape = x.shape
    if mode == "outward":
        shape = (halves, 2 * quads) + x.shape[1:]
    elif mode in ("shared", "all"):
        count = 4 * lanes * quads - 1
        if mode == "shared":
            shape = (count + 1,) + x.shape
    return pl.pallas_call(
        functools.partial(exchange_body, mode, lanes, quads, halves),
        out_shape=jax.ShapeDtypeStruct(shape, x.dtype),
        in_specs=[pl.BlockSpec(memory_space=pltpu.VMEM)],
        out_specs=pl.BlockSpec(memory_space=pltpu.VMEM),
        scratch_shapes=[
            pltpu.SemaphoreType.DMA,
            pltpu.SemaphoreType.DMA((count,)),
            pltpu.SemaphoreType.DMA((count,)),
        ],
        compiler_params=pltpu.CompilerParams(collective_id=number, has_side_effects=True),
        name=name,
    )(x)


def final_body(quads, lanes, count, *refs):
    inputs, outputs = refs[:count], refs[count : 2 * count]
    local, send, recv = refs[2 * count :]
    mover = Mover(send, recv, local)
    plane, planes = planes_of(lanes)
    here = ctx_place()
    devices = [all_at(lanes, quads, n) for n in range(4 * lanes * quads)]
    greet([device for device, _ in devices[1:]])
    me = plane * 2 * quads + here
    qkv, small = inputs[:2]
    copies = [(qkv.at[place], outputs[0].at[here], device) for device, place in
              [ctx_at(quads, n) for n in range(1, 2 * quads)]]
    for ref, out in zip(inputs[2:], outputs[2:]):
        copies += [(ref.at[place], out.at[plane], device) for device, place in planes]
    copies += [(small.at[place], outputs[1].at[me], device) for device, place in devices[1:]]
    started = [mover.copy(*c) for c in copies]
    mover.go(*started)
    mover.keep(qkv.at[here], outputs[0].at[here])
    mover.keep(small.at[me], outputs[1].at[me])
    for ref, out in zip(inputs[2:], outputs[2:]):
        mover.keep(ref.at[plane], out.at[plane])
    for c in started:
        c.wait_recv()
    mover.finish()


def final_exchange(qkv, small, planes):
    quads, lanes = lax.axis_size("quad"), lax.axis_size("lane")
    arrays = [qkv, small, *planes]
    sems = 2 * quads - 1 + 4 * lanes * quads - 1 + len(planes) * (2 * lanes - 1)
    vmem = pl.BlockSpec(memory_space=pltpu.VMEM)
    return pl.pallas_call(
        functools.partial(final_body, quads, lanes, len(arrays)),
        out_shape=[jax.ShapeDtypeStruct(x.shape, x.dtype) for x in arrays],
        in_specs=[vmem] * len(arrays),
        out_specs=[vmem] * len(arrays),
        scratch_shapes=[
            pltpu.SemaphoreType.DMA((len(arrays),)),
            pltpu.SemaphoreType.DMA((sems,)),
            pltpu.SemaphoreType.DMA((sems,)),
        ],
        compiler_params=pltpu.CompilerParams(collective_id=14, has_side_effects=True),
        name="final_exchange",
    )(*arrays)


def sum_body(quads, x_ref, out_ref, landed, send, recv):
    count = 2 * quads
    greet([ctx_at(quads, n)[0] for n in range(1, count)])
    started = []
    for n in range(1, count):
        c = pltpu.make_async_remote_copy(
            src_ref=x_ref, dst_ref=landed.at[n - 1], send_sem=send.at[n - 1],
            recv_sem=recv.at[n - 1], device_id=ctx_at(quads, n)[0], device_id_type=MESH,
        )
        c.start()
        started.append(c)
    for c in started:
        c.wait_recv()
    for j in range(count):
        total = x_ref[j]
        for n in range(1, count):
            total = total + landed[n - 1, j ^ n]
        out_ref[j] = total
    for c in started:
        c.wait_send()


def sum_ctx(x, name, number):
    quads = lax.axis_size("quad")
    count = 2 * quads - 1
    return pl.pallas_call(
        functools.partial(sum_body, quads),
        out_shape=jax.ShapeDtypeStruct(x.shape, x.dtype),
        in_specs=[pl.BlockSpec(memory_space=pltpu.VMEM)],
        out_specs=pl.BlockSpec(memory_space=pltpu.VMEM),
        scratch_shapes=[
            pltpu.VMEM((count,) + x.shape, x.dtype),
            pltpu.SemaphoreType.DMA((count,)),
            pltpu.SemaphoreType.DMA((count,)),
        ],
        compiler_params=pltpu.CompilerParams(collective_id=number, has_side_effects=True),
        name=name,
    )(x)


def nn(left, right):
    return lax.dot_general(left, right, (((1,), (0,)), ((), ())), preferred_element_type=F32)


def nt(left, right):
    return lax.dot_general(left, right, (((1,), (1,)), ((), ())), preferred_element_type=F32)


def tn(left, right):
    return lax.dot_general(left, right, (((0,), (0,)), ((), ())), preferred_element_type=F32)


def expert_body(quads, before, _, gate_ref, x_ref, go_ref, gp_ref, both_ref, down_ref, *refs):
    sums = refs[:2] if before else None
    moe_ref, d_ref, dgate_ref, hid_ref, dg_ref, du_ref = refs[-6:]
    t = pl.program_id(0)
    hidden, width = down_ref.shape
    x = x_ref[0, 0].reshape(-1, width)
    gate = gate_ref[0]
    wg = both_ref[:, 0].reshape(width, hidden)
    wu = both_ref[:, 1].reshape(width, hidden)
    wd = down_ref[...]

    g = jnp.where(t % 2 == 1, gp_ref[0, 0], go_ref[0]).reshape(-1, width)
    gate_pre = nn(x, wg)
    up_pre = nn(x, wu)
    d_hidden = nt(g, wd)
    sigma = 1.0 / (1.0 + jnp.exp(-gate_pre))
    silu = gate_pre * sigma
    hid = silu * up_pre
    dgate_ref[0] = jnp.sum(hid * d_hidden, axis=1, keepdims=True)
    d_hidden = d_hidden * gate
    scaled = (hid * gate).astype(BF)
    d_gate_pre = (d_hidden * up_pre * (sigma + silu * (1.0 - sigma))).astype(BF)
    d_up_pre = (d_hidden * silu).astype(BF)
    hid_ref[0] = scaled
    dg_ref[0] = d_gate_pre
    du_ref[0] = d_up_pre
    shape = moe_ref.shape[2:]
    moe = nn(scaled, wd).reshape(shape)
    d_rows = (nt(d_gate_pre, wg) + nt(d_up_pre, wu)).reshape(shape)
    if before:
        moe = moe + sums[0][0, 0].astype(F32)
        d_rows = d_rows + sums[1][0, 0].astype(F32)
    moe_ref[0, 0] = moe.astype(BF)
    d_ref[0, 0] = d_rows.astype(BF)


def expert(place, gates, x_rows, g_rows, both, down, before, name):
    _, quads, shards, rows, width = x_rows.shape
    batches = shards // 2
    hidden = down.shape[0]
    tiles = 4 * quads
    tile = batches * rows

    def row_block(t, p):
        return (t // (2 * quads), t // 2 % quads, t % 2, 0, 0)

    block = pl.BlockSpec((1, 1, batches, rows, width), row_block)
    saved_spec = pl.BlockSpec((1, tile, hidden), lambda t, p: (t, 0, 0))
    saved = jax.ShapeDtypeStruct((tiles, tile, hidden), BF)
    rows_shape = jax.ShapeDtypeStruct(x_rows.shape, BF)
    fixed = dict(pipeline_mode=pl.Buffered(1))
    column = pl.BlockSpec((1, tile, 1), lambda t, p: (t, 0, 0))
    return pl.pallas_call(
        functools.partial(expert_body, quads, bool(before)),
        out_shape=(rows_shape,) * 2
        + (jax.ShapeDtypeStruct((tiles, tile, 1), F32), saved, saved, saved),
        grid_spec=pltpu.PrefetchScalarGridSpec(
            num_scalar_prefetch=1,
            grid=(tiles,),
            in_specs=[
                column, block,
                pl.BlockSpec((1, batches, rows, width), lambda t, p: (p[t // 2], 0, 0, 0)),
                pl.BlockSpec(
                    (1, 1, batches, rows, width),
                    lambda t, p: (t // (2 * quads), t // 2 % quads, 0, 0, 0),
                ),
                pl.BlockSpec(both.shape, lambda t, p: (0, 0, 0, 0), **fixed),
                pl.BlockSpec(down.shape, lambda t, p: (0, 0), **fixed),
            ]
            + ([block] * 2 if before else []),
            out_specs=[block, block, column, saved_spec, saved_spec, saved_spec],
        ),
        input_output_aliases={7 + i: i for i in range(2)} if before else {},
        compiler_params=pltpu.CompilerParams(
            dimension_semantics=("arbitrary",), vmem_limit_bytes=60 << 20
        ),
        name=name,
    )(place, gates, x_rows, *g_rows, both, down, *before)


def grads_body(_, x_ref, go_ref, gp_ref, hid_ref, dg_ref, du_ref, both_ref, down_ref,
               gate_acc, up_acc, down_acc):
    t = pl.program_id(0)
    width = down_acc.shape[1]
    hidden = down_acc.shape[0]

    @pl.when(t == 0)
    def _():
        gate_acc[...] = jnp.zeros_like(gate_acc)
        up_acc[...] = jnp.zeros_like(up_acc)
        down_acc[...] = jnp.zeros_like(down_acc)

    x = x_ref[0, 0].reshape(-1, width)
    g = jnp.concatenate([go_ref[0].reshape(-1, width), gp_ref[0, 0].reshape(-1, width)], axis=0)
    gate_acc[...] += tn(x, dg_ref[...].reshape(-1, hidden))
    up_acc[...] += tn(x, du_ref[...].reshape(-1, hidden))
    down_acc[...] += tn(hid_ref[...].reshape(-1, hidden), g)

    @pl.when(t == pl.num_programs(0) - 1)
    def _():
        part = both_ref.shape[0]
        both_ref[:, 0] = gate_acc[...].astype(BF).reshape(part, -1, hidden)
        both_ref[:, 1] = up_acc[...].astype(BF).reshape(part, -1, hidden)
        down_ref[...] = down_acc[...].astype(BF)


def expert_grads(place, x_rows, g_rows, hid, dg, du, dp, name):
    _, quads, shards, rows, width = x_rows.shape
    batches = shards // 2
    tiles, tile, hidden = hid.shape

    saved = pl.BlockSpec((2, tile, hidden), lambda t, p: (t, 0, 0))

    def row_block(t, p):
        return (t // quads, t % quads, 0, 0, 0)

    return pl.pallas_call(
        grads_body,
        out_shape=(
            jax.ShapeDtypeStruct((dp, 2, width // dp, hidden), BF),
            jax.ShapeDtypeStruct((hidden, width), BF),
        ),
        grid_spec=pltpu.PrefetchScalarGridSpec(
            num_scalar_prefetch=1,
            grid=(tiles // 2,),
            in_specs=[
                pl.BlockSpec((1, 1, shards, rows, width), row_block),
                pl.BlockSpec((1, batches, rows, width), lambda t, p: (p[t], 0, 0, 0)),
                pl.BlockSpec((1, 1, batches, rows, width), row_block),
                saved, saved, saved,
            ],
            out_specs=[
                pl.BlockSpec((dp, 2, width // dp, hidden), lambda t, p: (0, 0, 0, 0)),
                pl.BlockSpec((hidden, width), lambda t, p: (0, 0)),
            ],
            scratch_shapes=[pltpu.VMEM((width, hidden), F32), pltpu.VMEM((width, hidden), F32),
                            pltpu.VMEM((hidden, width), F32)],
        ),
        compiler_params=pltpu.CompilerParams(
            dimension_semantics=("arbitrary",), vmem_limit_bytes=60 << 20
        ),
        name=name,
    )(place, x_rows, *g_rows, hid, dg, du)


def finish_body(lanes, *refs):
    gate_ref, up_ref = refs[-2:]
    for e, ref in enumerate(refs[:-2]):
        for kind, out_ref in enumerate((gate_ref, up_ref)):
            hidden = ref.shape[3]
            for h in range(2):
                total = ref[h * lanes, kind].astype(F32)
                for l in range(1, lanes):
                    total = total + ref[h * lanes + l, kind].astype(F32)
                out_ref[e, :, h * hidden : (h + 1) * hidden] = total


def finish_grads(parts):
    planes, _, depth, hidden = parts[0].shape
    step = 128
    shape = jax.ShapeDtypeStruct((len(parts), depth, 2 * hidden), F32)
    out_spec = pl.BlockSpec((len(parts), step, 2 * hidden), lambda i: (0, i, 0))
    return pl.pallas_call(
        functools.partial(finish_body, planes // 2),
        out_shape=(shape, shape),
        grid=(depth // step,),
        in_specs=[pl.BlockSpec((planes, 2, step, hidden), lambda i: (0, 0, i, 0))] * len(parts),
        out_specs=(out_spec, out_spec),
        name="finish_gradients",
    )(*parts)


def row_sums(values):
    ones = jnp.ones((8, values.shape[1]), F32)
    sums = lax.dot_general(
        ones, values, (((1,), (1,)), ((), ())), preferred_element_type=F32,
        precision=lax.Precision.HIGHEST,
    )
    return sums[:1]


def columns(values):
    turned = jnp.transpose(values)
    return jnp.concatenate([turned[:, i : i + 1] for i in range(values.shape[0])], axis=0)


def qkv_body(x_ref, gain_ref, w_ref, act_ref, pre_ref, square_ref):
    batches, rows, width = x_ref.shape[2:]
    head_width = w_ref.shape[1] // 3
    x = x_ref[0, 0].astype(F32).reshape(-1, width)
    root = lax.rsqrt(jnp.mean(x * x, axis=1, keepdims=True) + EPSILON)
    act = (x * root * gain_ref[...]).astype(BF)
    pre = nn(act, w_ref[...])
    pre_ref[:, 0] = pre.reshape(batches, rows, -1)
    for kind in range(2):
        part = pre[:, kind * head_width : (kind + 1) * head_width]
        sums = row_sums(part * part)
        for m in range(batches):
            i = kind * batches + m
            square_ref[0, i : i + 1] = sums[:, m * rows : (m + 1) * rows]
    act_ref[0, 0] = act.reshape(batches, rows, width)


def row_spec(quads, shape):
    return pl.BlockSpec((1, 1) + shape, lambda n: (n // quads, n % quads, 0, 0, 0))


def project(token_rows, gain, weights):
    _, quads, batches, rows, width = token_rows.shape
    total = weights.shape[1]
    fixed = dict(pipeline_mode=pl.Buffered(1))
    block = row_spec(quads, (batches, rows, width))
    return pl.pallas_call(
        qkv_body,
        out_shape=(
            jax.ShapeDtypeStruct(token_rows.shape, BF),
            jax.ShapeDtypeStruct((batches, 2 * quads, rows, total), F32),
            jax.ShapeDtypeStruct((2 * quads, 2 * batches, rows), F32),
        ),
        grid=(2 * quads,),
        in_specs=[
            block,
            pl.BlockSpec((1, width), lambda n: (0, 0)),
            pl.BlockSpec((width, total), lambda n: (0, 0), **fixed),
        ],
        out_specs=(
            block,
            pl.BlockSpec((batches, 1, rows, total), lambda n: (0, n, 0, 0)),
            pl.BlockSpec((1, 2 * batches, rows), lambda n: (n, 0, 0)),
        ),
        compiler_params=pltpu.CompilerParams(vmem_limit_bytes=40 << 20),
        name="project",
    )(token_rows, gain.reshape(1, width), weights)


def turned(values, cosine, sine):
    return values * cosine + pltpu.roll(values, HEAD // 2, 1) * sine


def turned_back(grad, cosine, sine):
    return grad * cosine - pltpu.roll(grad, HEAD // 2, 1) * sine


def head_probs(query, key, column, row, length):
    scores = nt(query, key) * (1.0 / math.sqrt(HEAD))
    scores = jnp.where((row <= column) & (row < length), scores, MASKED)
    expo = jnp.exp(scores - jnp.max(scores, axis=1, keepdims=True))
    return expo / jnp.sum(expo, axis=1, keepdims=True)


def attend_body(
    step, pre_ref, sum_ref, gain_ref, cos_ref, sin_ref, column_ref, row_ref, length_ref,
    query_ref, key_ref, value_ref, out_ref, att,
):
    m = pl.program_id(0)
    places, rows = pre_ref.shape[1:3]
    slot = places * rows
    head_width = query_ref.shape[2]
    cosine, sine = cos_ref[...], sin_ref[...]
    pre = pre_ref[0].reshape(slot, 3 * head_width)
    for kind, ref in enumerate((query_ref, key_ref)):
        root = lax.rsqrt(columns(sum_ref[0, kind]) / (head_width * places) + EPSILON)
        part = pre[:, kind * head_width : (kind + 1) * head_width] * root * gain_ref[kind]
        for h in range(head_width // HEAD):
            here = slice(h * HEAD, (h + 1) * HEAD)
            ref[0, :, here] = turned(part[:, here], cosine, sine).astype(BF)
    value_ref[0] = pre[:, 2 * head_width :].astype(BF)
    length = length_ref[m]
    row = row_ref[...]
    for h in range(head_width // HEAD):
        here = slice(h * HEAD, (h + 1) * HEAD)

        @pl.loop(0, slot // step)
        def _(i):
            part = pl.ds(pl.multiple_of(i * step, step), step)
            probs = head_probs(query_ref[0, part, here], key_ref[0, :, here], column_ref[part], row, length)
            att[part, here] = nn(probs.astype(BF), value_ref[0, :, here]).astype(BF)

    out_ref[:, 0] = att[...].reshape(places, rows, head_width)


def attend(pre, sums, gains, cosine, sine, column, row, lengths):
    batches, places, rows, total = pre.shape
    head_width, slot = total // 3, places * rows
    saved = jax.ShapeDtypeStruct((batches, slot, head_width), BF)
    saved_spec = pl.BlockSpec((1, slot, head_width), lambda m: (m, 0, 0))
    return pl.pallas_call(
        functools.partial(attend_body, 256),
        out_shape=(saved,) * 3
        + (jax.ShapeDtypeStruct((places, batches, rows, head_width), BF),),
        grid=(batches,),
        in_specs=[
            pl.BlockSpec((1,) + pre.shape[1:], lambda m: (m, 0, 0, 0)),
            pl.BlockSpec((1,) + sums.shape[1:], lambda m: (m, 0, 0, 0)),
            pl.BlockSpec(gains.shape, lambda m: (0, 0, 0)),
            pl.BlockSpec(cosine.shape, lambda m: (0, 0)),
            pl.BlockSpec(sine.shape, lambda m: (0, 0)),
            pl.BlockSpec(column.shape, lambda m: (0, 0)),
            pl.BlockSpec(row.shape, lambda m: (0, 0)),
            pl.BlockSpec(memory_space=pltpu.SMEM),
        ],
        out_specs=(saved_spec,) * 3
        + (pl.BlockSpec((places, 1, rows, head_width), lambda m: (0, m, 0, 0)),),
        scratch_shapes=[pltpu.VMEM((slot, head_width), BF)],
        compiler_params=pltpu.CompilerParams(vmem_limit_bytes=60 << 20),
        name="attend",
    )(pre, sums, gains, cosine, sine, column, row, lengths)


def attend_back_body(
    step, query_ref, key_ref, value_ref, datt_ref, pre_ref, sum_ref, gain_ref, cos_ref, sin_ref,
    column_ref, row_ref, length_ref, dn_ref, dv_ref, inner_ref, dgain_ref, att, dq, dk, dv,
):
    m = pl.program_id(0)
    places, rows = pre_ref.shape[1:3]
    slot = places * rows
    head_width = query_ref.shape[2]
    factor = 1.0 / math.sqrt(HEAD)
    att[...] = datt_ref[:, 0].reshape(slot, head_width)
    length = length_ref[m]
    row = row_ref[...]
    dk[...] = jnp.zeros_like(dk)
    dv[...] = jnp.zeros_like(dv)
    for h in range(head_width // HEAD):
        here = slice(h * HEAD, (h + 1) * HEAD)

        @pl.loop(0, slot // step)
        def _(i):
            part = pl.ds(pl.multiple_of(i * step, step), step)
            query, grad = query_ref[0, part, here], att[part, here]
            probs = head_probs(query, key_ref[0, :, here], column_ref[part], row, length)
            d_probs = nt(grad, value_ref[0, :, here])
            inner = jnp.sum(probs * d_probs, axis=1, keepdims=True)
            d_scores = (probs * (d_probs - inner)).astype(BF)
            dq[part, here] = nn(d_scores, key_ref[0, :, here]) * factor
            dk[:, here] += tn(d_scores, query) * factor
            dv[:, here] += tn(probs.astype(BF), grad)

    dv_ref[0] = dv[...].astype(BF)
    cosine, sine = cos_ref[...], sin_ref[...]
    for kind, ref in enumerate((dq, dk)):
        root = lax.rsqrt(columns(sum_ref[0, kind]) / (head_width * places) + EPSILON)
        for h in range(head_width // HEAD):
            here = slice(h * HEAD, (h + 1) * HEAD)
            ref[:, here] = turned_back(ref[:, here], cosine, sine)
        grad = ref[...]
        pre = pre_ref[0, :, :, kind * head_width : (kind + 1) * head_width].reshape(slot, head_width)
        product = grad * pre
        gain_part = jnp.sum(product * root, axis=0, keepdims=True)
        before = jnp.where(m == 0, jnp.zeros_like(gain_part), dgain_ref[kind])
        dgain_ref[kind] = before + gain_part
        weighted = grad * gain_ref[kind]
        dn_ref[0, kind] = weighted
        sums = row_sums(product * gain_ref[kind])
        for n in range(places):
            inner_ref[0, kind, n : n + 1] = sums[:, n * rows : (n + 1) * rows]


def attend_back(saved, d_att, pre, sums, gains, cosine, sine, column, row, lengths):
    batches, places, rows, total = pre.shape
    head_width, slot = total // 3, places * rows
    saved_spec = pl.BlockSpec((1, slot, head_width), lambda m: (m, 0, 0))
    return pl.pallas_call(
        functools.partial(attend_back_body, 256),
        out_shape=(
            jax.ShapeDtypeStruct((batches, 2, slot, head_width), F32),
            jax.ShapeDtypeStruct((batches, slot, head_width), BF),
            jax.ShapeDtypeStruct(sums.shape, F32),
            jax.ShapeDtypeStruct(gains.shape, F32),
        ),
        grid=(batches,),
        in_specs=[saved_spec] * 3
        + [
            pl.BlockSpec((places, 1, rows, head_width), lambda m: (0, m, 0, 0)),
            pl.BlockSpec((1,) + pre.shape[1:], lambda m: (m, 0, 0, 0)),
            pl.BlockSpec((1,) + sums.shape[1:], lambda m: (m, 0, 0, 0)),
            pl.BlockSpec(gains.shape, lambda m: (0, 0, 0)),
            pl.BlockSpec(cosine.shape, lambda m: (0, 0)),
            pl.BlockSpec(sine.shape, lambda m: (0, 0)),
            pl.BlockSpec(column.shape, lambda m: (0, 0)),
            pl.BlockSpec(row.shape, lambda m: (0, 0)),
            pl.BlockSpec(memory_space=pltpu.SMEM),
        ],
        out_specs=(
            pl.BlockSpec((1, 2, slot, head_width), lambda m: (m, 0, 0, 0)),
            saved_spec,
            pl.BlockSpec((1,) + sums.shape[1:], lambda m: (m, 0, 0, 0)),
            pl.BlockSpec(gains.shape, lambda m: (0, 0, 0)),
        ),
        scratch_shapes=[pltpu.VMEM((slot, head_width), BF)]
        + [pltpu.VMEM((slot, head_width), F32)] * 3,
        compiler_params=pltpu.CompilerParams(vmem_limit_bytes=60 << 20),
        name="attend_back",
    )(*saved, d_att, pre, sums, gains, cosine, sine, column, row, lengths)


def back_body(
    quads, dn_ref, dv_ref, pre_ref, sum_ref, inner_ref, act_ref, w_ref, d_ref, dw_ref, dw, cols,
):
    n = pl.program_id(0)
    batches, _, rows, head_width = dn_ref.shape
    width = w_ref.shape[0]
    total = head_width * 2 * quads
    for m in range(batches):
        here = pl.ds(m * rows, rows)
        for kind in range(2):
            root = lax.rsqrt(columns(sum_ref[0, m, kind]) / total + EPSILON)
            inner = columns(inner_ref[0, m, kind]) / total
            part = slice(kind * head_width, (kind + 1) * head_width)
            pre = pre_ref[m, 0, :, part]
            grad = root * dn_ref[m, kind] - pre * (root * root * root) * inner
            cols[here, part] = grad.astype(BF)
        cols[here, 2 * head_width :] = dv_ref[m]
    d_pre = cols[...]
    act = act_ref[0, 0].reshape(-1, width)
    d_ref[0, 0] = nt(d_pre, w_ref[...]).astype(BF).reshape(batches, rows, width)
    part = tn(act, d_pre)

    @pl.when(n == 0)
    def _():
        dw[...] = part

    @pl.when(n > 0)
    def _():
        dw[...] += part

    @pl.when(n == pl.num_programs(0) - 1)
    def _():
        dw_ref[...] = dw[...].astype(BF)


def project_back(d_norm, d_value, pre, sums, inners, act, weights):
    batches, places, rows, total = pre.shape
    quads, width, head_width = places // 2, weights.shape[0], total // 3
    fixed = dict(pipeline_mode=pl.Buffered(1))
    block = row_spec(quads, (batches, act.shape[3], width))
    sums = sums.transpose(2, 0, 1, 3)[:, :, :, None]
    inners = inners[:, :, :, None]
    small = pl.BlockSpec((1, batches, 2, 1, rows), lambda n: (n, 0, 0, 0, 0))
    return pl.pallas_call(
        functools.partial(back_body, quads),
        out_shape=(
            jax.ShapeDtypeStruct(act.shape, BF), jax.ShapeDtypeStruct(weights.shape, BF),
        ),
        grid=(places,),
        in_specs=[
            pl.BlockSpec((batches, 2, rows, head_width), lambda n: (0, 0, n, 0)),
            pl.BlockSpec((batches, rows, head_width), lambda n: (0, n, 0)),
            pl.BlockSpec((batches, 1, rows, total), lambda n: (0, n, 0, 0)),
            small, small, block,
            pl.BlockSpec(weights.shape, lambda n: (0, 0), **fixed),
        ],
        out_specs=(block, pl.BlockSpec(weights.shape, lambda n: (0, 0))),
        scratch_shapes=[
            pltpu.VMEM(weights.shape, F32), pltpu.VMEM((batches * rows, total), BF)
        ],
        compiler_params=pltpu.CompilerParams(vmem_limit_bytes=60 << 20),
        name="project_back",
    )(d_norm, d_value, pre, sums, inners, act, weights)


def scatter_all(kinds, partners, name, number, extra=()):
    if kinds[0].shape[1] == 4:
        return scatter_rows(kinds, partners, name, number, extra)
    sums = []
    for i, (kind, partner) in enumerate(zip(kinds, partners)):
        count = kind.shape[2] // 2 if partner else kind.shape[2]
        parts = [
            scatter_rows([kind[:, :, m::count]], (partner,), name, number + 8 * i)[0]
            for m in range(count)
        ]
        sums.append(jnp.concatenate(parts))
    return sums + [exchange(blocks, DP) for blocks in extra]


def on_device(
    tokens,
    cotangent,
    routes,
    lengths,
    block_order,
    w_query,
    w_key,
    w_value,
    w_out,
    w_router,
    w_gate,
    w_up,
    w_down,
    attn_gain,
    mlp_gain,
    query_gain,
    key_gain,
):
    batches, _, rows, width = tokens.shape
    dp_size = lax.axis_size(DP)
    ctx_size = lax.axis_size(CTX)
    quads = lax.axis_size("quad")
    lanes = lax.axis_size("lane")
    slot_len = rows * ctx_size
    block_rows = rows // 2
    head_width = width // ctx_size
    shard = w_query.shape[0]
    expert_count = w_router.shape[1]
    local_experts = w_gate.shape[0]
    hidden_units = w_gate.shape[2]
    hidden_half = hidden_units // 2
    depth_part = w_gate.shape[1]
    pair = lax.axis_index("pair")

    qkv = jnp.stack([w_query, w_key, w_value], axis=1).reshape(shard, 3, ctx_size, head_width)
    qkv = qkv.transpose(2, 0, 1, 3).reshape(ctx_size, shard, 3 * head_width)
    small = jnp.concatenate(
        [attn_gain, mlp_gain, query_gain, key_gain, w_router.reshape(shard * expert_count)]
    )
    grad_low = cotangent[:, 0]
    token_rows, qkv_w, small, out_w = start_gather(
        tokens[:, 0], qkv, small.reshape(1, -1), w_out
    )
    out_w = lax.all_gather(out_w, CTX, axis=1, tiled=False).reshape(width, width)
    qkv_w = qkv_w.reshape(width, 3 * head_width)
    small = small.reshape(dp_size * ctx_size, -1)
    gain_attn = small[:, :shard].reshape(width).astype(F32)
    gain_mlp = small[:, shard : 2 * shard].reshape(width).astype(F32)
    gain_query = small[:, 2 * shard : 3 * shard].reshape(ctx_size, head_width)
    gain_key = small[:, 3 * shard : 4 * shard].reshape(ctx_size, head_width)
    router_w = small[:, 4 * shard :].reshape(width, expert_count)
    here = lax.axis_index(CTX)
    gain_query = lax.dynamic_index_in_dim(gain_query, here, 0, keepdims=False).astype(F32)
    gain_key = lax.dynamic_index_in_dim(gain_key, here, 0, keepdims=False).astype(F32)

    w_gate, w_up, w_down, crossing, qkv_w = lax.optimization_barrier(
        (w_gate, w_up, w_down, grad_low, qkv_w)
    )
    halves = [
        jnp.stack(
            [
                jnp.stack([w_gate[e, :, part], w_up[e, :, part]])
                for part in (slice(0, hidden_half), slice(hidden_half, hidden_units))
            ]
        )
        for e in range(local_experts)
    ]
    halves = [jnp.repeat(part, lanes, axis=0) for part in halves]
    next_w = exchange(halves[0], DP)
    down_parts = lane_parts(w_down)
    g_own = lax.all_gather(crossing, CTX, axis=0, tiled=False)

    def places_of(device):
        stored = device * rows + jnp.arange(rows, dtype=jnp.int32)
        match_marks = (stored // block_rows)[:, None] == jnp.arange(
            block_order.shape[0], dtype=jnp.int32
        )[None, :]
        first_place = jnp.sum(jnp.where(match_marks, block_order[None, :], 0), axis=1)
        return first_place * block_rows + stored % block_rows

    places = jnp.concatenate(
        [
            places_of((lax.axis_index("quad") ^ k) * 2 + (pair ^ other))
            for other in range(2)
            for k in range(quads)
        ]
    )
    cosine, sine = angles(places, HEAD)
    expert_range = jnp.arange(expert_count, dtype=jnp.int32)

    inputs = tokens[:, 0].astype(F32)
    attn_root = inv_rms(inputs)
    act, pre, squares = project(token_rows, gain_attn, qkv_w)
    squares = sum_ctx(squares, "sum_squares", 6)
    squares, crossing = lax.optimization_barrier((squares, crossing))
    crossing = swap(crossing, "half")
    squares = squares.reshape(2 * quads, 2, batches, rows).transpose(2, 1, 0, 3)
    qk_gains = jnp.stack([gain_query, gain_key])[:, None]
    signed = jnp.where(jnp.arange(HEAD) < HEAD // 2, -sine[:, 0], sine[:, 0])
    context = (pre, squares, qk_gains, cosine[:, 0], signed, places[:, None], places[None, :])
    context = context + (lengths[:, 0],)
    *saved, attended = attend(*context)
    attended = exchange_rows(attended[None], "inward", "attended_to_rows", 7)[0]
    attended, next_w = lax.optimization_barrier((attended, next_w))
    attended = attended.transpose(1, 2, 0, 3).reshape(batches, rows, width)
    x_mid = inputs + dot("mtd,de->mte", attended, out_w)
    mlp_root = inv_rms(x_mid)
    mixed_in = (x_mid * mlp_root * gain_mlp).astype(BF)
    router = jax.nn.softmax(dot("mtd,de->mte", mixed_in, router_w), axis=-1)
    routed = jnp.any(routes[:, 0, :, :, None] == expert_range, axis=2).astype(F32)
    gates = (router * routed).transpose(2, 0, 1).reshape(ctx_size, local_experts, batches, rows)
    x_rows, cross_rows = gather_rows([mixed_in, crossing], ("both", "own"), "gather_mixed", 2)
    gates, x_rows = lax.optimization_barrier((gates, x_rows))
    gates = exchange_rows(gates, "outward", "gates_to_experts", 8, 2)
    g_rows = (g_own, cross_rows)
    gates = gates.transpose(1, 0, 3, 4, 2).reshape(4 * quads, batches * rows, local_experts)
    number = jnp.arange(2 * quads, dtype=jnp.int32)
    place = (lax.axis_index("quad") ^ (number % quads)) * 2 + (pair ^ (number // quads))
    x_rows, next_w, down_parts, halves, gates = lax.optimization_barrier(
        (x_rows, next_w, down_parts, halves, gates)
    )
    down_w = gather_lane(w_down, down_parts).swapaxes(0, 1)
    down_w = down_w.reshape(local_experts, hidden_half, width)

    sums = ()
    d_gates, grads_both, grads_down = [], [], []
    for e in range(local_experts):
        both_w = next_w
        if e < local_experts - 1:
            next_w = exchange(halves[e + 1], DP)
        *sums, d_gate, hid, d_gate_pre, d_up_pre = expert(
            place, gates[..., e : e + 1], x_rows, g_rows, both_w, down_w[e], tuple(sums),
            f"expert_{e}",
        )
        d_gates.append(d_gate)
        grad_both, grad_down = expert_grads(
            place, x_rows, g_rows, hid, d_gate_pre, d_up_pre, dp_size, f"expert_grads_{e}"
        )
        sums[0], grad_both, next_w = lax.optimization_barrier((sums[0], grad_both, next_w))
        grads_both.append(exchange(grad_both, DP) if e < local_experts - 1 else grad_both)
        grads_down.append(grad_down)
    moe_rows, d_rows = sums
    done, grads_down, d_rows = lax.optimization_barrier((grads_both[:-1], grads_down, d_rows))
    grads_both[:-1] = done
    grads_down = jnp.stack(grads_down)
    grads_down = grads_down.reshape(local_experts, lanes, -1, width).swapaxes(0, 1)
    lane = lax.axis_index("lane")
    down_others = [
        lax.ppermute(
            lax.dynamic_index_in_dim(grads_down, lane ^ d, 0, keepdims=False),
            "lane", [(i, i ^ d) for i in range(lanes)],
        )
        for d in range(1, lanes)
    ]
    d_mixed, moe_sum = scatter_all(
        [d_rows, moe_rows], (True, True), "scatter_experts", 24
    )
    d_gates = jnp.concatenate(d_gates, axis=-1)
    d_gates = d_gates.reshape(2 * quads, 2, batches, rows, local_experts)
    d_gates = d_gates.transpose(1, 0, 4, 2, 3)
    d_gates, d_mixed, down_others = lax.optimization_barrier((d_gates, d_mixed, down_others))
    d_router = exchange_rows(d_gates, "inward", "gate_gradients", 9, 2)
    d_router, last_both = lax.optimization_barrier((d_router, grads_both[-1]))
    grads_both[-1] = exchange(last_both, DP)
    d_router = jnp.sum(d_router, axis=0).reshape(expert_count, batches, rows)
    d_router = d_router.transpose(1, 2, 0) * routed
    d_logits = (
        router * (d_router - jnp.sum(router * d_router, axis=-1, keepdims=True))
    ).astype(BF)
    d_mixed = d_mixed + dot("mte,de->mtd", d_logits, router_w)

    def norm_back_all(values, root, gain, grad):
        d_values, d_gain = norm_back(values, root, gain, grad)
        return d_values, jnp.sum(d_gain, axis=0)

    d_mid, part_mlp_gain = norm_back_all(x_mid, mlp_root, gain_mlp, d_mixed)
    d_mid = d_mid + grad_low.astype(F32)
    d_att_out = d_mid.astype(BF)
    grad_out = dot("mtd,mte->de", attended, d_att_out).astype(BF)
    d_attended = dot("mte,de->mtd", d_att_out, out_w).astype(BF)
    beside = quads == 4 and dp_size * shard == batches * rows
    if not beside:
        grad_out = lax.psum_scatter(grad_out, ALL, scatter_dimension=0, tiled=True).astype(F32)
    d_attended = d_attended.reshape(batches, rows, ctx_size, head_width).transpose(2, 0, 1, 3)
    d_attended = exchange_rows(d_attended, "outward", "attended_gradients", 10)[0]
    d_norm, d_value, inners, d_gains = attend_back(saved, d_attended, *context)
    inners = inners.transpose(2, 0, 1, 3).reshape(2 * quads, 2 * batches, rows)
    inners = sum_ctx(inners, "sum_inner", 11).reshape(2 * quads, batches, 2, rows)
    d_act, grad_qkv = project_back(d_norm, d_value, pre, squares, inners, act, qkv_w)
    grad_qkv = grad_qkv.reshape(dp_size, -1, 3 * head_width)
    kinds = [d_act]
    if beside:
        kinds.append(grad_out.reshape(dp_size, ctx_size, shard, width))
    d_act, *grad_planes, grad_qkv = scatter_all(
        kinds, (False,) * len(kinds), "scatter_act", 25, (grad_qkv,)
    )
    d_inputs, part_attn_gain = norm_back_all(inputs, attn_root, gain_attn, d_act)
    mixed = (x_mid + moe_sum).astype(BF)

    grad_gate, grad_up = finish_grads(grads_both)
    grad_down = lax.dynamic_index_in_dim(grads_down, lane, 0, keepdims=False).astype(F32)
    for part in down_others:
        grad_down = grad_down + part.astype(F32)

    grad_qkv = jnp.sum(grad_qkv.astype(F32), axis=0).astype(BF)
    grad_qkv = grad_qkv.reshape(ctx_size, shard, 3 * head_width)
    grad_planes = [part.reshape(dp_size, shard, width).astype(BF) for part in grad_planes]
    grad_router = dot("mtd,mte->de", mixed_in, d_logits)
    columns = jnp.arange(ctx_size, dtype=jnp.int32)[:, None] == here

    def placed(part):
        return jnp.where(columns, part[None, :], 0.0).reshape(width)

    gains = jnp.stack(
        [part_attn_gain, part_mlp_gain, placed(d_gains[0, 0]), placed(d_gains[1, 0])]
    )
    gains = gains.reshape(4, dp_size, ctx_size, shard).transpose(1, 2, 0, 3)
    packed = jnp.concatenate(
        [
            gains.reshape(dp_size * ctx_size, 1, 4 * shard),
            grad_router.reshape(dp_size * ctx_size, 1, shard * expert_count),
        ],
        axis=2,
    )
    grad_qkv, packed, *grad_planes = final_exchange(grad_qkv, packed, grad_planes)
    packed = jnp.sum(packed, axis=(0, 1))
    grad_qkv = grad_qkv.astype(F32)
    if beside:
        grad_out = jnp.sum(grad_planes[0].astype(F32), axis=0)
    grad_qkv = grad_qkv.reshape(ctx_size, shard, 3, head_width).transpose(2, 1, 0, 3)
    grad_qkv = grad_qkv.reshape(3, shard, width)

    return (
        mixed[:, None],
        (d_inputs + d_mid)[:, None],
        grad_qkv[0],
        grad_qkv[1],
        grad_qkv[2],
        grad_out,
        packed[4 * shard :].reshape(shard, expert_count),
        grad_gate,
        grad_up,
        grad_down,
        packed[:shard],
        packed[shard : 2 * shard],
        packed[2 * shard : 3 * shard],
        packed[3 * shard : 4 * shard],
    )


def solution(mesh):
    dp_size, ctx_size = mesh.shape["dp"], mesh.shape["ctx"]
    grid = Mesh(mesh.devices.reshape(2, dp_size // 2, ctx_size // 2, 2), ALL)
    rows = P(None, DP, CTX, None)
    dense = P(ALL, None)
    expert = P(CTX, DP, None)
    vector = P(ALL)
    return jax.shard_map(
        on_device,
        mesh=grid,
        in_specs=(rows, rows, rows, P(None, DP), P())
        + (dense,) * 5
        + (expert,) * 3
        + (vector,) * 4,
        out_specs=(rows, rows) + (dense,) * 5 + (expert,) * 3 + (vector,) * 4,
        check_vma=False,
    )
```

```python
import functools
import math

import jax
import jax.numpy as jnp
from jax import lax
from jax.experimental import pallas as pl
from jax.experimental.pallas import tpu as pltpu
from jax.sharding import Mesh
from jax.sharding import PartitionSpec as P

HEAD = 128
EPSILON = 1e-05
ROPE_BASE = 10000.0
MASKED = -1e30
BF = jnp.bfloat16
F32 = jnp.float32
DP = ("half", "lane")
CTX = ("quad", "pair")
ALL = DP + CTX
MESH = pl.DeviceIdType.MESH


def dot(spec, left, right):
    return jnp.einsum(spec, left, right, preferred_element_type=F32)


def inv_rms(values):
    return lax.rsqrt(jnp.mean(values * values, axis=-1, keepdims=True) + EPSILON)


def norm_back(values, inv_root, gain_vec, grad_in):
    weighted = grad_in * gain_vec
    inner = jnp.mean(weighted * values, axis=-1, keepdims=True)
    grad_values = inv_root * weighted - values * (inv_root * inv_root * inv_root) * inner
    return (grad_values, jnp.sum(grad_in * values * inv_root, axis=0))


def angles(places, head_width):
    index = jnp.arange(head_width // 2, dtype=F32)
    freqs = jnp.power(ROPE_BASE, -2.0 * index / head_width)
    turning = places.astype(F32)[:, None] * freqs[None, :]
    turning = jnp.concatenate([turning, turning], axis=1)
    return (jnp.cos(turning)[:, None, :], jnp.sin(turning)[:, None, :])


def swap(values, axis):
    return lax.ppermute(values, axis, [(0, 1), (1, 0)])


def exchange(blocks, axes):
    return lax.all_to_all(blocks, axes, split_axis=0, concat_axis=0, tiled=True)


def lane_parts(values):
    if lax.axis_size("lane") == 2:
        return swap(values, "lane")
    return lax.all_gather(values, "lane", axis=0, tiled=False)


def gather_lane(values, parts):
    if lax.axis_size("lane") == 2:
        first = lax.axis_index("lane") == 0
        return jnp.stack([jnp.where(first, values, parts), jnp.where(first, parts, values)])
    return parts


def toggled(index, bits):
    step = 1
    while step <= bits:
        if bits & step:
            index = index + step - 2 * step * ((index // step) % 2)
        step *= 2
    return index


def greet(peers):
    barrier = pltpu.get_barrier_semaphore()
    for peer in peers:
        pl.semaphore_signal(barrier, inc=1, device_id=peer, device_id_type=MESH)
    pl.semaphore_wait(barrier, len(peers))


class Mover:
    def __init__(self, send, recv, local):
        self.send, self.recv, self.local = send, recv, local
        self.number, self.local_number = 0, 0
        self.sent, self.kept = [], []

    def copy(self, src, dst, device):
        i = self.number
        self.number += 1
        return pltpu.make_async_remote_copy(
            src_ref=src, dst_ref=dst, send_sem=self.send.at[i], recv_sem=self.recv.at[i],
            device_id=device, device_id_type=MESH,
        )

    def go(self, *copies):
        for c in copies:
            c.start()
            self.sent.append(c)

    def keep(self, src, dst):
        c = pltpu.make_async_copy(src, dst, self.local.at[self.local_number])
        self.local_number += 1
        c.start()
        self.kept.append(c)
        return c

    def finish(self):
        for c in self.sent:
            c.wait_send()
        for c in self.kept:
            c.wait()


class Spread:
    def __init__(self, mover, quads, src, slot):
        self.mover, self.quads = mover, quads
        quad = lax.axis_index("quad")
        to_quad = [{"quad": toggled(quad, k)} for k in range(quads)]
        sibling = {"pair": 1 - lax.axis_index("pair")}
        rows = src.shape[0]
        halves = (("a", pl.ds(0, rows // 2)), ("b", pl.ds(rows // 2, rows // 2)))
        p = {"o0": mover.copy(src, slot(1, 0, 0), sibling)}
        if quads == 4:
            for k in (1, 2):
                for name, part in halves:
                    p[f"s{k}{name}"] = mover.copy(
                        src.at[part], slot(0, k, 0).at[part], to_quad[k]
                    )
            for k, (name, part) in zip((1, 2), halves):
                p[f"f3{name}"] = mover.copy(
                    slot(0, k, k).at[part], slot(0, 3, k).at[part], to_quad[3 - k]
                )
            for k in (1, 2, 3):
                for name, part in halves:
                    p[f"o{k}{name}"] = mover.copy(
                        slot(0, k, k).at[part], slot(1, k, k).at[part], sibling
                    )
        else:
            for k in range(1, quads):
                p[f"s{k}"] = mover.copy(src, slot(0, k, 0), to_quad[k])
                p[f"o{k}"] = mover.copy(slot(0, k, k), slot(1, k, k), sibling)
        self.copies = p

    @staticmethod
    def count(quads):
        return 13 if quads == 4 else 2 * quads - 1

    def begin(self):
        names = [f"s{k}" for k in range(1, self.quads)]
        if self.quads == 4:
            names = ["s1a", "s2b", "s1b", "s2a"]
        self.mover.go(*[self.copies[name] for name in names + ["o0"]])

    def forward(self):
        p = self.copies
        steps = [(f"s{k}", (f"o{k}",)) for k in range(1, self.quads)]
        if self.quads == 4:
            steps = [
                ("s1a", ("f3a", "o1a")), ("s2b", ("f3b", "o2b")), ("s1b", ("o1b",)),
                ("s2a", ("o2a",)), ("f3a", ("o3a",)), ("f3b", ("o3b",)),
            ]
        for name, then in steps:
            p[name].wait_recv()
            self.mover.go(*[p[t] for t in then])

    def arrive(self):
        for name, c in self.copies.items():
            if name[0] == "o":
                c.wait_recv()


def relative_slots(ref, s):
    return lambda core, kr, km: ref.at[core, kr, s]


def ctx_peers(quads):
    return [ctx_at(quads, n)[0] for n in range(1, 2 * quads)]


def planes_of(lanes):
    half, lane = lax.axis_index("half"), lax.axis_index("lane")
    result = []
    for n in range(1, 2 * lanes):
        h, l = toggled(half, n // lanes), toggled(lane, n % lanes)
        result.append(({"half": h, "lane": l}, h * lanes + l))
    return half * lanes + lane, result


def gather_body(quads, partners, *refs):
    inputs = refs[: len(partners)]
    refs = refs[len(partners) :]
    outputs = refs[: len(partners)]
    refs = refs[len(partners) :]
    keeps = {}
    for i, partner in enumerate(partners):
        if partner != "own":
            keeps[i], refs = refs[0], refs[1:]
    local, send, recv = refs
    mover = Mover(send, recv, local)
    across = {"half": 1 - lax.axis_index("half")}
    quad = lax.axis_index("quad")
    peers = [{"quad": toggled(quad, k)} for k in range(1, quads)]
    peers.append({"pair": 1 - lax.axis_index("pair")})
    greet(peers + ([across] if keeps else []))

    def add(sources, i, offset):
        plans = []
        for s, src in enumerate(sources):
            p = Spread(mover, quads, src, relative_slots(outputs[i], offset + s))
            p.begin()
            plans.append(p)
            mover.keep(src, outputs[i].at[0, 0, offset + s])
        return plans

    crossing = {}
    for i, keep in keeps.items():
        crossing[i] = [
            mover.copy(inputs[i].at[s], keep.at[s], across) for s in range(inputs[i].shape[0])
        ]
        mover.go(*crossing[i])
    plans = []
    for i, ref in enumerate(inputs):
        if partners[i] == "partner":
            continue
        plans += add([ref.at[s] for s in range(ref.shape[0])], i, 0)
    for p in plans:
        p.forward()
    late = []
    for i, keep in keeps.items():
        for c in crossing[i]:
            c.wait_recv()
        offset = keep.shape[0] if partners[i] == "both" else 0
        added = add([keep.at[s] for s in range(keep.shape[0])], i, offset)
        for p in added:
            p.forward()
        late += added
    for p in plans + late:
        p.arrive()
    mover.finish()


def gather_rows(sources, partners, name, number):
    quads = lax.axis_size("quad")
    shapes, keeps = [], []
    sems = total = 0
    for x, partner in zip(sources, partners):
        count = x.shape[0] * (2 if partner == "both" else 1)
        total += count
        sems += count * Spread.count(quads) + (x.shape[0] if partner != "own" else 0)
        shapes.append(jax.ShapeDtypeStruct((2, quads, count) + x.shape[1:], x.dtype))
        if partner != "own":
            keeps.append(pltpu.VMEM(x.shape, x.dtype))
    return pl.pallas_call(
        functools.partial(gather_body, quads, partners),
        out_shape=shapes,
        in_specs=[pl.BlockSpec(memory_space=pltpu.VMEM)] * len(sources),
        out_specs=[pl.BlockSpec(memory_space=pl.ANY)] * len(shapes),
        scratch_shapes=keeps
        + [
            pltpu.SemaphoreType.DMA((total,)),
            pltpu.SemaphoreType.DMA((sems,)),
            pltpu.SemaphoreType.DMA((sems,)),
        ],
        compiler_params=pltpu.CompilerParams(collective_id=number, has_side_effects=True),
        name=name,
    )(*sources)


def start_body(
    quads, lanes, tok_ref, qkv_ref, small_ref, wout_ref,
    tok_out, qkv_out, small_out, wout_out, local, send, recv,
):
    mover = Mover(send, recv, local)
    half, lane = lax.axis_index("half"), lax.axis_index("lane")
    plane, here = half * lanes + lane, ctx_place()
    partner = (1 - half) * lanes + lane
    across = {"half": 1 - half}
    devices = 4 * lanes * quads
    others = [all_at(lanes, quads, n)[0] for n in range(1, devices)]
    greet(others)
    mine = mover.keep(small_ref, small_out.at[plane * 2 * quads + here])
    shared = [mover.copy(small_ref, small_out.at[plane * 2 * quads + here], d) for d in others]
    mover.go(*shared)

    def planes(src, view):
        first = mover.copy(src, view(plane), across)
        rest = [
            mover.copy(src, view(plane), {"lane": toggled(lane, d)}) for d in range(1, lanes)
        ]
        then = [
            mover.copy(view(partner), view(partner), {"lane": toggled(lane, d)})
            for d in range(1, lanes)
        ]
        mover.go(first, *rest)
        return first, rest, then

    mover.keep(wout_ref, wout_out.at[plane])
    w_first, w_rest, w_then = planes(wout_ref, lambda p: wout_out.at[p])
    kept = mover.keep(qkv_ref.at[here], qkv_out.at[plane, here])
    columns = []
    for n in range(1, 2 * quads):
        device, place = ctx_at(quads, n)
        columns.append(mover.copy(qkv_ref.at[place], qkv_out.at[plane, here], device))
    mover.go(*columns)
    tokens = []
    for s in range(tok_ref.shape[0]):
        p = Spread(mover, quads, tok_ref.at[s], relative_slots(tok_out, s))
        p.begin()
        tokens.append(p)
        mover.keep(tok_ref.at[s], tok_out.at[0, 0, s])
    for c in columns:
        c.wait_recv()
    kept.wait()
    mover.kept = [c for c in mover.kept if c is not kept]
    q_first, q_rest, q_then = planes(qkv_out.at[plane], lambda p: qkv_out.at[p])
    w_first.wait_recv()
    mover.go(*w_then)
    tokens[0].forward()
    q_first.wait_recv()
    mover.go(*q_then)
    for p in tokens[1:]:
        p.forward()
    for p in tokens:
        p.arrive()
    for c in shared + q_rest + q_then + w_rest + w_then:
        c.wait_recv()
    mover.finish()


def start_gather(tokens, qkv, small, w_out):
    quads, lanes = lax.axis_size("quad"), lax.axis_size("lane")
    count = tokens.shape[0]
    planes, devices = 2 * lanes, 4 * lanes * quads

    def like(lead, x, dtype=BF):
        return jax.ShapeDtypeStruct(lead + x.shape, dtype)

    sems = (devices - 1) + 2 * (2 * lanes - 1) + (2 * quads - 1)
    sems += Spread.count(quads) * count
    return pl.pallas_call(
        functools.partial(start_body, quads, lanes),
        out_shape=[like((2, quads), tokens)]
        + [like((planes,), qkv), like((devices,), small), like((planes,), w_out)],
        in_specs=[pl.BlockSpec(memory_space=pltpu.VMEM)] * 4,
        out_specs=[pl.BlockSpec(memory_space=pl.ANY)] * 4,
        scratch_shapes=[
            pltpu.SemaphoreType.DMA((3 + count,)),
            pltpu.SemaphoreType.DMA((sems,)),
            pltpu.SemaphoreType.DMA((sems,)),
        ],
        compiler_params=pltpu.CompilerParams(collective_id=0, has_side_effects=True),
        name="start_gather",
    )(tokens, qkv, small, w_out)


def add_rows(out_ref, *refs):
    rows = out_ref.shape[0]
    step = 16

    @pl.loop(0, rows // step)
    def _(i):
        part = pl.ds(pl.multiple_of(i * step, step), step)
        total = refs[0][part].astype(F32)
        for ref in refs[1:]:
            total = total + ref[part].astype(F32)
        out_ref[part] = total.astype(out_ref.dtype)


def scatter_body(quads, lanes, partners, count, extra, *refs):
    kinds = len(partners)
    inputs, refs = refs[:kinds], refs[kinds:]
    if extra:
        blocks_ref, *refs = refs
    outputs, refs = refs[:kinds], refs[kinds:]
    if extra:
        blocks_out, held, *refs = refs
    mine, theirs, relay, arrived, *rest = refs
    if any(partners):
        summed, back, *rest = rest
    local, send, recv = rest
    mover = Mover(send, recv, local)
    mover.local_number = local.shape[0] - 2
    rows = inputs[0].shape[3]
    first, second = pl.ds(0, rows // 2), pl.ds(rows // 2, rows // 2)
    quad = lax.axis_index("quad")
    to_quad = [{"quad": toggled(quad, k)} for k in range(quads)]
    sibling = {"pair": 1 - lax.axis_index("pair")}
    across = {"half": 1 - lax.axis_index("half")}
    peers = to_quad[1:] + [sibling]
    if extra:
        me, planes = planes_of(lanes)
        peers += [device for device, _ in planes]
    elif any(partners):
        peers.append(across)
    greet(peers)

    def go(src, dst, device):
        c = mover.copy(src, dst, device)
        mover.go(c)
        return c

    order = [(i, s) for i in range(kinds) if partners[i] for s in range(count, 2 * count)]
    order += [(i, s) for i in range(kinds) for s in range(count)]
    ks = [3, 1, 2, 0] if quads == 4 else list(range(quads - 1, -1, -1))
    sib, loc = {}, {}

    def pieces(i, core, k, s):
        if len(inputs[i].shape) == 5:
            return [(inputs[i].at[core, k, s], pl.ds(0, rows))]
        shard = inputs[i].shape[2]
        place = ctx_at(quads, core * quads + k)[1]
        each = rows // shard
        return [
            (inputs[i].at[s * each + j, place], pl.ds(j * shard, shard)) for j in range(each)
        ]

    def load(src, dst, number):
        c = pltpu.make_async_copy(src, dst, local.at[number])
        c.start()
        return c

    for n, (i, s) in enumerate(order):
        for k in ks:
            sib[n, k] = [
                go(src, theirs.at[n, k, part], sibling) for src, part in pieces(i, 1, k, s)
            ]
            loc[n, k] = [
                load(src, mine.at[n, k, part], (n * quads + k) * 2 + j)
                for j, (src, part) in enumerate(pieces(i, 0, k, s))
            ]
    sends = {}

    def merge(n):
        for k in ks:
            for c in sib[n, k]:
                c.wait_recv()
            for c in loc[n, k]:
                c.wait()
            add_rows(mine.at[n, k], mine.at[n, k], theirs.at[n, k])
            if quads == 4:
                if k == 3:
                    sends[n, "3a"] = go(mine.at[n, 3, first], relay.at[n, 0], to_quad[2])
                    sends[n, "3b"] = go(mine.at[n, 3, second], relay.at[n, 1], to_quad[1])
                elif k == 1:
                    sends[n, "1b"] = go(mine.at[n, 1, second], arrived.at[n, 0, second], to_quad[1])
                elif k == 2:
                    sends[n, "2a"] = go(mine.at[n, 2, first], arrived.at[n, 1, first], to_quad[2])
            elif k:
                sends[n, k] = go(mine.at[n, k], arrived.at[n, k - 1], to_quad[k])

    def pass_on(n):
        if quads == 4:
            sends[n, "3a"].wait_recv()
            add_rows(mine.at[n, 1, first], mine.at[n, 1, first], relay.at[n, 0])
            sends[n, "1a"] = go(mine.at[n, 1, first], arrived.at[n, 0, first], to_quad[1])
            sends[n, "3b"].wait_recv()
            add_rows(mine.at[n, 2, second], mine.at[n, 2, second], relay.at[n, 1])
            sends[n, "2b"] = go(mine.at[n, 2, second], arrived.at[n, 1, second], to_quad[2])

    backs = {}

    def total_of(n):
        i, s = order[n]
        for name in ("1b", "2a", "1a", "2b") if quads == 4 else range(1, quads):
            sends[n, name].wait_recv()
        parts = [mine.at[n, 0]] + [arrived.at[n, j] for j in range(arrived.shape[1])]
        if s >= count:
            slot = i * count + s - count
            add_rows(summed.at[slot], *parts)
            backs[slot] = go(summed.at[slot], back.at[slot], across)
        else:
            if partners[i]:
                backs[i * count + s].wait_recv()
                parts.append(back.at[i * count + s])
            add_rows(outputs[i].at[s], *parts)

    ahead = 2
    exchanged = []

    if extra:
        into = mover.keep(blocks_ref.at[me], held)
        for device, place in planes:
            exchanged.append(go(blocks_ref.at[place], blocks_out.at[me], device))
    for n in range(len(order) + 2 * ahead):
        if extra and n == 1:
            into.wait()
            mover.kept = [c for c in mover.kept if c is not into]
            mover.keep(held, blocks_out.at[me])
        if n < len(order):
            merge(n)
        if 0 <= n - 1 < len(order):
            pass_on(n - 1)
        if 0 <= n - 2 * ahead < len(order):
            total_of(n - 2 * ahead)
    for c in exchanged:
        c.wait_recv()
    mover.finish()


def scatter_rows(parts, partners, name, number, extra=()):
    lanes = lax.axis_size("lane")
    _, quads, _, rows, width = parts[0].shape
    shards = sum(
        part.shape[2] if len(part.shape) == 5 else part.shape[0] * part.shape[2] // rows
        for part in parts
    )
    kinds = len(parts)
    count = shards // sum(2 if partner else 1 for partner in partners)
    incoming = 2 if quads == 4 else quads - 1
    sems = shards * (2 * quads + (6 if quads == 4 else quads - 1)) + count * sum(partners)

    def buf(*lead):
        return pltpu.VMEM(lead + (rows, width), BF)

    scratch = [buf(shards, quads), buf(shards, quads)]
    scratch += [pltpu.VMEM((shards, 2, rows // 2, width), BF), buf(shards, incoming)]
    if any(partners):
        scratch += [buf(kinds * count), buf(kinds * count)]
    shapes = [jax.ShapeDtypeStruct((count, rows, width), F32)] * kinds
    specs = [pl.BlockSpec(memory_space=pltpu.VMEM)] * kinds
    anywhere = pl.BlockSpec(memory_space=pl.ANY)
    if extra:
        blocks = extra[0]
        shapes = shapes + [jax.ShapeDtypeStruct(blocks.shape, BF)]
        specs = specs + [anywhere]
        scratch = [pltpu.VMEM(blocks.shape[1:], BF)] + scratch
        sems += 2 * lanes - 1
    return pl.pallas_call(
        functools.partial(scatter_body, quads, lanes, partners, count, bool(extra)),
        out_shape=shapes,
        in_specs=[anywhere] * (kinds + len(extra)),
        out_specs=specs,
        scratch_shapes=scratch
        + [
            pltpu.SemaphoreType.DMA((2 * shards * quads + 2,)),
            pltpu.SemaphoreType.DMA((sems,)),
            pltpu.SemaphoreType.DMA((sems,)),
        ],
        compiler_params=pltpu.CompilerParams(
            collective_id=number, has_side_effects=True, vmem_limit_bytes=60 << 20
        ),
        name=name,
    )(*parts, *extra)


def ctx_place():
    return lax.axis_index("quad") * 2 + lax.axis_index("pair")


def ctx_at(quads, number):
    core, distance = number // quads, number % quads
    quad = toggled(lax.axis_index("quad"), distance)
    pair = toggled(lax.axis_index("pair"), core)
    return {"quad": quad, "pair": pair}, quad * 2 + pair


def all_at(lanes, quads, number):
    half = toggled(lax.axis_index("half"), number // (lanes * 2 * quads))
    lane = toggled(lax.axis_index("lane"), number // (2 * quads) % lanes)
    device, place = ctx_at(quads, number % (2 * quads))
    return {"half": half, "lane": lane, **device}, (half * lanes + lane) * 2 * quads + place


def exchange_body(mode, lanes, quads, halves, x_ref, out_ref, local, send, recv):
    copies = []
    peers = []
    if mode in ("shared", "all"):
        me = (lax.axis_index("half") * lanes + lax.axis_index("lane")) * 2 * quads + ctx_place()
        for n in range(2 * lanes * 2 * quads):
            device, place = all_at(lanes, quads, n)
            copies.append((x_ref if mode == "shared" else x_ref.at[place], out_ref.at[me], device))
    else:
        for h in range(halves):
            for n in range(2 * quads):
                device, place = ctx_at(quads, n)
                if halves == 2:
                    device = {"half": toggled(lax.axis_index("half"), h), **device}
                if mode == "inward":
                    pair = (x_ref.at[h, n], out_ref.at[h, ctx_place()])
                elif mode == "outward":
                    pair = (x_ref.at[place], out_ref.at[h, n])
                else:
                    pair = (x_ref.at[place], out_ref.at[ctx_place()])
                copies.append(pair + (device,))
    own = pltpu.make_async_copy(copies[0][0], copies[0][1], local)
    own.start()
    greet([device for _, _, device in copies[1:]])
    started = []
    for i, (src, dst, device) in enumerate(copies[1:]):
        c = pltpu.make_async_remote_copy(
            src_ref=src, dst_ref=dst, send_sem=send.at[i], recv_sem=recv.at[i],
            device_id=device, device_id_type=MESH,
        )
        c.start()
        started.append(c)
    own.wait()
    for c in started:
        c.wait_recv()
    for c in started:
        c.wait_send()


def exchange_rows(x, mode, name, number, halves=1):
    quads, lanes = lax.axis_size("quad"), lax.axis_size("lane")
    count = halves * 2 * quads - 1
    shape = x.shape
    if mode == "outward":
        shape = (halves, 2 * quads) + x.shape[1:]
    elif mode in ("shared", "all"):
        count = 4 * lanes * quads - 1
        if mode == "shared":
            shape = (count + 1,) + x.shape
    return pl.pallas_call(
        functools.partial(exchange_body, mode, lanes, quads, halves),
        out_shape=jax.ShapeDtypeStruct(shape, x.dtype),
        in_specs=[pl.BlockSpec(memory_space=pltpu.VMEM)],
        out_specs=pl.BlockSpec(memory_space=pltpu.VMEM),
        scratch_shapes=[
            pltpu.SemaphoreType.DMA,
            pltpu.SemaphoreType.DMA((count,)),
            pltpu.SemaphoreType.DMA((count,)),
        ],
        compiler_params=pltpu.CompilerParams(collective_id=number, has_side_effects=True),
        name=name,
    )(x)


def final_body(quads, lanes, count, *refs):
    inputs, outputs = refs[:count], refs[count : 2 * count]
    local, send, recv = refs[2 * count :]
    mover = Mover(send, recv, local)
    plane, planes = planes_of(lanes)
    here = ctx_place()
    devices = [all_at(lanes, quads, n) for n in range(4 * lanes * quads)]
    greet([device for device, _ in devices[1:]])
    me = plane * 2 * quads + here
    qkv, small = inputs[:2]
    part = qkv.shape[2] // 3
    columns = pl.ds(pl.multiple_of(here * part, 128), part)
    split = [(slice(kind * part, (kind + 1) * part), kind) for kind in range(3)]
    copies = [
        (qkv.at[place, :, src], outputs[0].at[kind, :, columns], device)
        for device, place in [ctx_at(quads, n) for n in range(1, 2 * quads)]
        for src, kind in split
    ]
    for ref, out in zip(inputs[2:], outputs[2:]):
        copies += [(ref.at[place], out.at[plane], device) for device, place in planes]
    copies += [(small.at[place], outputs[1].at[me], device) for device, place in devices[1:]]
    started = [mover.copy(*c) for c in copies]
    mover.go(*started)
    for src, kind in split:
        mover.keep(qkv.at[here, :, src], outputs[0].at[kind, :, columns])
    mover.keep(small.at[me], outputs[1].at[me])
    for ref, out in zip(inputs[2:], outputs[2:]):
        mover.keep(ref.at[plane], out.at[plane])
    for c in started:
        c.wait_recv()
    mover.finish()


def final_exchange(qkv, small, planes):
    quads, lanes = lax.axis_size("quad"), lax.axis_size("lane")
    arrays = [qkv, small, *planes]
    sems = 3 * (2 * quads - 1) + 4 * lanes * quads - 1 + len(planes) * (2 * lanes - 1)
    shapes = [x.shape for x in arrays]
    shapes[0] = (3, qkv.shape[1], qkv.shape[0] * qkv.shape[2] // 3)
    vmem = pl.BlockSpec(memory_space=pltpu.VMEM)
    return pl.pallas_call(
        functools.partial(final_body, quads, lanes, len(arrays)),
        out_shape=[jax.ShapeDtypeStruct(shape, x.dtype) for shape, x in zip(shapes, arrays)],
        in_specs=[vmem] * len(arrays),
        out_specs=[vmem] * len(arrays),
        scratch_shapes=[
            pltpu.SemaphoreType.DMA((len(arrays) + 2,)),
            pltpu.SemaphoreType.DMA((sems,)),
            pltpu.SemaphoreType.DMA((sems,)),
        ],
        compiler_params=pltpu.CompilerParams(collective_id=14, has_side_effects=True),
        name="final_exchange",
    )(*arrays)


def sum_body(quads, x_ref, out_ref, landed, send, recv):
    count = 2 * quads
    greet([ctx_at(quads, n)[0] for n in range(1, count)])
    started = []
    for n in range(1, count):
        c = pltpu.make_async_remote_copy(
            src_ref=x_ref, dst_ref=landed.at[n - 1], send_sem=send.at[n - 1],
            recv_sem=recv.at[n - 1], device_id=ctx_at(quads, n)[0], device_id_type=MESH,
        )
        c.start()
        started.append(c)
    for c in started:
        c.wait_recv()
    for j in range(count):
        total = x_ref[j]
        for n in range(1, count):
            total = total + landed[n - 1, j ^ n]
        out_ref[j] = total
    for c in started:
        c.wait_send()


def sum_ctx(x, name, number):
    quads = lax.axis_size("quad")
    count = 2 * quads - 1
    return pl.pallas_call(
        functools.partial(sum_body, quads),
        out_shape=jax.ShapeDtypeStruct(x.shape, x.dtype),
        in_specs=[pl.BlockSpec(memory_space=pltpu.VMEM)],
        out_specs=pl.BlockSpec(memory_space=pltpu.VMEM),
        scratch_shapes=[
            pltpu.VMEM((count,) + x.shape, x.dtype),
            pltpu.SemaphoreType.DMA((count,)),
            pltpu.SemaphoreType.DMA((count,)),
        ],
        compiler_params=pltpu.CompilerParams(collective_id=number, has_side_effects=True),
        name=name,
    )(x)


def nn(left, right):
    return lax.dot_general(left, right, (((1,), (0,)), ((), ())), preferred_element_type=F32)


def nt(left, right):
    return lax.dot_general(left, right, (((1,), (1,)), ((), ())), preferred_element_type=F32)


def tn(left, right):
    return lax.dot_general(left, right, (((0,), (0,)), ((), ())), preferred_element_type=F32)


def expert_body(quads, before, _, gate_ref, x_ref, go_ref, gp_ref, both_ref, down_ref, *refs):
    sums = refs[:2] if before else None
    moe_ref, d_ref, dgate_ref, hid_ref, dg_ref, du_ref = refs[-6:]
    t = pl.program_id(0)
    hidden, width = down_ref.shape
    x = x_ref[0, 0].reshape(-1, width)
    gate = gate_ref[0]
    wg = both_ref[:, 0].reshape(width, hidden)
    wu = both_ref[:, 1].reshape(width, hidden)
    wd = down_ref[...]

    g = jnp.where(t % 2 == 1, gp_ref[0, 0], go_ref[0]).reshape(-1, width)
    gate_pre = nn(x, wg)
    up_pre = nn(x, wu)
    d_hidden = nt(g, wd)
    sigma = 1.0 / (1.0 + jnp.exp(-gate_pre))
    silu = gate_pre * sigma
    hid = silu * up_pre
    dgate_ref[0] = jnp.sum(hid * d_hidden, axis=1, keepdims=True)
    d_hidden = d_hidden * gate
    scaled = (hid * gate).astype(BF)
    d_gate_pre = (d_hidden * up_pre * (sigma + silu * (1.0 - sigma))).astype(BF)
    d_up_pre = (d_hidden * silu).astype(BF)
    hid_ref[0] = scaled
    dg_ref[0] = d_gate_pre
    du_ref[0] = d_up_pre
    shape = moe_ref.shape[2:]
    moe = nn(scaled, wd).reshape(shape)
    d_rows = (nt(d_gate_pre, wg) + nt(d_up_pre, wu)).reshape(shape)
    if before:
        moe = moe + sums[0][0, 0].astype(F32)
        d_rows = d_rows + sums[1][0, 0].astype(F32)
    moe_ref[0, 0] = moe.astype(BF)
    d_ref[0, 0] = d_rows.astype(BF)


def expert(place, gates, x_rows, g_rows, both, down, before, name):
    _, quads, shards, rows, width = x_rows.shape
    batches = shards // 2
    hidden = down.shape[0]
    tiles = 4 * quads
    tile = batches * rows

    def row_block(t, p):
        return (t // (2 * quads), t // 2 % quads, t % 2, 0, 0)

    block = pl.BlockSpec((1, 1, batches, rows, width), row_block)
    saved_spec = pl.BlockSpec((1, tile, hidden), lambda t, p: (t, 0, 0))
    saved = jax.ShapeDtypeStruct((tiles, tile, hidden), BF)
    rows_shape = jax.ShapeDtypeStruct(x_rows.shape, BF)
    fixed = dict(pipeline_mode=pl.Buffered(1))
    column = pl.BlockSpec((1, tile, 1), lambda t, p: (t, 0, 0))
    return pl.pallas_call(
        functools.partial(expert_body, quads, bool(before)),
        out_shape=(rows_shape,) * 2
        + (jax.ShapeDtypeStruct((tiles, tile, 1), F32), saved, saved, saved),
        grid_spec=pltpu.PrefetchScalarGridSpec(
            num_scalar_prefetch=1,
            grid=(tiles,),
            in_specs=[
                column, block,
                pl.BlockSpec((1, batches, rows, width), lambda t, p: (p[t // 2], 0, 0, 0)),
                pl.BlockSpec(
                    (1, 1, batches, rows, width),
                    lambda t, p: (t // (2 * quads), t // 2 % quads, 0, 0, 0),
                ),
                pl.BlockSpec(both.shape, lambda t, p: (0, 0, 0, 0), **fixed),
                pl.BlockSpec(down.shape, lambda t, p: (0, 0), **fixed),
            ]
            + ([block] * 2 if before else []),
            out_specs=[block, block, column, saved_spec, saved_spec, saved_spec],
        ),
        input_output_aliases={7 + i: i for i in range(2)} if before else {},
        compiler_params=pltpu.CompilerParams(
            dimension_semantics=("arbitrary",), vmem_limit_bytes=60 << 20
        ),
        name=name,
    )(place, gates, x_rows, *g_rows, both, down, *before)


def grads_body(_, x_ref, go_ref, gp_ref, hid_ref, dg_ref, du_ref, both_ref, down_ref,
               gate_acc, up_acc, down_acc):
    t = pl.program_id(0)
    width = down_acc.shape[1]
    hidden = down_acc.shape[0]

    @pl.when(t == 0)
    def _():
        gate_acc[...] = jnp.zeros_like(gate_acc)
        up_acc[...] = jnp.zeros_like(up_acc)
        down_acc[...] = jnp.zeros_like(down_acc)

    x = x_ref[0, 0].reshape(-1, width)
    g = jnp.concatenate([go_ref[0].reshape(-1, width), gp_ref[0, 0].reshape(-1, width)], axis=0)
    gate_acc[...] += tn(x, dg_ref[...].reshape(-1, hidden))
    up_acc[...] += tn(x, du_ref[...].reshape(-1, hidden))
    down_acc[...] += tn(hid_ref[...].reshape(-1, hidden), g)

    @pl.when(t == pl.num_programs(0) - 1)
    def _():
        part = both_ref.shape[0]
        both_ref[:, 0] = gate_acc[...].astype(BF).reshape(part, -1, hidden)
        both_ref[:, 1] = up_acc[...].astype(BF).reshape(part, -1, hidden)
        down_ref[...] = down_acc[...].astype(BF)


def expert_grads(place, x_rows, g_rows, hid, dg, du, dp, name):
    _, quads, shards, rows, width = x_rows.shape
    batches = shards // 2
    tiles, tile, hidden = hid.shape

    saved = pl.BlockSpec((2, tile, hidden), lambda t, p: (t, 0, 0))

    def row_block(t, p):
        return (t // quads, t % quads, 0, 0, 0)

    return pl.pallas_call(
        grads_body,
        out_shape=(
            jax.ShapeDtypeStruct((dp, 2, width // dp, hidden), BF),
            jax.ShapeDtypeStruct((hidden, width), BF),
        ),
        grid_spec=pltpu.PrefetchScalarGridSpec(
            num_scalar_prefetch=1,
            grid=(tiles // 2,),
            in_specs=[
                pl.BlockSpec((1, 1, shards, rows, width), row_block),
                pl.BlockSpec((1, batches, rows, width), lambda t, p: (p[t], 0, 0, 0)),
                pl.BlockSpec((1, 1, batches, rows, width), row_block),
                saved, saved, saved,
            ],
            out_specs=[
                pl.BlockSpec((dp, 2, width // dp, hidden), lambda t, p: (0, 0, 0, 0)),
                pl.BlockSpec((hidden, width), lambda t, p: (0, 0)),
            ],
            scratch_shapes=[pltpu.VMEM((width, hidden), F32), pltpu.VMEM((width, hidden), F32),
                            pltpu.VMEM((hidden, width), F32)],
        ),
        compiler_params=pltpu.CompilerParams(
            dimension_semantics=("arbitrary",), vmem_limit_bytes=60 << 20
        ),
        name=name,
    )(place, x_rows, *g_rows, hid, dg, du)


def finish_body(lanes, *refs):
    gate_ref, up_ref = refs[-2:]
    for e, ref in enumerate(refs[:-2]):
        for kind, out_ref in enumerate((gate_ref, up_ref)):
            hidden = ref.shape[3]
            for h in range(2):
                total = ref[h * lanes, kind].astype(F32)
                for l in range(1, lanes):
                    total = total + ref[h * lanes + l, kind].astype(F32)
                out_ref[e, :, h * hidden : (h + 1) * hidden] = total


def finish_grads(parts):
    planes, _, depth, hidden = parts[0].shape
    step = 128
    shape = jax.ShapeDtypeStruct((len(parts), depth, 2 * hidden), F32)
    out_spec = pl.BlockSpec((len(parts), step, 2 * hidden), lambda i: (0, i, 0))
    return pl.pallas_call(
        functools.partial(finish_body, planes // 2),
        out_shape=(shape, shape),
        grid=(depth // step,),
        in_specs=[pl.BlockSpec((planes, 2, step, hidden), lambda i: (0, 0, i, 0))] * len(parts),
        out_specs=(out_spec, out_spec),
        name="finish_gradients",
    )(*parts)


def row_sums(values):
    ones = jnp.ones((8, values.shape[1]), F32)
    sums = lax.dot_general(
        ones, values, (((1,), (1,)), ((), ())), preferred_element_type=F32,
        precision=lax.Precision.HIGHEST,
    )
    return sums[:1]


def columns(values):
    turned = jnp.transpose(values)
    return jnp.concatenate([turned[:, i : i + 1] for i in range(values.shape[0])], axis=0)


def qkv_body(x_ref, gain_ref, w_ref, act_ref, pre_ref, square_ref):
    batches, rows, width = x_ref.shape[2:]
    head_width = w_ref.shape[1] // 3
    x = x_ref[0, 0].astype(F32).reshape(-1, width)
    root = lax.rsqrt(jnp.mean(x * x, axis=1, keepdims=True) + EPSILON)
    act = (x * root * gain_ref[...]).astype(BF)
    pre = nn(act, w_ref[...])
    pre_ref[:, 0] = pre.reshape(batches, rows, -1)
    for kind in range(2):
        part = pre[:, kind * head_width : (kind + 1) * head_width]
        sums = row_sums(part * part)
        for m in range(batches):
            i = kind * batches + m
            square_ref[0, i : i + 1] = sums[:, m * rows : (m + 1) * rows]
    act_ref[0, 0] = act.reshape(batches, rows, width)


def row_spec(quads, shape):
    return pl.BlockSpec((1, 1) + shape, lambda n: (n // quads, n % quads, 0, 0, 0))


def project(token_rows, gain, weights):
    _, quads, batches, rows, width = token_rows.shape
    total = weights.shape[1]
    fixed = dict(pipeline_mode=pl.Buffered(1))
    block = row_spec(quads, (batches, rows, width))
    return pl.pallas_call(
        qkv_body,
        out_shape=(
            jax.ShapeDtypeStruct(token_rows.shape, BF),
            jax.ShapeDtypeStruct((batches, 2 * quads, rows, total), F32),
            jax.ShapeDtypeStruct((2 * quads, 2 * batches, rows), F32),
        ),
        grid=(2 * quads,),
        in_specs=[
            block,
            pl.BlockSpec((1, width), lambda n: (0, 0)),
            pl.BlockSpec((width, total), lambda n: (0, 0), **fixed),
        ],
        out_specs=(
            block,
            pl.BlockSpec((batches, 1, rows, total), lambda n: (0, n, 0, 0)),
            pl.BlockSpec((1, 2 * batches, rows), lambda n: (n, 0, 0)),
        ),
        compiler_params=pltpu.CompilerParams(vmem_limit_bytes=40 << 20),
        name="project",
    )(token_rows, gain.reshape(1, width), weights)


def turned(values, cosine, sine):
    return values * cosine + pltpu.roll(values, HEAD // 2, 1) * sine


def turned_back(grad, cosine, sine):
    return grad * cosine - pltpu.roll(grad, HEAD // 2, 1) * sine


def head_probs(query, key, column, row, length):
    scores = nt(query, key) * (1.0 / math.sqrt(HEAD))
    scores = jnp.where((row <= column) & (row < length), scores, MASKED)
    expo = jnp.exp(scores - jnp.max(scores, axis=1, keepdims=True))
    return expo / jnp.sum(expo, axis=1, keepdims=True)


def attend_body(
    step, pre_ref, sum_ref, gain_ref, cos_ref, sin_ref, column_ref, row_ref, length_ref,
    query_ref, key_ref, value_ref, out_ref, att,
):
    m = pl.program_id(0)
    places, rows = pre_ref.shape[1:3]
    slot = places * rows
    head_width = query_ref.shape[2]
    cosine, sine = cos_ref[...], sin_ref[...]
    pre = pre_ref[0].reshape(slot, 3 * head_width)
    for kind, ref in enumerate((query_ref, key_ref)):
        root = lax.rsqrt(columns(sum_ref[0, kind]) / (head_width * places) + EPSILON)
        part = pre[:, kind * head_width : (kind + 1) * head_width] * root * gain_ref[kind]
        for h in range(head_width // HEAD):
            here = slice(h * HEAD, (h + 1) * HEAD)
            ref[0, :, here] = turned(part[:, here], cosine, sine).astype(BF)
    value_ref[0] = pre[:, 2 * head_width :].astype(BF)
    length = length_ref[m]
    row = row_ref[...]
    for h in range(head_width // HEAD):
        here = slice(h * HEAD, (h + 1) * HEAD)

        @pl.loop(0, slot // step)
        def _(i):
            part = pl.ds(pl.multiple_of(i * step, step), step)
            probs = head_probs(query_ref[0, part, here], key_ref[0, :, here], column_ref[part], row, length)
            att[part, here] = nn(probs.astype(BF), value_ref[0, :, here]).astype(BF)

    out_ref[:, 0] = att[...].reshape(places, rows, head_width)


def attend(pre, sums, gains, cosine, sine, column, row, lengths):
    batches, places, rows, total = pre.shape
    head_width, slot = total // 3, places * rows
    saved = jax.ShapeDtypeStruct((batches, slot, head_width), BF)
    saved_spec = pl.BlockSpec((1, slot, head_width), lambda m: (m, 0, 0))
    return pl.pallas_call(
        functools.partial(attend_body, 256),
        out_shape=(saved,) * 3
        + (jax.ShapeDtypeStruct((places, batches, rows, head_width), BF),),
        grid=(batches,),
        in_specs=[
            pl.BlockSpec((1,) + pre.shape[1:], lambda m: (m, 0, 0, 0)),
            pl.BlockSpec((1,) + sums.shape[1:], lambda m: (m, 0, 0, 0)),
            pl.BlockSpec(gains.shape, lambda m: (0, 0, 0)),
            pl.BlockSpec(cosine.shape, lambda m: (0, 0)),
            pl.BlockSpec(sine.shape, lambda m: (0, 0)),
            pl.BlockSpec(column.shape, lambda m: (0, 0)),
            pl.BlockSpec(row.shape, lambda m: (0, 0)),
            pl.BlockSpec(memory_space=pltpu.SMEM),
        ],
        out_specs=(saved_spec,) * 3
        + (pl.BlockSpec((places, 1, rows, head_width), lambda m: (0, m, 0, 0)),),
        scratch_shapes=[pltpu.VMEM((slot, head_width), BF)],
        compiler_params=pltpu.CompilerParams(vmem_limit_bytes=60 << 20),
        name="attend",
    )(pre, sums, gains, cosine, sine, column, row, lengths)


def attend_back_body(
    step, query_ref, key_ref, value_ref, datt_ref, pre_ref, sum_ref, gain_ref, cos_ref, sin_ref,
    column_ref, row_ref, length_ref, dn_ref, dv_ref, inner_ref, dgain_ref, att, dq, dk, dv,
):
    m = pl.program_id(0)
    places, rows = pre_ref.shape[1:3]
    slot = places * rows
    head_width = query_ref.shape[2]
    factor = 1.0 / math.sqrt(HEAD)
    att[...] = datt_ref[:, 0].reshape(slot, head_width)
    length = length_ref[m]
    row = row_ref[...]
    dk[...] = jnp.zeros_like(dk)
    dv[...] = jnp.zeros_like(dv)
    for h in range(head_width // HEAD):
        here = slice(h * HEAD, (h + 1) * HEAD)

        @pl.loop(0, slot // step)
        def _(i):
            part = pl.ds(pl.multiple_of(i * step, step), step)
            query, grad = query_ref[0, part, here], att[part, here]
            probs = head_probs(query, key_ref[0, :, here], column_ref[part], row, length)
            d_probs = nt(grad, value_ref[0, :, here])
            inner = jnp.sum(probs * d_probs, axis=1, keepdims=True)
            d_scores = (probs * (d_probs - inner)).astype(BF)
            dq[part, here] = nn(d_scores, key_ref[0, :, here]) * factor
            dk[:, here] += tn(d_scores, query) * factor
            dv[:, here] += tn(probs.astype(BF), grad)

    dv_ref[0] = dv[...].astype(BF)
    cosine, sine = cos_ref[...], sin_ref[...]
    for kind, ref in enumerate((dq, dk)):
        root = lax.rsqrt(columns(sum_ref[0, kind]) / (head_width * places) + EPSILON)
        for h in range(head_width // HEAD):
            here = slice(h * HEAD, (h + 1) * HEAD)
            ref[:, here] = turned_back(ref[:, here], cosine, sine)
        grad = ref[...]
        pre = pre_ref[0, :, :, kind * head_width : (kind + 1) * head_width].reshape(slot, head_width)
        product = grad * pre
        gain_part = jnp.sum(product * root, axis=0, keepdims=True)
        before = jnp.where(m == 0, jnp.zeros_like(gain_part), dgain_ref[kind])
        dgain_ref[kind] = before + gain_part
        weighted = grad * gain_ref[kind]
        dn_ref[0, kind] = weighted
        sums = row_sums(product * gain_ref[kind])
        for n in range(places):
            inner_ref[0, kind, n : n + 1] = sums[:, n * rows : (n + 1) * rows]


def attend_back(saved, d_att, pre, sums, gains, cosine, sine, column, row, lengths):
    batches, places, rows, total = pre.shape
    head_width, slot = total // 3, places * rows
    saved_spec = pl.BlockSpec((1, slot, head_width), lambda m: (m, 0, 0))
    return pl.pallas_call(
        functools.partial(attend_back_body, 256),
        out_shape=(
            jax.ShapeDtypeStruct((batches, 2, slot, head_width), F32),
            jax.ShapeDtypeStruct((batches, slot, head_width), BF),
            jax.ShapeDtypeStruct(sums.shape, F32),
            jax.ShapeDtypeStruct(gains.shape, F32),
        ),
        grid=(batches,),
        in_specs=[saved_spec] * 3
        + [
            pl.BlockSpec((places, 1, rows, head_width), lambda m: (0, m, 0, 0)),
            pl.BlockSpec((1,) + pre.shape[1:], lambda m: (m, 0, 0, 0)),
            pl.BlockSpec((1,) + sums.shape[1:], lambda m: (m, 0, 0, 0)),
            pl.BlockSpec(gains.shape, lambda m: (0, 0, 0)),
            pl.BlockSpec(cosine.shape, lambda m: (0, 0)),
            pl.BlockSpec(sine.shape, lambda m: (0, 0)),
            pl.BlockSpec(column.shape, lambda m: (0, 0)),
            pl.BlockSpec(row.shape, lambda m: (0, 0)),
            pl.BlockSpec(memory_space=pltpu.SMEM),
        ],
        out_specs=(
            pl.BlockSpec((1, 2, slot, head_width), lambda m: (m, 0, 0, 0)),
            saved_spec,
            pl.BlockSpec((1,) + sums.shape[1:], lambda m: (m, 0, 0, 0)),
            pl.BlockSpec(gains.shape, lambda m: (0, 0, 0)),
        ),
        scratch_shapes=[pltpu.VMEM((slot, head_width), BF)]
        + [pltpu.VMEM((slot, head_width), F32)] * 3,
        compiler_params=pltpu.CompilerParams(vmem_limit_bytes=60 << 20),
        name="attend_back",
    )(*saved, d_att, pre, sums, gains, cosine, sine, column, row, lengths)


def back_body(
    quads, dn_ref, dv_ref, pre_ref, sum_ref, inner_ref, act_ref, w_ref, d_ref, dw_ref, dw, cols,
):
    n = pl.program_id(0)
    batches, _, rows, head_width = dn_ref.shape
    width = w_ref.shape[0]
    total = head_width * 2 * quads
    for m in range(batches):
        here = pl.ds(m * rows, rows)
        for kind in range(2):
            root = lax.rsqrt(columns(sum_ref[0, m, kind]) / total + EPSILON)
            inner = columns(inner_ref[0, m, kind]) / total
            part = slice(kind * head_width, (kind + 1) * head_width)
            pre = pre_ref[m, 0, :, part]
            grad = root * dn_ref[m, kind] - pre * (root * root * root) * inner
            cols[here, part] = grad.astype(BF)
        cols[here, 2 * head_width :] = dv_ref[m]
    d_pre = cols[...]
    act = act_ref[0, 0].reshape(-1, width)
    d_ref[0, 0] = nt(d_pre, w_ref[...]).astype(BF).reshape(batches, rows, width)
    part = tn(act, d_pre)

    @pl.when(n == 0)
    def _():
        dw[...] = part

    @pl.when(n > 0)
    def _():
        dw[...] += part

    @pl.when(n == pl.num_programs(0) - 1)
    def _():
        dw_ref[...] = dw[...].astype(BF)


def project_back(d_norm, d_value, pre, sums, inners, act, weights):
    batches, places, rows, total = pre.shape
    quads, width, head_width = places // 2, weights.shape[0], total // 3
    fixed = dict(pipeline_mode=pl.Buffered(1))
    block = row_spec(quads, (batches, act.shape[3], width))
    sums = sums.transpose(2, 0, 1, 3)[:, :, :, None]
    inners = inners[:, :, :, None]
    small = pl.BlockSpec((1, batches, 2, 1, rows), lambda n: (n, 0, 0, 0, 0))
    return pl.pallas_call(
        functools.partial(back_body, quads),
        out_shape=(
            jax.ShapeDtypeStruct(act.shape, BF), jax.ShapeDtypeStruct(weights.shape, BF),
        ),
        grid=(places,),
        in_specs=[
            pl.BlockSpec((batches, 2, rows, head_width), lambda n: (0, 0, n, 0)),
            pl.BlockSpec((batches, rows, head_width), lambda n: (0, n, 0)),
            pl.BlockSpec((batches, 1, rows, total), lambda n: (0, n, 0, 0)),
            small, small, block,
            pl.BlockSpec(weights.shape, lambda n: (0, 0), **fixed),
        ],
        out_specs=(block, pl.BlockSpec(weights.shape, lambda n: (0, 0))),
        scratch_shapes=[
            pltpu.VMEM(weights.shape, F32), pltpu.VMEM((batches * rows, total), BF)
        ],
        compiler_params=pltpu.CompilerParams(vmem_limit_bytes=60 << 20),
        name="project_back",
    )(d_norm, d_value, pre, sums, inners, act, weights)


def scatter_all(kinds, partners, name, number, extra=()):
    if kinds[0].shape[1] == 4:
        return scatter_rows(kinds, partners, name, number, extra)
    sums = []
    for i, (kind, partner) in enumerate(zip(kinds, partners)):
        count = kind.shape[2] // 2 if partner else kind.shape[2]
        parts = [
            scatter_rows([kind[:, :, m::count]], (partner,), name, number + 8 * i)[0]
            for m in range(count)
        ]
        sums.append(jnp.concatenate(parts))
    return sums + [exchange(blocks, DP) for blocks in extra]


def on_device(
    tokens,
    cotangent,
    routes,
    lengths,
    block_order,
    w_query,
    w_key,
    w_value,
    w_out,
    w_router,
    w_gate,
    w_up,
    w_down,
    attn_gain,
    mlp_gain,
    query_gain,
    key_gain,
):
    batches, _, rows, width = tokens.shape
    dp_size = lax.axis_size(DP)
    ctx_size = lax.axis_size(CTX)
    quads = lax.axis_size("quad")
    lanes = lax.axis_size("lane")
    slot_len = rows * ctx_size
    block_rows = rows // 2
    head_width = width // ctx_size
    shard = w_query.shape[0]
    expert_count = w_router.shape[1]
    local_experts = w_gate.shape[0]
    hidden_units = w_gate.shape[2]
    hidden_half = hidden_units // 2
    depth_part = w_gate.shape[1]
    pair = lax.axis_index("pair")

    qkv = jnp.stack([w_query, w_key, w_value], axis=1).reshape(shard, 3, ctx_size, head_width)
    qkv = qkv.transpose(2, 0, 1, 3).reshape(ctx_size, shard, 3 * head_width)
    small = jnp.concatenate(
        [attn_gain, mlp_gain, query_gain, key_gain, w_router.reshape(shard * expert_count)]
    )
    grad_low = cotangent[:, 0]
    token_rows, qkv_w, small, out_w = start_gather(
        tokens[:, 0], qkv, small.reshape(1, -1), w_out
    )
    out_w = lax.all_gather(out_w, CTX, axis=1, tiled=False).reshape(width, width)
    qkv_w = qkv_w.reshape(width, 3 * head_width)
    small = small.reshape(dp_size * ctx_size, -1)
    gain_attn = small[:, :shard].reshape(width).astype(F32)
    gain_mlp = small[:, shard : 2 * shard].reshape(width).astype(F32)
    gain_query = small[:, 2 * shard : 3 * shard].reshape(ctx_size, head_width)
    gain_key = small[:, 3 * shard : 4 * shard].reshape(ctx_size, head_width)
    router_w = small[:, 4 * shard :].reshape(width, expert_count)
    here = lax.axis_index(CTX)
    gain_query = lax.dynamic_index_in_dim(gain_query, here, 0, keepdims=False).astype(F32)
    gain_key = lax.dynamic_index_in_dim(gain_key, here, 0, keepdims=False).astype(F32)

    w_gate, w_up, w_down, crossing, qkv_w = lax.optimization_barrier(
        (w_gate, w_up, w_down, grad_low, qkv_w)
    )
    halves = [
        jnp.stack(
            [
                jnp.stack([w_gate[e, :, part], w_up[e, :, part]])
                for part in (slice(0, hidden_half), slice(hidden_half, hidden_units))
            ]
        )
        for e in range(local_experts)
    ]
    halves = [jnp.repeat(part, lanes, axis=0) for part in halves]
    next_w = exchange(halves[0], DP)
    down_parts = lane_parts(w_down)
    g_own = lax.all_gather(crossing, CTX, axis=0, tiled=False)

    def places_of(device):
        stored = device * rows + jnp.arange(rows, dtype=jnp.int32)
        match_marks = (stored // block_rows)[:, None] == jnp.arange(
            block_order.shape[0], dtype=jnp.int32
        )[None, :]
        first_place = jnp.sum(jnp.where(match_marks, block_order[None, :], 0), axis=1)
        return first_place * block_rows + stored % block_rows

    places = jnp.concatenate(
        [
            places_of((lax.axis_index("quad") ^ k) * 2 + (pair ^ other))
            for other in range(2)
            for k in range(quads)
        ]
    )
    cosine, sine = angles(places, HEAD)
    expert_range = jnp.arange(expert_count, dtype=jnp.int32)

    inputs = tokens[:, 0].astype(F32)
    attn_root = inv_rms(inputs)
    act, pre, squares = project(token_rows, gain_attn, qkv_w)
    squares = sum_ctx(squares, "sum_squares", 6)
    squares, crossing = lax.optimization_barrier((squares, crossing))
    crossing = swap(crossing, "half")
    squares = squares.reshape(2 * quads, 2, batches, rows).transpose(2, 1, 0, 3)
    qk_gains = jnp.stack([gain_query, gain_key])[:, None]
    signed = jnp.where(jnp.arange(HEAD) < HEAD // 2, -sine[:, 0], sine[:, 0])
    context = (pre, squares, qk_gains, cosine[:, 0], signed, places[:, None], places[None, :])
    context = context + (lengths[:, 0],)
    *saved, attended = attend(*context)
    attended = exchange_rows(attended[None], "inward", "attended_to_rows", 7)[0]
    attended, next_w, halves = lax.optimization_barrier((attended, next_w, halves))
    attended = attended.transpose(1, 2, 0, 3).reshape(batches, rows, width)
    x_mid = inputs + dot("mtd,de->mte", attended, out_w)
    mlp_root = inv_rms(x_mid)
    mixed_in = (x_mid * mlp_root * gain_mlp).astype(BF)
    router = jax.nn.softmax(dot("mtd,de->mte", mixed_in, router_w), axis=-1)
    routed = jnp.any(routes[:, 0, :, :, None] == expert_range, axis=2).astype(F32)
    gates = (router * routed).transpose(2, 0, 1).reshape(ctx_size, local_experts, batches, rows)
    x_rows, cross_rows = gather_rows([mixed_in, crossing], ("both", "own"), "gather_mixed", 2)
    gates, x_rows = lax.optimization_barrier((gates, x_rows))
    gates = exchange_rows(gates, "outward", "gates_to_experts", 8, 2)
    g_rows = (g_own, cross_rows)
    gates = gates.transpose(1, 0, 3, 4, 2).reshape(4 * quads, batches * rows, local_experts)
    number = jnp.arange(2 * quads, dtype=jnp.int32)
    place = (lax.axis_index("quad") ^ (number % quads)) * 2 + (pair ^ (number // quads))
    x_rows, next_w, down_parts, halves, gates = lax.optimization_barrier(
        (x_rows, next_w, down_parts, halves, gates)
    )
    down_w = gather_lane(w_down, down_parts).swapaxes(0, 1)
    down_w = down_w.reshape(local_experts, hidden_half, width)

    sums = ()
    d_gates, grads_both, grads_down = [], [], []
    for e in range(local_experts):
        both_w = next_w
        if e < local_experts - 1:
            next_w = exchange(halves[e + 1], DP)
        *sums, d_gate, hid, d_gate_pre, d_up_pre = expert(
            place, gates[..., e : e + 1], x_rows, g_rows, both_w, down_w[e], tuple(sums),
            f"expert_{e}",
        )
        d_gates.append(d_gate)
        grad_both, grad_down = expert_grads(
            place, x_rows, g_rows, hid, d_gate_pre, d_up_pre, dp_size, f"expert_grads_{e}"
        )
        sums[0], grad_both, next_w = lax.optimization_barrier((sums[0], grad_both, next_w))
        grads_both.append(exchange(grad_both, DP) if e < local_experts - 1 else grad_both)
        grads_down.append(grad_down)
    moe_rows, d_rows = sums
    done, grads_down, d_rows = lax.optimization_barrier((grads_both[:-1], grads_down, d_rows))
    grads_both[:-1] = done
    grads_down = jnp.stack(grads_down)
    grads_down = grads_down.reshape(local_experts, lanes, -1, width).swapaxes(0, 1)
    lane = lax.axis_index("lane")
    down_others = [
        lax.ppermute(
            lax.dynamic_index_in_dim(grads_down, lane ^ d, 0, keepdims=False),
            "lane", [(i, i ^ d) for i in range(lanes)],
        )
        for d in range(1, lanes)
    ]
    d_mixed, moe_sum = scatter_all(
        [d_rows, moe_rows], (True, True), "scatter_experts", 24
    )
    d_gates = jnp.concatenate(d_gates, axis=-1)
    d_gates = d_gates.reshape(2 * quads, 2, batches, rows, local_experts)
    d_gates = d_gates.transpose(1, 0, 4, 2, 3)
    d_gates, d_mixed, down_others = lax.optimization_barrier((d_gates, d_mixed, down_others))
    d_router = exchange_rows(d_gates, "inward", "gate_gradients", 9, 2)
    d_router, last_both = lax.optimization_barrier((d_router, grads_both[-1]))
    grads_both[-1] = exchange(last_both, DP)
    d_router = jnp.sum(d_router, axis=0).reshape(expert_count, batches, rows)
    d_router = d_router.transpose(1, 2, 0) * routed
    d_logits = (
        router * (d_router - jnp.sum(router * d_router, axis=-1, keepdims=True))
    ).astype(BF)
    d_mixed = d_mixed + dot("mte,de->mtd", d_logits, router_w)

    def norm_back_all(values, root, gain, grad):
        d_values, d_gain = norm_back(values, root, gain, grad)
        return d_values, jnp.sum(d_gain, axis=0)

    d_mid, part_mlp_gain = norm_back_all(x_mid, mlp_root, gain_mlp, d_mixed)
    d_mid = d_mid + grad_low.astype(F32)
    d_att_out = d_mid.astype(BF)
    grad_out = dot("mtd,mte->de", attended, d_att_out).astype(BF)
    d_attended = dot("mte,de->mtd", d_att_out, out_w).astype(BF)
    beside = quads == 4 and dp_size * shard == batches * rows
    if not beside:
        grad_out = lax.psum_scatter(grad_out, ALL, scatter_dimension=0, tiled=True).astype(F32)
    d_attended = d_attended.reshape(batches, rows, ctx_size, head_width).transpose(2, 0, 1, 3)
    d_attended = exchange_rows(d_attended, "outward", "attended_gradients", 10)[0]
    d_norm, d_value, inners, d_gains = attend_back(saved, d_attended, *context)
    inners = inners.transpose(2, 0, 1, 3).reshape(2 * quads, 2 * batches, rows)
    inners = sum_ctx(inners, "sum_inner", 11).reshape(2 * quads, batches, 2, rows)
    d_act, grad_qkv = project_back(d_norm, d_value, pre, squares, inners, act, qkv_w)
    grad_qkv = grad_qkv.reshape(dp_size, -1, 3 * head_width)
    kinds = [d_act]
    if beside:
        kinds.append(grad_out.reshape(dp_size, ctx_size, shard, width))
    d_act, *grad_planes, grad_qkv = scatter_all(
        kinds, (False,) * len(kinds), "scatter_act", 25, (grad_qkv,)
    )
    d_inputs, part_attn_gain = norm_back_all(inputs, attn_root, gain_attn, d_act)
    mixed = (x_mid + moe_sum).astype(BF)

    grad_gate, grad_up = finish_grads(grads_both)
    grad_down = lax.dynamic_index_in_dim(grads_down, lane, 0, keepdims=False).astype(F32)
    for part in down_others:
        grad_down = grad_down + part.astype(F32)

    grad_qkv = jnp.sum(grad_qkv.astype(F32), axis=0).astype(BF)
    grad_qkv = grad_qkv.reshape(ctx_size, shard, 3 * head_width)
    grad_planes = [part.reshape(dp_size, shard, width).astype(BF) for part in grad_planes]
    grad_router = dot("mtd,mte->de", mixed_in, d_logits)
    columns = jnp.arange(ctx_size, dtype=jnp.int32)[:, None] == here

    def placed(part):
        return jnp.where(columns, part[None, :], 0.0).reshape(width)

    gains = jnp.stack(
        [part_attn_gain, part_mlp_gain, placed(d_gains[0, 0]), placed(d_gains[1, 0])]
    )
    gains = gains.reshape(4, dp_size, ctx_size, shard).transpose(1, 2, 0, 3)
    packed = jnp.concatenate(
        [
            gains.reshape(dp_size * ctx_size, 1, 4 * shard),
            grad_router.reshape(dp_size * ctx_size, 1, shard * expert_count),
        ],
        axis=2,
    )
    grad_qkv, packed, *grad_planes = final_exchange(grad_qkv, packed, grad_planes)
    packed = jnp.sum(packed, axis=(0, 1))
    grad_qkv = grad_qkv.astype(F32)
    if beside:
        grad_out = jnp.sum(grad_planes[0].astype(F32), axis=0)

    return (
        mixed[:, None],
        (d_inputs + d_mid)[:, None],
        grad_qkv[0],
        grad_qkv[1],
        grad_qkv[2],
        grad_out,
        packed[4 * shard :].reshape(shard, expert_count),
        grad_gate,
        grad_up,
        grad_down,
        packed[:shard],
        packed[shard : 2 * shard],
        packed[2 * shard : 3 * shard],
        packed[3 * shard : 4 * shard],
    )


def solution(mesh):
    dp_size, ctx_size = mesh.shape["dp"], mesh.shape["ctx"]
    grid = Mesh(mesh.devices.reshape(2, dp_size // 2, ctx_size // 2, 2), ALL)
    rows = P(None, DP, CTX, None)
    dense = P(ALL, None)
    expert = P(CTX, DP, None)
    vector = P(ALL)
    return jax.shard_map(
        on_device,
        mesh=grid,
        in_specs=(rows, rows, rows, P(None, DP), P())
        + (dense,) * 5
        + (expert,) * 3
        + (vector,) * 4,
        out_specs=(rows, rows) + (dense,) * 5 + (expert,) * 3 + (vector,) * 4,
        check_vma=False,
    )
```
